32 devices in a mesh: lat: 4 (over z), lon: 8 (over y, x, core).
Axes of the slice: x: 2, y: 2, z: 4, core: 2. Of those that a mesh axis runs over, the one named last changes fastest.
Arguments:
- mesh_latent: bfloat16 [32, 64, 512], P('lat', 'lon'), may hold values from -6 to 6
- grid_cotangent: bfloat16 [32768, 512], P(('lat', 'lon')), may hold values from -6 to 6
- w_source: bfloat16 [512, 512], replicated, may hold values from -0.25 to 0.25
- w_target: bfloat16 [512, 512], replicated, may hold values from -0.25 to 0.25
- w_node: bfloat16 [512, 512], replicated, may hold values from -0.25 to 0.25
- w_coarse: bfloat16 [512, 512], replicated, may hold values from -0.25 to 0.25
- w_decode: bfloat16 [512, 512], replicated, may hold values from -0.25 to 0.25
- neighbour_codes: int32 [6, 32, 64], P(None, 'lat', 'lon'), may hold values from 0 to 8, as said below
- coarse_ids: int32 [32, 64, 1], P('lat', 'lon'), may hold values from 0 to 641
- edge_source: int32 [98304], P(('lat', 'lon')), may hold values from 0 to 63
- edge_target: int32 [98304], P(('lat', 'lon')), may hold values from 0 to 1023
- edge_owner: int32 [768, 1], P(('lat', 'lon')), may hold values from 0 to 7, as said below
Outputs:
- mesh_out: bfloat16 [32, 64, 512], P('lat', 'lon')
- grid_out: bfloat16 [32768, 512], P(('lat', 'lon'))
- clipped: float32 [5, 262144], P(None, ('lat', 'lon'))
The draws below stay inside these ranges and needn't reach their ends.
Inputs may be any that keep to these rules, and one draw needn't show every extreme that they name: `neighbour_codes`: code c names the row offset c // 3 - 1 and the column offset c % 3 - 1 and is never 4; the six codes of one node differ. `coarse_ids`: every coarse node has at least one mesh node. `edge_owner`: the owner of a block held by the device at longitude index b is b, or b - 1 or b + 1 on the periodic cycle of longitude indices. Among the 24 blocks of one device at most 3 name b - 1 and at most 3 name b + 1; in every draw some device receives 3 blocks from each of its two neighbours.
All inputs are finite; a program needn't handle non-finite values.
Results may differ from the reference program's by a relative error of at most 0.008.
Values may be sent and summed in bfloat16 or wider, within the bound.
A program may use at most 64 MiB of HBM per device.

```python
import jax
import jax.numpy as jnp
from jax import lax

D = 512
ROWS_DEV = 8
COLS_DEV = 8
GRID_DEV = 1024
BLOCK = 128
COARSE = 642
BLOCKS_DEV = 24
CAP = 3
MESH_ROWS = 32
MESH_COLS = 64
GRID = 32768
EDGES = 98304
N_LAT = 4
N_LON = 8
DEVICES = 32


def draw_neighbour_codes(key, part):
    scores = jax.random.randint(key, (N_LAT * ROWS_DEV, N_LON * COLS_DEV, 8), 0, 1 << 20) * 8 + jnp.arange(8, dtype=jnp.int32)
    order = jnp.argsort(scores, axis=-1, stable=True)[..., :6]
    codes = order + (order >= 4).astype(jnp.int32)
    return jnp.transpose(codes, (2, 0, 1)).astype(jnp.int32)


def draw_edge_owner(key, part):
    devices = N_LAT * N_LON
    base = jax.random.fold_in(key, 7)
    key_counts, key_star, key_order = jax.random.split(base, 3)
    counts = jax.random.randint(key_counts, (devices, 2), 0, CAP + 1).astype(jnp.int32)
    star = jax.random.randint(key_star, (), 0, devices).astype(jnp.int32)
    star_lat = star // N_LON
    star_lon = star % N_LON
    sender_left = star_lat * N_LON + (star_lon + N_LON - 1) % N_LON
    sender_right = star_lat * N_LON + (star_lon + 1) % N_LON
    dev_ids = jnp.arange(devices, dtype=jnp.int32)
    to_left = jnp.where(dev_ids == sender_right, CAP, counts[:, 0])
    to_right = jnp.where(dev_ids == sender_left, CAP, counts[:, 1])
    scores = jax.random.randint(key_order, (devices, BLOCKS_DEV), 0, 1 << 20) * BLOCKS_DEV + jnp.arange(BLOCKS_DEV, dtype=jnp.int32)[None]
    order = jnp.argsort(scores, axis=1, stable=True)
    ranks = jnp.argsort(order, axis=1, stable=True).astype(jnp.int32)
    offset = jnp.where(ranks < to_left[:, None], -1, jnp.where(ranks < (to_left + to_right)[:, None], 1, 0))
    lon_ids = dev_ids % N_LON
    owner = (lon_ids[:, None] + offset + N_LON) % N_LON
    return owner.reshape(devices * BLOCKS_DEV, 1).astype(jnp.int32)


def with_ends(array, rng, low, high):
    longest = array.shape.index(max(array.shape))
    spots = []
    for shift in (0, 1):
        where = [jax.random.randint(jax.random.fold_in(rng, axis), (), 0, length) for axis, length in enumerate(array.shape)]
        where[longest] = (where[longest] + shift) % array.shape[longest]
        spots.append(tuple(where))
    return array.at[spots[0]].set(low).at[spots[1]].set(high)


def block_levels(key, extent, shards, low, top_value):
    gain, own = 1.0, jax.random.fold_in(key, 6)
    for axis_at, parts in shards:
        draws = jnp.exp(jax.random.uniform(jax.random.fold_in(own, axis_at), (parts,), jnp.float32, low / len(shards), top_value / len(shards)))
        gain = gain * jnp.repeat(draws, extent[axis_at] // parts).reshape([-1 if axis == axis_at else 1 for axis in range(len(extent))])
    return gain


def different_ones(stream_key, rows, number_of, top, lift):
    sequence = jax.random.permutation(jax.random.fold_in(stream_key, 1), number_of)
    pull = sequence
    for power in range(3):
        pull = pull * pull // number_of
    pull = pull * lift // number_of
    lots = jax.random.randint(jax.random.fold_in(stream_key, 2), (rows, number_of), 0, 4096) + pull
    fixed_rows = jax.random.permutation(jax.random.fold_in(stream_key, 3), rows)[jnp.arange(number_of) % rows]
    lots = jnp.where(jnp.arange(rows)[:, None] == fixed_rows[None, :], 1 << 14, lots)
    merit = lots * number_of + jnp.arange(number_of)
    return lax.top_k(merit.astype(jnp.int32), top)[1].astype(jnp.int32)


def bell_draw(stream_key, dims, scale, reach, shards=(), held_as=jnp.bfloat16):
    entries = jax.random.normal(stream_key, dims, jnp.float32) * scale
    if len(shards) > 0:
        entries = block_levels(stream_key, dims, shards, -0.22, 0.18) * entries
    return jnp.clip(entries, min=-reach, max=reach).astype(held_as)


def setup_inputs(seed: int = 0) -> dict:
    arg_keys = jax.random.split(jax.random.key(seed), 13)
    return {
        "mesh_latent": bell_draw(arg_keys[0], (MESH_ROWS, MESH_COLS, D), 1.0, 6.0, ((0, 4), (1, 8))),
        "grid_cotangent": bell_draw(arg_keys[1], (GRID, D), 1.0, 6.0, ((0, 32),)),
        "w_source": bell_draw(arg_keys[2], (D, D), D ** -0.5, 0.25),
        "w_target": bell_draw(arg_keys[3], (D, D), D ** -0.5, 0.25),
        "w_node": bell_draw(arg_keys[4], (D, D), D ** -0.5, 0.25),
        "w_coarse": bell_draw(arg_keys[5], (D, D), D ** -0.5, 0.25),
        "w_decode": bell_draw(arg_keys[6], (D, D), D ** -0.5, 0.25),
        "neighbour_codes": draw_neighbour_codes(jax.random.fold_in(arg_keys[12], 71), 0),
        "coarse_ids": different_ones(arg_keys[8], MESH_ROWS * MESH_COLS, COARSE, 1, 12).reshape((MESH_ROWS, MESH_COLS, 1)),
        "edge_source": with_ends(jax.random.randint(arg_keys[9], (EDGES,), 0, ROWS_DEV * COLS_DEV), jax.random.fold_in(arg_keys[9], 1), 0, (ROWS_DEV * COLS_DEV) - 1).astype(jnp.int32),
        "edge_target": with_ends(jax.random.randint(arg_keys[10], (EDGES,), 0, GRID_DEV), jax.random.fold_in(arg_keys[10], 1), 0, GRID_DEV - 1).astype(jnp.int32),
        "edge_owner": draw_edge_owner(jax.random.fold_in(arg_keys[12], 71), 0),
    }


def silu_slope(value):
    sig = jax.nn.sigmoid(value)
    return sig * (1.0 + value * (1.0 - sig))

def reference(mesh_latent, grid_cotangent, w_source, w_target, w_node, w_coarse, w_decode, neighbour_codes, coarse_ids, edge_source, edge_target, edge_owner):
    height, breadth, width = mesh_latent.shape
    nodes = height * breadth
    wrapped = jnp.concatenate([mesh_latent[:, -1:], mesh_latent, mesh_latent[:, :1]], 1)
    padded = jnp.pad(wrapped, ((1, 1), (0, 0), (0, 0)))
    flat_pad = padded.reshape(-1, width)
    row_at = jnp.arange(height, dtype=jnp.int32)[None, :, None] + neighbour_codes // 3
    col_at = jnp.arange(breadth, dtype=jnp.int32)[None, None, :] + neighbour_codes % 3
    where_idx = (row_at * (breadth + 2) + col_at).reshape(-1).astype(jnp.int32)
    beside = jnp.take(flat_pad, where_idx, axis=0)
    latent = mesh_latent.reshape(nodes, width)
    toward = jnp.dot(latent, w_target, preferred_element_type=jnp.float32)
    edges_pre = jnp.dot(beside, w_source, preferred_element_type=jnp.float32).reshape(6, nodes, width) + toward[None]
    agg = lax.optimization_barrier(jnp.sum(jax.nn.silu(edges_pre), 0)).astype(jnp.bfloat16)
    onehot = (coarse_ids.reshape(nodes, 1) == jnp.arange(COARSE, dtype=jnp.int32)[None]).astype(jnp.bfloat16)
    pooled = jnp.dot(onehot.T, latent, preferred_element_type=jnp.float32)
    count = lax.optimization_barrier(jnp.sum(onehot.astype(jnp.float32), 0))
    coarse_in = (pooled * lax.rsqrt(count)[:, None]).astype(jnp.bfloat16)
    cpre = jnp.dot(coarse_in, w_coarse, preferred_element_type=jnp.float32)
    coarse_out = jax.nn.silu(cpre).astype(jnp.bfloat16)
    child = jnp.dot(onehot, coarse_out, preferred_element_type=jnp.float32)
    npre = jnp.dot(agg, w_node, preferred_element_type=jnp.float32) + child
    mesh_out = (latent.astype(jnp.float32) + jax.nn.silu(npre)).astype(jnp.bfloat16)
    per_dev = BLOCKS_DEV * BLOCK
    edge_ids = jnp.arange(EDGES, dtype=jnp.int32)
    device = edge_ids // per_dev
    lat_pos = device // N_LON
    lon_pos = device % N_LON
    owner = jnp.repeat(edge_owner[:, 0], BLOCK).astype(jnp.int32)
    src_row = lat_pos * ROWS_DEV + edge_source // COLS_DEV
    src_col = lon_pos * COLS_DEV + edge_source % COLS_DEV
    src_flat = (src_row * breadth + src_col).astype(jnp.int32)
    target = ((lat_pos * N_LON + owner) * GRID_DEV + edge_target).astype(jnp.int32)

    def decode_step(carry, pieces):
        grid_acc, grad_acc, source_acc = carry
        sources, targets = pieces
        gathered = jnp.take(mesh_out, sources, axis=0)
        pre = jnp.dot(gathered, w_decode, preferred_element_type=jnp.float32)
        message = jax.nn.silu(pre).astype(jnp.bfloat16)
        grid_acc = grid_acc.at[targets].add(message.astype(jnp.float32))
        edge_cot = jnp.take(grid_cotangent, targets, axis=0).astype(jnp.float32)
        d_pre = (edge_cot * silu_slope(pre)).astype(jnp.bfloat16)
        grad_acc = grad_acc + jnp.dot(gathered.T, d_pre, preferred_element_type=jnp.float32)
        source_acc = source_acc.at[sources].add(d_pre.astype(jnp.float32))
        return ((grid_acc, grad_acc, source_acc), None)
    start = (jnp.zeros((GRID, width), jnp.float32), jnp.zeros((width, width), jnp.float32), jnp.zeros((nodes, width), jnp.float32))
    pieces = (src_flat.reshape(DEVICES, per_dev), target.reshape(DEVICES, per_dev))
    (grid_acc, grad_decode, source_acc), _ = lax.scan(decode_step, start, pieces)
    grid_out = grid_acc.astype(jnp.bfloat16)
    per_source = source_acc.astype(jnp.bfloat16)
    d_out = jnp.dot(per_source, w_decode.T, preferred_element_type=jnp.float32)
    d_node = (d_out * silu_slope(npre)).astype(jnp.bfloat16)
    grad_node = jnp.dot(agg.T, d_node, preferred_element_type=jnp.float32)
    d_coarse = jnp.dot(onehot.T, d_node, preferred_element_type=jnp.float32)
    grad_coarse = jnp.dot(coarse_in.astype(jnp.float32).T, d_coarse * silu_slope(cpre), precision=lax.Precision.HIGHEST)
    d_agg = jnp.dot(d_node, w_node.T, preferred_element_type=jnp.float32)
    d_edges = (d_agg[None] * silu_slope(edges_pre)).astype(jnp.bfloat16)
    grad_source = jnp.dot(beside.T, d_edges.reshape(6 * nodes, width), preferred_element_type=jnp.float32)
    d_sum = lax.optimization_barrier(jnp.sum(d_edges.astype(jnp.float32), 0)).astype(jnp.bfloat16)
    grad_target = jnp.dot(latent.T, d_sum, preferred_element_type=jnp.float32)
    grads = jnp.stack([grad_source, grad_target, grad_node, grad_coarse, grad_decode])
    norm = jnp.sqrt(jnp.sum(grads * grads))
    clipped = (grads / (norm + 1e-06)).reshape(5, width * width)
    return (mesh_out.reshape(height, breadth, width), grid_out, clipped)
```

```python
import functools
import math

import jax
import jax.numpy as jnp
from jax import lax
from jax.experimental import pallas as pl
from jax.experimental.pallas import tpu as pltpu
from jax.sharding import PartitionSpec as P

CAP = 3
F32 = jnp.float32
BF16 = jnp.bfloat16


def silu_slope(value):
    sig = jax.nn.sigmoid(value)
    return sig * (1.0 + value * (1.0 - sig))


def mm(left, right):
    return jnp.dot(left, right, preferred_element_type=F32)


def mm_t(left, right):
    return lax.dot_general(left, right, (((0,), (0,)), ((), ())), preferred_element_type=F32)


def mm_nt(left, right):
    return lax.dot_general(left, right, (((1,), (1,)), ((), ())), preferred_element_type=F32)


def split_float(value):
    high = value.astype(BF16)
    return high, (value - high.astype(F32)).astype(BF16)


MESH = pl.DeviceIdType.MESH


class Place:
    def __init__(self, sizes):
        self.Z, self.Y, self.X, self.C = sizes
        self.L = self.Y * self.X * self.C
        self.lat, self.lon = lax.axis_index("lat"), lax.axis_index("lon")
        self.z, self.c = self.lat, lax.rem(self.lon, self.C)
        self.x = lax.rem(self.lon // self.C, self.X)
        self.y = self.lon // (self.C * self.X)

    def at(self, y=None, x=None, c=None):
        y, x, c = (old if new is None else new for new, old in ((y, self.y), (x, self.x), (c, self.c)))
        return (self.lat, (y * self.X + x) * self.C + c)

    def meet(self):
        barrier = pltpu.get_barrier_semaphore()
        for step in range(1, self.Z):
            peer = (lax.rem(self.z + step, self.Z), self.lon)
            pl.semaphore_signal(barrier, inc=1, device_id=peer, device_id_type=MESH)
        for step in range(1, self.L):
            peer = (self.lat, lax.rem(self.lon + step, self.L))
            pl.semaphore_signal(barrier, inc=1, device_id=peer, device_id_type=MESH)

    def met(self):
        pl.semaphore_wait(pltpu.get_barrier_semaphore(), self.Z - 1 + self.L - 1)


def send(src, dst, sems, slot, peer):
    copy = pltpu.make_async_remote_copy(
        src_ref=src, dst_ref=dst, send_sem=sems.at[0, slot], recv_sem=sems.at[1, slot],
        device_id=peer, device_id_type=MESH,
    )
    copy.start()
    return copy


def iota(shape, dim):
    return lax.broadcasted_iota(jnp.int32, shape, dim)


def step_kernel(sizes, *refs):
    (lat_ref, cot_ref, ws_ref, wt_ref, wn_ref, wc_ref, wd_ref, code_ref, coarse_ref, src_ref, tgt_ref,
     owner_ref) = refs[:12]
    mesh_ref, grid_ref, out_ref = refs[12:15]
    (all_ref, all_id, near, pack, erow, counts, cnt_high, cnt_low, back, backs, msgs, grad, s1, r1, acc1, s2, r2, acc2,
     s3, r3, acc3, s4, r4, sq, zq, lq, id_ref, share) = refs[15:43]
    gsem, esem, sem1, sem2, sem3, sem4, zsem, lsem = refs[43:]
    p = Place(sizes)
    Z, Y, X, C, z, y, x, c = p.Z, p.Y, p.X, p.C, p.z, p.y, p.x, p.c
    nodes, width = lat_ref.shape
    grid_rows = cot_ref.shape[0]
    blocks, block_len = src_ref.shape
    lanes = counts.shape[1]
    to_left = (p.lat, lax.rem(p.lon + p.L - 1, p.L))
    to_right = (p.lat, lax.rem(p.lon + 1, p.L))
    many = out_ref.shape[0]
    R = share.shape[1]
    w2 = width // 2
    halves = (pl.ds(0, w2), pl.ds(w2, w2))
    half = nodes // 2
    low, high = pl.ds(0, half), pl.ds(half, half)
    copies = []
    used = [0]

    def go(src, dst, sems, slot, peer):
        copy = send(src, dst, sems, slot, peer)
        copies.append(copy)
        return copy

    def pass_on(src, dst, peer):
        used[0] += 1
        return go(src, dst, gsem, used[0] - 1, peer)

    p.meet()
    all_ref[z, y, x, c] = lat_ref[...]
    slots, height, breadth = code_ref.shape

    def column(square):
        tall = jnp.concatenate([jnp.broadcast_to(square[i:i + 1], (breadth, breadth)) for i in range(height)], 0)
        keep = iota(tall.shape, 0) % breadth == iota(tall.shape, 1)
        return jnp.sum(jnp.where(keep, tall, 0), 1, keepdims=True)

    id_column = column(coarse_ref[...]) + 1
    spread = (nodes, id_ref.shape[1])
    keep = iota(spread, 1) == iota(spread, 0) + c * nodes
    id_ref[...] = jnp.sum(jnp.where(keep, jnp.broadcast_to(id_column, spread), 0), 0, keepdims=True)
    all_id[z, y, x, c] = id_ref[...]
    sub, lane = iota((blocks, blocks), 0), iota((blocks, blocks), 1)
    owner = jnp.broadcast_to(owner_ref[...], (blocks, blocks))
    owner = jnp.sum(jnp.where(sub == lane, owner, 0), 1, keepdims=True)
    is_left = (owner == lax.rem(p.lon + p.L - 1, p.L)).astype(jnp.int32)
    is_right = (owner == lax.rem(p.lon + 1, p.L)).astype(jnp.int32)

    def ranks(column):
        row = jnp.sum(jnp.where(sub == lane, jnp.broadcast_to(column, sub.shape), 0), 0, keepdims=True)
        return jnp.sum(jnp.where(lane < sub, jnp.broadcast_to(row, sub.shape), 0), 1, keepdims=True)

    place = jnp.where(is_left == 1, ranks(is_left), jnp.where(is_right == 1, CAP + ranks(is_right), -1))
    wide_place = jnp.broadcast_to(place, (blocks, block_len))
    for r in range(2 * CAP):
        mine = wide_place == r
        side, row = divmod(r, CAP)
        pack[side, 0, row:row + 1] = jnp.sum(jnp.where(mine, src_ref[...], 0), 0, keepdims=True)
        pack[side, 1, row:row + 1] = jnp.sum(jnp.where(mine, tgt_ref[...] + 1, 0), 0, keepdims=True) - 1
    p.met()
    first = []
    for step in range(1, Z):
        peer = (lax.rem(z + step, Z), p.lon)
        first.append([
            pass_on(lat_ref, all_ref.at[z, y, x, c], peer),
            pass_on(id_ref, all_id.at[z, y, x, c], peer),
        ])
    edges = [go(pack.at[0], pack.at[3], esem, 0, to_left), go(pack.at[1], pack.at[2], esem, 1, to_right)]
    second, third, fourth = [], [], []

    def hop_two(step):
        line = lax.rem(z + Z - step, Z)
        if step:
            for copy in first[step - 1]:
                copy.wait_recv()
        mine = []
        block = all_ref.at[line, y, x, c]
        src_low = block.at[low] if step else lat_ref.at[low]
        src_high = block.at[high] if step else lat_ref.at[high]
        src_id = all_id.at[line, y, x, c] if step else id_ref
        for off in range(1, X):
            peer = p.at(x=lax.rem(x + off, X))
            mine.append(pass_on(src_low, block.at[low], peer))
            mine.append(pass_on(src_id, all_id.at[line, y, x, c], peer))
        for off in range(1, Y):
            mine.append(pass_on(src_high, block.at[high], p.at(y=lax.rem(y + off, Y))))
        second.append(mine)

    def hop_three(step):
        line = lax.rem(z + Z - step, Z)
        for copy in second[step]:
            copy.wait_recv()
        mine = []
        for off in range(1, Y):
            peer = p.at(y=lax.rem(y + off, Y))
            part = all_ref.at[line, y, :, c, low]
            mine.append(pass_on(part, part, peer))
            part = all_id.at[line, y, :, c]
            mine.append(pass_on(part, part, peer))
        for off in range(1, X):
            part = all_ref.at[line, :, x, c, high]
            mine.append(pass_on(part, part, p.at(x=lax.rem(x + off, X))))
        third.append(mine)

    def hop_four(step):
        line = lax.rem(z + Z - step, Z)
        for copy in third[step]:
            copy.wait_recv()
        mine = []
        for off in range(1, C):
            peer = p.at(c=lax.rem(c + off, C))
            part = all_ref.at[line, :, :, c]
            mine.append(pass_on(part, part, peer))
            part = all_id.at[line, :, :, c]
            mine.append(pass_on(part, part, peer))
        fourth.append(mine)

    stays = jnp.broadcast_to((owner == p.lon).astype(jnp.int32), (blocks, block_len))
    erow[0, 0:blocks] = src_ref[...]
    erow[1, 0:blocks] = jnp.where(stays == 1, tgt_ref[...], -1)
    pair = 2 if blocks % 2 == 0 else 1

    def count(start, stop):
        for b in range(start, stop, pair):
            upto = min(b + pair, stop)
            tgt = jnp.concatenate([jnp.broadcast_to(erow[1, r:r + 1], (grid_rows, block_len)) for r in range(b, upto)], 1)
            src = jnp.concatenate([jnp.broadcast_to(erow[0, r:r + 1], (lanes, block_len)) for r in range(b, upto)], 1)
            hot_t = jnp.where(tgt == iota(tgt.shape, 0), 1.0, 0.0).astype(BF16)
            hot_s = jnp.where(src == iota(src.shape, 0), 1.0, 0.0).astype(BF16)
            more = mm_nt(hot_t, hot_s)
            counts[...] = more if b == 0 else counts[...] + more

    quarter = blocks // 4 // pair * pair
    hop_two(0)
    count(0, quarter)
    for step in range(1, Z):
        hop_two(step)
    count(quarter, 2 * quarter)
    for step in range(Z):
        hop_three(step)
    count(2 * quarter, 3 * quarter)
    for step in range(Z):
        hop_four(step)
    count(3 * quarter, blocks)
    for copy in edges:
        copy.wait_recv()
    for side in range(2):
        erow[0, blocks + side * CAP:blocks + (side + 1) * CAP] = pack[2 + side, 0] + (side + 1) * nodes
        erow[1, blocks + side * CAP:blocks + (side + 1) * CAP] = pack[2 + side, 1]
    count(blocks, blocks + 2 * CAP)
    over = jnp.floor(counts[...] * (1.0 / 256.0)) * 256.0
    cnt_high[...] = over.astype(BF16)
    cnt_low[...] = (counts[...] - over).astype(BF16)
    cot_sums = mm_t(cnt_high[...], cot_ref[...]) + mm_t(cnt_low[...], cot_ref[...])
    backs[0] = cot_sums[nodes:2 * nodes].astype(BF16)
    backs[1] = cot_sums[2 * nodes:3 * nodes].astype(BF16)
    returns = [go(backs.at[0], back.at[0], esem, 2, to_left), go(backs.at[1], back.at[1], esem, 3, to_right)]
    latent = lat_ref[...]
    toward = mm(latent, wt_ref[...])

    pooled = jnp.zeros((nodes, width), F32)
    count_of = jnp.zeros((nodes, 1), F32)
    for step in range(Z):
        line = lax.rem(z + Z - step, Z)
        for copy in fourth[step]:
            copy.wait_recv()
        ids = jnp.sum(all_id[line].reshape(Y * X, C, C * nodes), 1)
        row = jnp.concatenate([ids[q:q + 1] for q in range(Y * X)], 1)
        wide = jnp.broadcast_to(row, (nodes, row.shape[1]))
        same = jnp.where(wide == jnp.broadcast_to(id_column, wide.shape), 1.0, 0.0)
        count_of = count_of + jnp.sum(same, 1, keepdims=True)
        pooled = pooled + mm(same.astype(BF16), all_ref[line].reshape(p.L * nodes, width))
    coarse_in = (pooled * lax.rsqrt(count_of)).astype(BF16)
    cpre = mm(coarse_in, wc_ref[...])
    coarse_out = (cpre * jax.nn.sigmoid(cpre)).astype(BF16)

    for r in range(3):
        for q in range(3):
            lon = lax.rem(p.lon + q - 1 + p.L, p.L)
            line = lax.rem(z + r - 1 + Z, Z)
            block = all_ref[line, lon // (C * X), lax.rem(lon // C, X), lax.rem(lon, C)]
            near[(r * 3 + q) * nodes:(r * 3 + q + 1) * nodes] = block
    at_row, at_col = iota((height, breadth), 0), iota((height, breadth), 1)
    wheres = []
    for k in range(slots):
        code = code_ref[k]
        down = jnp.where(code >= 6, 1, jnp.where(code >= 3, 0, -1))
        rows, cols = at_row + down, at_col + code - 3 * down - 4
        below, above = jnp.where(rows < 0, 1, 0), jnp.where(rows >= height, 1, 0)
        before, after = jnp.where(cols < 0, 1, 0), jnp.where(cols >= breadth, 1, 0)
        block = (1 + above - below) * 3 + 1 + after - before
        inner = (rows + height * (below - above)) * breadth + cols + breadth * (before - after)
        first_line, last_line = jnp.where(z == 0, 1, 0), jnp.where(z == Z - 1, 1, 0)
        outside = below * first_line + above * last_line
        wheres.append(column(jnp.where(outside > 0, -1, block * nodes + inner)))
    where = jnp.concatenate(wheres, 0)
    hot = jnp.broadcast_to(where, (where.shape[0], near.shape[0]))
    hot = jnp.where(hot == iota(hot.shape, 1), 1.0, 0.0).astype(BF16)
    beside = mm(hot, near[...]).astype(BF16)
    edges_pre = mm(beside, ws_ref[...]).reshape(slots, nodes, width) + toward[None]
    agg = jnp.sum(edges_pre * jax.nn.sigmoid(edges_pre), 0).astype(BF16)

    npre = mm(agg, wn_ref[...]) + coarse_out.astype(F32)
    mesh_out = (latent.astype(F32) + npre * jax.nn.sigmoid(npre)).astype(BF16)
    mesh_ref[...] = mesh_out

    pre = mm(mesh_out, wd_ref[...])
    msgs[0:nodes] = (pre * jax.nn.sigmoid(pre)).astype(BF16)
    if lanes > 3 * nodes:
        msgs[3 * nodes:] = jnp.zeros((lanes - 3 * nodes, width), BF16)
    mine = msgs.at[pl.ds(0, nodes)]
    spoken = [
        go(mine, msgs.at[pl.ds(nodes, nodes)], esem, 4, to_right),
        go(mine, msgs.at[pl.ds(2 * nodes, nodes)], esem, 5, to_left),
    ]

    one, two, three, four = {}, {}, {}, {}

    def hop_core(m, value):
        if R % 8 == 0:
            grad[m] = value.reshape(Z, Y, X, C, R, width)
        else:
            for q in range(Z * p.L):
                spot = (q // p.L, q // (C * X) % Y, q // C % X, q % C)
                grad[(m, *spot)] = value[q * R:(q + 1) * R]
        one[m] = []
        for off in range(1, C):
            there = lax.rem(c + off, C)
            k = m * (C - 1) + off - 1
            s1[k] = grad[m, :, :, :, there].astype(BF16)
            one[m].append((k, go(s1.at[k], r1.at[k], sem1, k, p.at(c=there))))

    def hop_first(m):
        total = grad[m, :, :, :, c]
        for k, copy in one[m]:
            copy.wait_recv()
            total = total + r1[k].astype(F32)
        acc1[m] = total
        two[m] = ([], [])
        for off in range(1, X):
            there = lax.rem(x + off, X)
            k = m * (X - 1) + off - 1
            s2[0][k] = acc1[m, :, :, there, :, halves[0]].astype(BF16)
            two[m][0].append((k, go(s2[0].at[k], r2[0].at[k], sem2[0], k, p.at(x=there))))
        for off in range(1, Y):
            there = lax.rem(y + off, Y)
            k = m * (Y - 1) + off - 1
            s2[1][k] = acc1[m, :, there, :, :, halves[1]].astype(BF16)
            two[m][1].append((k, go(s2[1].at[k], r2[1].at[k], sem2[1], k, p.at(y=there))))

    def hop_other(m):
        three[m] = ([], [])
        total = acc1[m, :, :, x, :, halves[0]]
        for k, copy in two[m][0]:
            copy.wait_recv()
            total = total + r2[0][k].astype(F32)
        acc2[0][m] = total
        for off in range(1, Y):
            there = lax.rem(y + off, Y)
            k = m * (Y - 1) + off - 1
            s3[0][k] = acc2[0][m, :, there].astype(BF16)
            three[m][0].append((k, go(s3[0].at[k], r3[0].at[k], sem3[0], k, p.at(y=there))))
        total = acc1[m, :, y, :, :, halves[1]]
        for k, copy in two[m][1]:
            copy.wait_recv()
            total = total + r2[1][k].astype(F32)
        acc2[1][m] = total
        for off in range(1, X):
            there = lax.rem(x + off, X)
            k = m * (X - 1) + off - 1
            s3[1][k] = acc2[1][m, :, there].astype(BF16)
            three[m][1].append((k, go(s3[1].at[k], r3[1].at[k], sem3[1], k, p.at(x=there))))

    def hop_line(m):
        for side, own in ((0, y), (1, x)):
            total = acc2[side][m, :, own]
            for k, copy in three[m][side]:
                copy.wait_recv()
                total = total + r3[side][k].astype(F32)
            acc3[m, :, :, halves[side]] = total
        four[m] = []
        for off in range(1, Z):
            there = lax.rem(z + off, Z)
            k = m * (Z - 1) + off - 1
            s4[k] = acc3[m, there].astype(BF16)
            four[m].append((k, go(s4.at[k], r4.at[k], sem4, k, (there, p.lon))))

    for copy in returns:
        copy.wait_recv()
    cot_sum = cot_sums[:nodes] + back[0].astype(F32) + back[1].astype(F32)
    d_high, d_low = split_float(cot_sum * silu_slope(pre))
    hop_core(4, mm_t(mesh_out, d_high) + mm_t(mesh_out, d_low))
    d_node = (mm_nt(d_high, wd_ref[...]) * silu_slope(npre)).astype(BF16)
    hop_core(2, mm_t(agg, d_node))
    hop_first(4)
    c_high, c_low = split_float(d_node.astype(F32) * silu_slope(cpre))
    hop_core(3, mm_t(coarse_in, c_high) + mm_t(coarse_in, c_low))
    hop_first(2)
    d_edges = (mm_nt(d_node, wn_ref[...])[None] * silu_slope(edges_pre)).astype(BF16)
    d_sum = jnp.sum(d_edges.astype(F32), 0).astype(BF16)
    hop_core(1, mm_t(latent, d_sum))
    hop_first(3)
    hop_core(0, mm_t(beside, d_edges.reshape(slots * nodes, width)))
    hop_first(1)
    hop_first(0)
    order = (4, 2, 3, 1, 0)
    hop_other(order[0])
    for copy in spoken:
        copy.wait_recv()
    grid_ref[...] = (mm(cnt_high[...], msgs[...]) + mm(cnt_low[...], msgs[...])).astype(BF16)
    for m in order[1:]:
        hop_other(m)
    for m in order:
        hop_line(m)
    square = jnp.zeros(share.shape[1:], F32)
    for m in order:
        total = acc3[m, z]
        for k, copy in four[m]:
            copy.wait_recv()
            total = total + r4[k].astype(F32)
        share[m] = total
        square = square + total * total
    sq[0] = jnp.broadcast_to(jnp.sum(square, keepdims=True), sq.shape[1:])
    mine = []
    for off in range(1, Z):
        mine.append(go(sq.at[0], zq.at[off - 1], zsem, off - 1, (lax.rem(z + off, Z), p.lon)))
    whole = sq[0]
    for off, copy in enumerate(mine):
        copy.wait_recv()
        whole = whole + zq[off]
    sq[1] = whole
    mine = []
    for off in range(1, p.L):
        mine.append(go(sq.at[1], lq.at[off - 1], lsem, off - 1, (p.lat, lax.rem(p.lon + off, p.L))))
    for off, copy in enumerate(mine):
        copy.wait_recv()
        whole = whole + lq[off]
    norm = jnp.sqrt(whole[0:1, 0:1]) + 1e-06
    for m in range(many):
        total = share[m] / norm
        for r in range(R):
            out_ref[m:m + 1, r * width:(r + 1) * width] = total[r:r + 1]
    for copy in copies:
        copy.wait_send()


def run_step(sizes, latent, cot, weights, codes, ids, source, target, owner):
    Z, Y, X, C = sizes
    L = Y * X * C
    many = len(weights)
    nodes, width = latent.shape
    grid_rows = cot.shape[0]
    blocks, block_len = source.shape
    lanes = -(-3 * nodes // 128) * 128
    R = width // (Z * L)
    w2 = width // 2
    vmem = pl.BlockSpec(memory_space=pltpu.VMEM)

    def buf(dtype, *dims):
        return pltpu.VMEM(dims, dtype)

    def sems(*counts):
        return [pltpu.SemaphoreType.DMA((2, n)) for n in counts]

    nx, ny, nz, nc = many * (X - 1), many * (Y - 1), many * (Z - 1), many * (C - 1)
    second = [buf(BF16, nx, Z, Y, R, w2), buf(BF16, ny, Z, X, R, w2)]
    third = [buf(BF16, ny, Z, R, w2), buf(BF16, nx, Z, R, w2)]
    gathers = (Z - 1) * 2 + Z * (3 * (X - 1) + 3 * (Y - 1) + 2 * (C - 1))
    return pl.pallas_call(
        functools.partial(step_kernel, sizes),
        out_shape=(
            pltpu.VMEM((nodes, width), BF16),
            pltpu.VMEM((grid_rows, width), BF16),
            pltpu.VMEM((many, R * width), F32),
        ),
        in_specs=[vmem] * (7 + many),
        out_specs=(vmem,) * 3,
        scratch_shapes=[
            buf(BF16, Z, Y, X, C, nodes, width), buf(jnp.int32, Z, Y, X, C, 1, C * nodes),
            buf(BF16, 9 * nodes, width), buf(jnp.int32, 4, 2, CAP, block_len),
            buf(jnp.int32, 2, blocks + 2 * CAP, block_len),
            buf(F32, grid_rows, lanes), buf(BF16, grid_rows, lanes), buf(BF16, grid_rows, lanes),
            buf(BF16, 2, nodes, width), buf(BF16, 2, nodes, width), buf(BF16, lanes, width),
            buf(F32, many, Z, Y, X, C, R, width),
            buf(BF16, nc, Z, Y, X, R, width), buf(BF16, nc, Z, Y, X, R, width),
            buf(F32, many, Z, Y, X, R, width),
            second, second, [buf(F32, many, Z, Y, R, w2), buf(F32, many, Z, X, R, w2)],
            third, third, buf(F32, many, Z, R, width),
            buf(BF16, nz, R, width), buf(BF16, nz, R, width),
            buf(F32, 2, 8, 128), buf(F32, Z - 1, 8, 128), buf(F32, L - 1, 8, 128),
            buf(jnp.int32, 1, C * nodes), buf(F32, many, R, width),
            *sems(gathers, 6, nc), sems(nx, ny), sems(ny, nx), *sems(nz, Z - 1, L - 1),
        ],
        compiler_params=pltpu.CompilerParams(
            collective_id=0, has_side_effects=True, vmem_limit_bytes=62 * 1024 * 1024
        ),
        name="whole_step",
    )(latent, cot, *weights, codes, ids, source, target, owner)


def write_kernel(*refs):
    count = len(refs) // 2
    sems = refs[-1]
    moves = [pltpu.make_async_copy(refs[i], refs[count + i], sems.at[i]) for i in range(count)]
    for move in moves:
        move.start()
    for move in moves:
        move.wait()


def write_results(*results):
    return pl.pallas_call(
        write_kernel,
        out_shape=tuple(jax.ShapeDtypeStruct(r.shape, r.dtype) for r in results),
        in_specs=[pl.BlockSpec(memory_space=pltpu.VMEM)] * len(results),
        out_specs=(pl.BlockSpec(memory_space=pl.ANY),) * len(results),
        scratch_shapes=[pltpu.SemaphoreType.DMA((len(results),))],
        compiler_params=pltpu.CompilerParams(vmem_limit_bytes=8 * 1024 * 1024),
        name="write_results",
    )(*results)


def lon_parts(lat_count, lon_count):
    chips = lon_count // 2
    x = next(d for d in range(math.isqrt(chips), 0, -1) if chips % d == 0)
    return lat_count, chips // x, x, 2


def local(
    mesh_latent,
    grid_cotangent,
    w_source,
    w_target,
    w_node,
    w_coarse,
    w_decode,
    neighbour_codes,
    coarse_ids,
    edge_source,
    edge_target,
    edge_owner,
):
    height, breadth, width = mesh_latent.shape
    nodes = height * breadth
    sizes = lon_parts(lax.axis_size("lat"), lax.axis_size("lon"))
    blocks = edge_owner.shape[0]
    mesh_out, grid_out, clipped = run_step(
        sizes,
        mesh_latent.reshape(nodes, width),
        grid_cotangent,
        (w_source, w_target, w_node, w_coarse, w_decode),
        neighbour_codes,
        coarse_ids.reshape(height, breadth),
        edge_source.reshape(blocks, -1),
        edge_target.reshape(blocks, -1),
        edge_owner.reshape(1, blocks),
    )
    mesh_out, grid_out, clipped = write_results(mesh_out, grid_out, clipped)
    return (mesh_out.reshape(height, breadth, width), grid_out, clipped)


def solution(mesh):
    in_specs = (
        P("lat", "lon", None),
        P(("lat", "lon"), None),
        P(),
        P(),
        P(),
        P(),
        P(),
        P(None, "lat", "lon"),
        P("lat", "lon", None),
        P(("lat", "lon")),
        P(("lat", "lon")),
        P(("lat", "lon"), None),
    )
    out_specs = (P("lat", "lon", None), P(("lat", "lon"), None), P(None, ("lat", "lon")))
    return jax.shard_map(local, mesh=mesh, in_specs=in_specs, out_specs=out_specs, check_vma=False)
```

```python
import functools
import math

import jax
import jax.numpy as jnp
from jax import lax
from jax.experimental import pallas as pl
from jax.experimental.pallas import tpu as pltpu
from jax.sharding import PartitionSpec as P

CAP = 3
F32 = jnp.float32
BF16 = jnp.bfloat16


def silu_slope(value):
    sig = jax.nn.sigmoid(value)
    return sig * (1.0 + value * (1.0 - sig))


def mm(left, right):
    return jnp.dot(left, right, preferred_element_type=F32)


def mm_t(left, right):
    return lax.dot_general(left, right, (((0,), (0,)), ((), ())), preferred_element_type=F32)


def mm_nt(left, right):
    return lax.dot_general(left, right, (((1,), (1,)), ((), ())), preferred_element_type=F32)


def split_float(value):
    high = value.astype(BF16)
    return high, (value - high.astype(F32)).astype(BF16)


MESH = pl.DeviceIdType.MESH


class Place:
    def __init__(self, sizes):
        self.Z, self.Y, self.X, self.C = sizes
        self.L = self.Y * self.X * self.C
        self.lat, self.lon = lax.axis_index("lat"), lax.axis_index("lon")
        self.z, self.c = self.lat, lax.rem(self.lon, self.C)
        self.x = lax.rem(self.lon // self.C, self.X)
        self.y = self.lon // (self.C * self.X)
        self.Q, self.q = self.Y * self.X, self.lon // self.C
        self.rows = (lax.rem(self.z + self.Z - 1, self.Z), lax.rem(self.z + 1, self.Z))
        self.sides = (lax.rem(self.lon + self.L - 1, self.L), lax.rem(self.lon + 1, self.L))

    def at(self, y=None, x=None, c=None):
        y, x, c = (old if new is None else new for new, old in ((y, self.y), (x, self.x), (c, self.c)))
        return (self.lat, (y * self.X + x) * self.C + c)

    def greeted(self):
        line = [(lax.rem(self.z + step, self.Z), self.q * self.C + core) for step in range(1, self.Z) for core in range(self.C)]
        plane = [(self.z, lax.rem(self.lon + step, self.L)) for step in range(1, self.L)]
        return line + plane + [(lat, lon) for lat in self.rows for lon in self.sides]

    def meet(self):
        barrier = pltpu.get_barrier_semaphore()
        for peer in self.greeted():
            pl.semaphore_signal(barrier, inc=1, device_id=peer, device_id_type=MESH)

    def met(self):
        pl.semaphore_wait(pltpu.get_barrier_semaphore(), len(self.greeted()))


def send(src, dst, sems, slot, peer):
    copy = pltpu.make_async_remote_copy(
        src_ref=src, dst_ref=dst, send_sem=sems.at[0, slot], recv_sem=sems.at[1, slot],
        device_id=peer, device_id_type=MESH,
    )
    copy.start()
    return copy


def iota(shape, dim):
    return lax.broadcasted_iota(jnp.int32, shape, dim)


def step_kernel(sizes, *refs):
    (lat_hbm, cot_hbm, ws_hbm, wt_hbm, wn_hbm, wc_hbm, wd_hbm, code_hbm, coarse_hbm, src_hbm, tgt_hbm,
     owner_hbm) = refs[:12]
    mesh_ref, grid_ref, out_ref = refs[12:15]
    (lat_ref, cot_ref, ws_ref, wt_ref, wn_ref, wc_ref, wd_ref, code_ref, coarse_ref, src_ref, tgt_ref, owner_ref,
     pool, parts, got, ids, plane_ids, halo, cols, pack, tally_high, tally_low, back, backs, msgs, grad, s1, r1, acc1, s2,
     r2, acc2, s3, r3, acc3, s4, r4, sq, zq, lq, id_ref, share) = refs[15:57]
    load_sem, out_sem, pool_sem, got_sem, id_sem, halo_sem, esem, sem1, sem2, sem3, sem4, zsem, lsem = refs[57:]
    p = Place(sizes)
    Z, Y, X, C, z, y, x, c = p.Z, p.Y, p.X, p.C, p.z, p.y, p.x, p.c
    Q, q = p.Q, p.q
    nodes, width = lat_ref.shape
    grid_rows = cot_ref.shape[0]
    blocks, block_len = src_ref.shape
    groups, _, group_rows = tally_high.shape
    many = out_ref.shape[0]
    R = share.shape[1]
    w2 = width // 2
    halves = (pl.ds(0, w2), pl.ds(w2, w2))
    copies, pushed = [], []
    mate = (z, q * C + 1 - c)
    most = max(Z, Q)
    role_size, role_at = jnp.where(c == 0, Z, Q), jnp.where(c == 0, z, q)
    other_size, other_at = jnp.where(c == 0, Q, Z), jnp.where(c == 0, q, z)

    def go(src, dst, sems, slot, peer):
        copy = send(src, dst, sems, slot, peer)
        copies.append(copy)
        return copy

    used = [0]

    def describe(src, dst, recv, peer, send_sem=None):
        return pltpu.make_async_remote_copy(
            src_ref=src, dst_ref=dst, send_sem=recv if send_sem is None else send_sem, recv_sem=recv, device_id=peer,
            device_id_type=MESH)

    def push(src, dst, recv, peer, only=None):
        copy = describe(src, dst, recv, peer, out_sem.at[used[0]])
        used[0] += 1
        if only is None:
            copy.start()
        else:
            pl.when(only)(copy.start)
        pushed.append((only, copy))

    def arrive(dst, recv, only=None):
        if only is None:
            describe(dst, dst, recv, mate).wait_recv()
        else:
            pl.when(only)(lambda: describe(dst, dst, recv, mate).wait_recv())

    def role_step(step):
        return jnp.where(c == 0, lax.rem(z + most * Z + step, Z), lax.rem(q + most * Q + step, Q))

    def limit(step, size):
        return step < size if step >= min(Z, Q) else None

    if Z != Q:
        pool[...] = jnp.zeros_like(pool)
    p.meet()
    needed = (src_hbm, tgt_hbm, owner_hbm, coarse_hbm, lat_hbm, code_hbm, cot_hbm, wt_hbm, ws_hbm, wn_hbm, wc_hbm, wd_hbm)
    places = (src_ref, tgt_ref, owner_ref, coarse_ref, lat_ref, code_ref, cot_ref, wt_ref, ws_ref, wn_ref, wc_ref, wd_ref)
    loads = [pltpu.make_async_copy(a, b, load_sem.at[i]) for i, (a, b) in enumerate(zip(needed, places))]
    for load in loads:
        load.start()
    slots, height, breadth = code_ref.shape
    edge = halo.shape[1]

    def column(square):
        tall = jnp.concatenate([jnp.broadcast_to(square[i:i + 1], (breadth, breadth)) for i in range(height)], 0)
        keep = iota(tall.shape, 0) % breadth == iota(tall.shape, 1)
        return jnp.sum(jnp.where(keep, tall, 0), 1, keepdims=True)

    for load in loads[:4]:
        load.wait()
    id_column = column(coarse_ref[...]) + 1
    spread = (nodes, id_ref.shape[1])
    keep = iota(spread, 1) == iota(spread, 0) + c * nodes
    id_row = jnp.sum(jnp.where(keep, jnp.broadcast_to(id_column, spread), 0), 0, keepdims=True)
    id_ref[...] = id_row
    ids[q, z, c] = id_row
    plane_ids[q, c] = id_row
    sub, lane = iota((blocks, blocks), 0), iota((blocks, blocks), 1)
    owner = jnp.broadcast_to(owner_ref[...], (blocks, blocks))
    owner = jnp.sum(jnp.where(sub == lane, owner, 0), 1, keepdims=True)
    left, right = p.sides
    is_left = (owner == left).astype(jnp.int32)
    is_right = (owner == right).astype(jnp.int32)

    def ranks(column):
        row = jnp.sum(jnp.where(sub == lane, jnp.broadcast_to(column, sub.shape), 0), 0, keepdims=True)
        return jnp.sum(jnp.where(lane < sub, jnp.broadcast_to(row, sub.shape), 0), 1, keepdims=True)

    place = jnp.where(is_left == 1, ranks(is_left), jnp.where(is_right == 1, CAP + ranks(is_right), -1))
    wide_place = jnp.broadcast_to(place, (blocks, block_len))
    for r in range(2 * CAP):
        mine = wide_place == r
        side, row = divmod(r, CAP)
        pack[side, 0, row:row + 1] = jnp.sum(jnp.where(mine, src_ref[...], 0), 0, keepdims=True)
        pack[side, 1, row:row + 1] = jnp.sum(jnp.where(mine, tgt_ref[...] + 1, 0), 0, keepdims=True) - 1
    loads[4].wait()
    latent = lat_ref[...]
    pick = iota((edge, nodes), 0)
    pick = jnp.where(pick < height, pick * breadth, (pick - height) * breadth + breadth - 1)
    cols[...] = mm(jnp.where(pick == iota(pick.shape, 1), 1.0, 0.0).astype(BF16), latent).astype(BF16)
    pool[role_at * C + c] = lat_ref[:, pl.ds(pl.multiple_of(c * w2, 128), w2)]

    def tally(source, target):
        tall = jnp.where(target < 0, -1, target % group_rows)
        both = jnp.where(target < 0, 0, target // group_rows) * nodes + source
        count = source.shape[0]
        tall = jnp.concatenate([tall[r:r + 1] for r in range(count)], 1)
        both = jnp.concatenate([both[r:r + 1] for r in range(count)], 1)
        tall = jnp.broadcast_to(tall, (group_rows, tall.shape[1]))
        both = jnp.broadcast_to(both, (groups * nodes, both.shape[1]))
        hot_t = jnp.where(tall == iota(tall.shape, 0), 1.0, 0.0).astype(BF16)
        hot_b = jnp.where(both == iota(both.shape, 0), 1.0, 0.0).astype(BF16)
        return mm_nt(hot_b, hot_t)

    def keep_tally(kind, counts):
        over = jnp.floor(counts * (1.0 / 256.0)) * 256.0
        high, low = over.astype(BF16), (counts - over).astype(BF16)
        for g in range(groups):
            tally_high[g, kind * nodes:(kind + 1) * nodes] = high[g * nodes:(g + 1) * nodes]
            tally_low[g, kind * nodes:(kind + 1) * nodes] = low[g * nodes:(g + 1) * nodes]

    stays = jnp.broadcast_to((owner == p.lon).astype(jnp.int32), (blocks, block_len))
    keep_tally(0, tally(src_ref[...], jnp.where(stays == 1, tgt_ref[...], -1)))
    p.met()

    for step in range(1, most):
        if step < Z:
            push(lat_ref.at[:, halves[0]], pool.at[z * C + c], pool_sem.at[step * C + c], (lax.rem(z + step, Z), q * C))
        if step < Q:
            push(lat_ref.at[:, halves[1]], pool.at[q * C + c], pool_sem.at[step * C + c], (z, lax.rem(q + step, Q) * C + 1))
    give = pl.ds(pl.multiple_of((1 - c) * w2, 128), w2)
    push(lat_ref.at[:, give], pool.at[other_at * C + c], pool_sem.at[c], mate)
    edges = [go(pack.at[0], pack.at[3], esem, 0, (z, left)), go(pack.at[1], pack.at[2], esem, 1, (z, right))]
    for core in range(C):
        for step in range(1, Z):
            push(id_ref, ids.at[q, z, c], id_sem.at[step * C + c], (lax.rem(z + step, Z), q * C + core))
        for step in range(1, Q):
            push(id_ref, plane_ids.at[q, c], id_sem.at[(Z + step) * C + c], (z, lax.rem(q + step, Q) * C + core))
    push(id_ref, ids.at[q, z, c], id_sem.at[c], mate)
    push(id_ref, plane_ids.at[q, c], id_sem.at[Z * C + c], mate)
    above, below = p.rows
    first_rows, last_rows = lat_ref.at[pl.ds(0, edge)], lat_ref.at[pl.ds(nodes - edge, edge)]
    borders = [
        (last_rows, (below, p.lon)), (first_rows, (above, p.lon)), (cols, (z, right)), (cols, (z, left)),
        (last_rows, (below, right)), (last_rows, (below, left)), (first_rows, (above, right)), (first_rows, (above, left)),
    ]
    for k, (src, peer) in enumerate(borders):
        push(src, halo.at[k], halo_sem.at[k], peer)

    loads[5].wait()
    at_row, at_col = iota((height, breadth), 0), iota((height, breadth), 1)
    wheres = []
    first_line, last_line = jnp.where(z == 0, 1, 0), jnp.where(z == Z - 1, 1, 0)
    for k in range(slots):
        code = code_ref[k]
        down = jnp.where(code >= 6, 1, jnp.where(code >= 3, 0, -1))
        rows, columns = at_row + down, at_col + code - 3 * down - 4
        up, low = rows < 0, rows >= height
        before, after = columns < 0, columns >= breadth
        middle = jnp.where(before, nodes + 2 * edge + height + rows, jnp.where(after, nodes + 3 * edge + rows, rows * breadth + columns))
        top = jnp.where(before, nodes + 4 * edge + edge - 1, jnp.where(after, nodes + 5 * edge + edge - breadth, nodes + edge - breadth + columns))
        bottom = jnp.where(before, nodes + 6 * edge + breadth - 1, jnp.where(after, nodes + 7 * edge, nodes + edge + columns))
        spot = jnp.where(up, top - first_line * (1 << 20), jnp.where(low, bottom - last_line * (1 << 20), middle))
        wheres.append(column(spot))
    where = jnp.concatenate(wheres, 0)
    hot = jnp.broadcast_to(where, (where.shape[0], nodes + 8 * edge))
    hot = jnp.where(hot == iota(hot.shape, 1), 1.0, 0.0).astype(BF16)

    for copy in edges:
        copy.wait_recv()
    for side in range(2):
        keep_tally(side + 1, tally(pack[2 + side, 0], pack[2 + side, 1]))
    loads[6].wait()
    cot_sums = jnp.zeros((3 * nodes, width), F32)
    for g in range(groups):
        part = cot_ref[g * group_rows:(g + 1) * group_rows]
        cot_sums = cot_sums + mm(tally_high[g], part) + mm(tally_low[g], part)
    backs[0] = cot_sums[nodes:2 * nodes].astype(BF16)
    backs[1] = cot_sums[2 * nodes:3 * nodes].astype(BF16)
    returns = [go(backs.at[0], back.at[0], esem, 2, (z, left)), go(backs.at[1], back.at[1], esem, 3, (z, right))]

    for step in range(1, Z):
        for core in range(C):
            arrive(ids.at[q, lax.rem(z + Z - step, Z), core], id_sem.at[step * C + core])
    arrive(ids.at[q, z, 1 - c], id_sem.at[1 - c])
    for step in range(1, Q):
        push(ids.at[q], ids.at[q], id_sem.at[(Z + Q) * C + step], (z, lax.rem(q + step, Q) * C + c))
    for step in range(1, Q):
        for core in range(C):
            arrive(plane_ids.at[lax.rem(q + Q - step, Q), core], id_sem.at[(Z + step) * C + core])
    arrive(plane_ids.at[q, 1 - c], id_sem.at[Z * C + 1 - c])

    def id_rows(rows):
        rows = [jnp.sum(rows[at].reshape(C, C * nodes), 0, keepdims=True) for at in range(rows.shape[0])]
        return rows + [jnp.zeros_like(rows[0])] * (most - len(rows))

    line_rows, plane_rows = id_rows(ids[q]), id_rows(plane_ids[...])
    source_row = jnp.concatenate([jnp.where(c == 0, a, b) for a, b in zip(line_rows, plane_rows)], 1)
    eye = iota((C * nodes, C * nodes), 0) == iota((C * nodes, C * nodes), 1)
    tall = [jnp.where(c == 0, b, a) for a, b in zip(line_rows, plane_rows)]
    tall = [jnp.sum(jnp.where(eye, jnp.broadcast_to(row, eye.shape), 0), 1, keepdims=True) for row in tall]
    tall = jnp.concatenate(tall, 0)
    same = jnp.broadcast_to(tall, (tall.shape[0], source_row.shape[1])) == jnp.broadcast_to(source_row, (tall.shape[0], source_row.shape[1]))
    same = jnp.where(same, 1.0, 0.0).astype(BF16)

    loads[7].wait()
    toward = mm(latent, wt_ref[...])
    for k in range(len(borders)):
        arrive(halo.at[k], halo_sem.at[k])
    near = jnp.concatenate([latent, halo[...].reshape(8 * edge, width)], 0)
    beside = mm(hot, near).astype(BF16)
    loads[8].wait()
    edges_pre = mm(beside, ws_ref[...]).reshape(slots, nodes, width) + toward[None]
    agg = jnp.sum(edges_pre * jax.nn.sigmoid(edges_pre), 0).astype(BF16)

    for step in range(1, most):
        at = role_step(-step)
        for core in range(C):
            arrive(pool.at[at * C + core], pool_sem.at[step * C + core], limit(step, role_size))
    arrive(pool.at[role_at * C + 1 - c], pool_sem.at[1 - c])
    sums = mm(same, pool[...].reshape(most * C * nodes, w2)).astype(BF16)
    parts[...] = sums.reshape(most * C, nodes, w2)
    got[c, other_at] = parts[other_at * C + c]
    for step in range(1, most):
        at = jnp.where(c == 0, lax.rem(q + step, Q), lax.rem(z + step, Z))
        for core in range(C):
            peer = (jnp.where(c == 0, z, at), jnp.where(c == 0, at, q) * C + core)
            push(parts.at[at * C + core], got.at[c, other_at], got_sem.at[c * most + step], peer, limit(step, other_size))
    push(parts.at[other_at * C + 1 - c], got.at[c, other_at], got_sem.at[0], mate)
    loads[9].wait()
    agg_out = mm(agg, wn_ref[...])
    slope_edges = silu_slope(edges_pre)
    for step in range(1, Q):
        at = lax.rem(q + Q - step, Q)
        arrive(ids.at[at], id_sem.at[(Z + Q) * C + step])
    row = jnp.concatenate([r for at in range(Q) for r in [jnp.sum(ids[at, line].reshape(C, C * nodes), 0, keepdims=True) for line in range(Z)]], 1)
    alike = jnp.broadcast_to(row, (nodes, row.shape[1])) == jnp.broadcast_to(id_column, (nodes, row.shape[1]))
    count_of = jnp.sum(jnp.where(alike, 1.0, 0.0), 1, keepdims=True)
    scale = lax.rsqrt(count_of)
    for step in range(1, Q):
        arrive(got.at[0, lax.rem(q + Q - step, Q)], got_sem.at[step])
    for step in range(1, Z):
        arrive(got.at[1, lax.rem(z + Z - step, Z)], got_sem.at[most + step])
    arrive(got.at[1 - c, role_at], got_sem.at[0])
    pooled = [jnp.sum(got[0, 0:Q].astype(F32), 0), jnp.sum(got[1, 0:Z].astype(F32), 0)]
    coarse_in = (jnp.concatenate(pooled, 1) * scale).astype(BF16)
    loads[10].wait()
    cpre = mm(coarse_in, wc_ref[...])
    coarse_out = (cpre * jax.nn.sigmoid(cpre)).astype(BF16)

    npre = agg_out + coarse_out.astype(F32)
    mesh_out = (latent.astype(F32) + npre * jax.nn.sigmoid(npre)).astype(BF16)
    mesh_ref[...] = mesh_out

    loads[11].wait()
    pre = mm(mesh_out, wd_ref[...])
    msgs[0:nodes] = (pre * jax.nn.sigmoid(pre)).astype(BF16)
    mine = msgs.at[pl.ds(0, nodes)]

    one, two, three, four = {}, {}, {}, {}

    def hop_core(m, value):
        if R % 8 == 0:
            grad[m] = value.reshape(Z, Y, X, C, R, width)
        else:
            for q in range(Z * p.L):
                spot = (q // p.L, q // (C * X) % Y, q // C % X, q % C)
                grad[(m, *spot)] = value[q * R:(q + 1) * R]
        one[m] = []
        for off in range(1, C):
            there = lax.rem(c + off, C)
            k = m * (C - 1) + off - 1
            s1[k] = grad[m, :, :, :, there].astype(BF16)
            one[m].append((k, go(s1.at[k], r1.at[k], sem1, k, p.at(c=there))))

    def hop_first(m):
        total = grad[m, :, :, :, c]
        for k, copy in one[m]:
            copy.wait_recv()
            total = total + r1[k].astype(F32)
        acc1[m] = total
        two[m] = ([], [])
        for off in range(1, X):
            there = lax.rem(x + off, X)
            k = m * (X - 1) + off - 1
            s2[0][k] = acc1[m, :, :, there, :, halves[0]].astype(BF16)
            two[m][0].append((k, go(s2[0].at[k], r2[0].at[k], sem2[0], k, p.at(x=there))))
        for off in range(1, Y):
            there = lax.rem(y + off, Y)
            k = m * (Y - 1) + off - 1
            s2[1][k] = acc1[m, :, there, :, :, halves[1]].astype(BF16)
            two[m][1].append((k, go(s2[1].at[k], r2[1].at[k], sem2[1], k, p.at(y=there))))

    def hop_other(m):
        three[m] = ([], [])
        total = acc1[m, :, :, x, :, halves[0]]
        for k, copy in two[m][0]:
            copy.wait_recv()
            total = total + r2[0][k].astype(F32)
        acc2[0][m] = total
        for off in range(1, Y):
            there = lax.rem(y + off, Y)
            k = m * (Y - 1) + off - 1
            s3[0][k] = acc2[0][m, :, there].astype(BF16)
            three[m][0].append((k, go(s3[0].at[k], r3[0].at[k], sem3[0], k, p.at(y=there))))
        total = acc1[m, :, y, :, :, halves[1]]
        for k, copy in two[m][1]:
            copy.wait_recv()
            total = total + r2[1][k].astype(F32)
        acc2[1][m] = total
        for off in range(1, X):
            there = lax.rem(x + off, X)
            k = m * (X - 1) + off - 1
            s3[1][k] = acc2[1][m, :, there].astype(BF16)
            three[m][1].append((k, go(s3[1].at[k], r3[1].at[k], sem3[1], k, p.at(x=there))))

    def hop_line(m):
        for side, own in ((0, y), (1, x)):
            total = acc2[side][m, :, own]
            for k, copy in three[m][side]:
                copy.wait_recv()
                total = total + r3[side][k].astype(F32)
            acc3[m, :, :, halves[side]] = total
        four[m] = []
        for off in range(1, Z):
            there = lax.rem(z + off, Z)
            k = m * (Z - 1) + off - 1
            s4[k] = acc3[m, there].astype(BF16)
            four[m].append((k, go(s4.at[k], r4.at[k], sem4, k, (there, p.lon))))

    for copy in returns:
        copy.wait_recv()
    cot_sum = cot_sums[:nodes] + back[0].astype(F32) + back[1].astype(F32)
    d_high, d_low = split_float(cot_sum * silu_slope(pre))
    hop_core(4, mm_t(mesh_out, d_high) + mm_t(mesh_out, d_low))
    d_node = (mm_nt(d_high, wd_ref[...]) * silu_slope(npre)).astype(BF16)
    hop_core(2, mm_t(agg, d_node))
    hop_first(4)
    c_high, c_low = split_float(d_node.astype(F32) * silu_slope(cpre))
    hop_core(3, mm_t(coarse_in, c_high) + mm_t(coarse_in, c_low))
    hop_first(2)
    d_edges = (mm_nt(d_node, wn_ref[...])[None] * slope_edges).astype(BF16)
    d_sum = jnp.sum(d_edges.astype(F32), 0).astype(BF16)
    hop_core(1, mm_t(latent, d_sum))
    hop_first(3)
    hop_core(0, mm_t(beside, d_edges.reshape(slots * nodes, width)))
    hop_first(1)
    hop_first(0)
    order = (4, 2, 3, 1, 0)
    for at, m in enumerate(order):
        hop_other(m)
        if at:
            hop_line(order[at - 1])
    spoken = [
        go(mine, msgs.at[pl.ds(nodes, nodes)], esem, 4, (z, right)),
        go(mine, msgs.at[pl.ds(2 * nodes, nodes)], esem, 5, (z, left)),
    ]
    hop_line(order[-1])
    square = jnp.zeros(share.shape[1:], F32)
    for m in order:
        total = acc3[m, z]
        for k, copy in four[m]:
            copy.wait_recv()
            total = total + r4[k].astype(F32)
        share[m] = total
        square = square + total * total
    sq[0] = jnp.broadcast_to(jnp.sum(square, keepdims=True), sq.shape[1:])
    mine = []
    for off in range(1, Z):
        mine.append(go(sq.at[0], zq.at[off - 1], zsem, off - 1, (lax.rem(z + off, Z), p.lon)))
    for copy in spoken:
        copy.wait_recv()
    for g in range(groups):
        decoded = mm_t(tally_high[g], msgs[...]) + mm_t(tally_low[g], msgs[...])
        grid_ref[g * group_rows:(g + 1) * group_rows] = decoded.astype(BF16)
    whole = sq[0]
    for off, copy in enumerate(mine):
        copy.wait_recv()
        whole = whole + zq[off]
    sq[1] = whole
    mine = []
    for off in range(1, p.L):
        mine.append(go(sq.at[1], lq.at[off - 1], lsem, off - 1, (p.lat, lax.rem(p.lon + off, p.L))))
    for off, copy in enumerate(mine):
        copy.wait_recv()
        whole = whole + lq[off]
    norm = jnp.sqrt(whole[0:1, 0:1]) + 1e-06
    for m in range(many):
        total = share[m] / norm
        for r in range(R):
            out_ref[m:m + 1, r * width:(r + 1) * width] = total[r:r + 1]
    for only, copy in pushed:
        if only is None:
            copy.wait_send()
        else:
            pl.when(only)(copy.wait_send)
    for copy in copies:
        copy.wait_send()


def run_step(sizes, latent, cot, weights, codes, ids, source, target, owner):
    Z, Y, X, C = sizes
    L = Y * X * C
    many = len(weights)
    nodes, width = latent.shape
    grid_rows = cot.shape[0]
    blocks, block_len = source.shape
    slots, height, breadth = codes.shape
    edge = 2 * max(height, breadth)
    groups = 4 if grid_rows % 4 == 0 else 1
    group_rows = grid_rows // groups
    Q, most = Y * X, max(Z, Y * X)
    R = width // (Z * L)
    w2 = width // 2
    vmem = pl.BlockSpec(memory_space=pltpu.VMEM)

    def buf(dtype, *dims):
        return pltpu.VMEM(dims, dtype)

    def sems(*counts):
        return [pltpu.SemaphoreType.DMA((2, n)) for n in counts]

    def single(*counts):
        return [pltpu.SemaphoreType.DMA((n,)) for n in counts]

    nx, ny, nz, nc = many * (X - 1), many * (Y - 1), many * (Z - 1), many * (C - 1)
    second = [buf(BF16, nx, Z, Y, R, w2), buf(BF16, ny, Z, X, R, w2)]
    third = [buf(BF16, ny, Z, R, w2), buf(BF16, nx, Z, R, w2)]
    operands = [latent, cot, *weights, codes, ids, source, target, owner]
    pushes = Z - 1 + Q - 1 + 1 + C * (Z - 1 + Q - 1) + 2 + 8 + Q - 1 + C * (most - 1) + 1
    return pl.pallas_call(
        functools.partial(step_kernel, sizes),
        out_shape=(
            pltpu.VMEM((nodes, width), BF16),
            pltpu.VMEM((grid_rows, width), BF16),
            pltpu.VMEM((many, R * width), F32),
        ),
        in_specs=[pl.BlockSpec(memory_space=pltpu.HBM)] * len(operands),
        out_specs=(vmem,) * 3,
        scratch_shapes=[
            *[pltpu.VMEM(a.shape, a.dtype) for a in operands],
            buf(BF16, most * C, nodes, w2), buf(BF16, most * C, nodes, w2), buf(BF16, 2, most, nodes, w2),
            buf(jnp.int32, Q, Z, C, 1, C * nodes), buf(jnp.int32, Q, C, 1, C * nodes),
            buf(BF16, 8, edge, width), buf(BF16, edge, width), buf(jnp.int32, 4, 2, CAP, block_len),
            buf(BF16, groups, 3 * nodes, group_rows), buf(BF16, groups, 3 * nodes, group_rows),
            buf(BF16, 2, nodes, width), buf(BF16, 2, nodes, width), buf(BF16, 3 * nodes, width),
            buf(F32, many, Z, Y, X, C, R, width),
            buf(BF16, nc, Z, Y, X, R, width), buf(BF16, nc, Z, Y, X, R, width),
            buf(F32, many, Z, Y, X, R, width),
            second, second, [buf(F32, many, Z, Y, R, w2), buf(F32, many, Z, X, R, w2)],
            third, third, buf(F32, many, Z, R, width),
            buf(BF16, nz, R, width), buf(BF16, nz, R, width),
            buf(F32, 2, 8, 128), buf(F32, Z - 1, 8, 128), buf(F32, L - 1, 8, 128),
            buf(jnp.int32, 1, C * nodes), buf(F32, many, R, width),
            *single(len(operands), pushes, most * C, 2 * most, (Z + Q) * C + Q, 8), *sems(6, nc), sems(nx, ny), sems(ny, nx), *sems(nz, Z - 1, L - 1),
        ],
        compiler_params=pltpu.CompilerParams(
            collective_id=0, has_side_effects=True, vmem_limit_bytes=56 * 1024 * 1024
        ),
        name="whole_step",
    )(*[pltpu.with_memory_space_constraint(a, pltpu.HBM) for a in operands])


def write_kernel(*refs):
    count = len(refs) // 2
    sems = refs[-1]
    moves = [pltpu.make_async_copy(refs[i], refs[count + i], sems.at[i]) for i in range(count)]
    for move in moves:
        move.start()
    for move in moves:
        move.wait()


def write_results(*results):
    return pl.pallas_call(
        write_kernel,
        out_shape=tuple(jax.ShapeDtypeStruct(r.shape, r.dtype) for r in results),
        in_specs=[pl.BlockSpec(memory_space=pltpu.VMEM)] * len(results),
        out_specs=(pl.BlockSpec(memory_space=pl.ANY),) * len(results),
        scratch_shapes=[pltpu.SemaphoreType.DMA((len(results),))],
        compiler_params=pltpu.CompilerParams(vmem_limit_bytes=8 * 1024 * 1024),
        name="write_results",
    )(*results)


def lon_parts(lat_count, lon_count):
    chips = lon_count // 2
    x = next(d for d in range(math.isqrt(chips), 0, -1) if chips % d == 0)
    return lat_count, chips // x, x, 2


def local(
    mesh_latent,
    grid_cotangent,
    w_source,
    w_target,
    w_node,
    w_coarse,
    w_decode,
    neighbour_codes,
    coarse_ids,
    edge_source,
    edge_target,
    edge_owner,
):
    height, breadth, width = mesh_latent.shape
    nodes = height * breadth
    sizes = lon_parts(lax.axis_size("lat"), lax.axis_size("lon"))
    blocks = edge_owner.shape[0]
    mesh_out, grid_out, clipped = run_step(
        sizes,
        mesh_latent.reshape(nodes, width),
        grid_cotangent,
        (w_source, w_target, w_node, w_coarse, w_decode),
        neighbour_codes,
        coarse_ids.reshape(height, breadth),
        edge_source.reshape(blocks, -1),
        edge_target.reshape(blocks, -1),
        edge_owner.reshape(1, blocks),
    )
    mesh_out, grid_out, clipped = write_results(mesh_out, grid_out, clipped)
    return (mesh_out.reshape(height, breadth, width), grid_out, clipped)


def solution(mesh):
    in_specs = (
        P("lat", "lon", None),
        P(("lat", "lon"), None),
        P(),
        P(),
        P(),
        P(),
        P(),
        P(None, "lat", "lon"),
        P("lat", "lon", None),
        P(("lat", "lon")),
        P(("lat", "lon")),
        P(("lat", "lon"), None),
    )
    out_specs = (P("lat", "lon", None), P(("lat", "lon"), None), P(None, ("lat", "lon")))
    return jax.shard_map(local, mesh=mesh, in_specs=in_specs, out_specs=out_specs, check_vma=False)
```

```python
import functools
import math

import jax
import jax.numpy as jnp
from jax import lax
from jax.experimental import pallas as pl
from jax.experimental.pallas import tpu as pltpu
from jax.sharding import PartitionSpec as P

CAP = 3
F32 = jnp.float32
BF16 = jnp.bfloat16


def silu_slope(value):
    sig = jax.nn.sigmoid(value)
    return sig * (1.0 + value * (1.0 - sig))


def mm(left, right):
    return jnp.dot(left, right, preferred_element_type=F32)


def mm_t(left, right):
    return lax.dot_general(left, right, (((0,), (0,)), ((), ())), preferred_element_type=F32)


def mm_nt(left, right):
    return lax.dot_general(left, right, (((1,), (1,)), ((), ())), preferred_element_type=F32)


def split_float(value):
    high = value.astype(BF16)
    return high, (value - high.astype(F32)).astype(BF16)


MESH = pl.DeviceIdType.MESH


class Place:
    def __init__(self, sizes):
        self.Z, self.Y, self.X, self.C = sizes
        self.L = self.Y * self.X * self.C
        self.lat, self.lon = lax.axis_index("lat"), lax.axis_index("lon")
        self.z, self.c = self.lat, lax.rem(self.lon, self.C)
        self.x = lax.rem(self.lon // self.C, self.X)
        self.y = self.lon // (self.C * self.X)
        self.Q, self.q = self.Y * self.X, self.lon // self.C
        self.rows = (lax.rem(self.z + self.Z - 1, self.Z), lax.rem(self.z + 1, self.Z))
        self.sides = (lax.rem(self.lon + self.L - 1, self.L), lax.rem(self.lon + 1, self.L))

    def at(self, y=None, x=None, c=None):
        y, x, c = (old if new is None else new for new, old in ((y, self.y), (x, self.x), (c, self.c)))
        return (self.lat, (y * self.X + x) * self.C + c)

    def greeted(self):
        line = [(lax.rem(self.z + step, self.Z), self.q * self.C + core) for step in range(1, self.Z) for core in range(self.C)]
        plane = [(self.z, lax.rem(self.lon + step, self.L)) for step in range(1, self.L)]
        return line + plane + [(lat, lon) for lat in self.rows for lon in self.sides]

    def meet(self):
        barrier = pltpu.get_barrier_semaphore()
        for peer in self.greeted():
            pl.semaphore_signal(barrier, inc=1, device_id=peer, device_id_type=MESH)

    def met(self):
        pl.semaphore_wait(pltpu.get_barrier_semaphore(), len(self.greeted()))


def send(src, dst, sems, slot, peer):
    copy = pltpu.make_async_remote_copy(
        src_ref=src, dst_ref=dst, send_sem=sems.at[0, slot], recv_sem=sems.at[1, slot],
        device_id=peer, device_id_type=MESH,
    )
    copy.start()
    return copy


def iota(shape, dim):
    return lax.broadcasted_iota(jnp.int32, shape, dim)


def step_kernel(sizes, *refs):
    (lat_hbm, cot_hbm, ws_hbm, wt_hbm, wn_hbm, wc_hbm, wd_hbm, code_hbm, coarse_hbm, src_hbm, tgt_hbm,
     owner_hbm) = refs[:12]
    mesh_ref, grid_ref, out_ref = refs[12:15]
    (lat_ref, cot_ref, ws_ref, wt_ref, wn_ref, wc_ref, wd_ref, code_ref, coarse_ref, src_ref, tgt_ref, owner_ref,
     pool, parts, got, ids, plane_ids, halo, cols, pack, tally_high, tally_low, back, backs, msgs, id_ref, grad, grad_out,
     core_in, pair, pair_out, line_wide, plane_wide, x_wide, y_wide, x_sum, y_sum, x_out, y_out, x_slim, y_slim, line_sum, line_out, plane_sum, plane_out, plane_slim, line_slim,
     share, square_out, square_line, squares) = refs[15:66]
    (load_sem, out_sem, pool_sem, got_sem, id_sem, halo_sem, esem, core_sem, line_wide_sem, x_sem, y_sem, x_slim_sem, y_slim_sem, plane_wide_sem, plane_slim_sem,
     line_slim_sem, square_sem) = refs[66:]
    p = Place(sizes)
    Z, Y, X, C, z, y, x, c = p.Z, p.Y, p.X, p.C, p.z, p.y, p.x, p.c
    Q, q = p.Q, p.q
    nodes, width = lat_ref.shape
    grid_rows = cot_ref.shape[0]
    blocks, block_len = src_ref.shape
    groups, _, group_rows = tally_high.shape
    many = out_ref.shape[0]
    R = line_sum.shape[3]
    w2 = width // 2
    halves = (pl.ds(0, w2), pl.ds(w2, w2))
    copies, pushed = [], []
    mate = (z, q * C + 1 - c)
    most = max(Z, Q)
    role_size, role_at = jnp.where(c == 0, Z, Q), jnp.where(c == 0, z, q)
    other_size, other_at = jnp.where(c == 0, Q, Z), jnp.where(c == 0, q, z)

    def go(src, dst, sems, slot, peer):
        copy = send(src, dst, sems, slot, peer)
        copies.append(copy)
        return copy

    used = [0]

    def describe(src, dst, recv, peer, send_sem=None):
        return pltpu.make_async_remote_copy(
            src_ref=src, dst_ref=dst, send_sem=recv if send_sem is None else send_sem, recv_sem=recv, device_id=peer,
            device_id_type=MESH)

    def push(src, dst, recv, peer, only=None):
        copy = describe(src, dst, recv, peer, out_sem.at[used[0]])
        used[0] += 1
        if only is None:
            copy.start()
        else:
            pl.when(only)(copy.start)
        pushed.append((only, copy))

    def arrive(dst, recv, only=None):
        if only is None:
            describe(dst, dst, recv, mate).wait_recv()
        else:
            pl.when(only)(lambda: describe(dst, dst, recv, mate).wait_recv())

    def role_step(step):
        return jnp.where(c == 0, lax.rem(z + most * Z + step, Z), lax.rem(q + most * Q + step, Q))

    def limit(step, size):
        return step < size if step >= min(Z, Q) else None

    if Z != Q:
        pool[...] = jnp.zeros_like(pool)
    p.meet()
    needed = (src_hbm, tgt_hbm, owner_hbm, coarse_hbm, lat_hbm, code_hbm, cot_hbm, wt_hbm, ws_hbm, wn_hbm, wc_hbm, wd_hbm)
    places = (src_ref, tgt_ref, owner_ref, coarse_ref, lat_ref, code_ref, cot_ref, wt_ref, ws_ref, wn_ref, wc_ref, wd_ref)
    loads = [pltpu.make_async_copy(a, b, load_sem.at[i]) for i, (a, b) in enumerate(zip(needed, places))]
    for at in (4, 3, 0, 1, 2, 5, 6, 7, 8, 9, 10, 11):
        loads[at].start()
    slots, height, breadth = code_ref.shape
    edge = halo.shape[1]

    def column(square):
        tall = jnp.concatenate([jnp.broadcast_to(square[i:i + 1], (breadth, breadth)) for i in range(height)], 0)
        keep = iota(tall.shape, 0) % breadth == iota(tall.shape, 1)
        return jnp.sum(jnp.where(keep, tall, 0), 1, keepdims=True)

    loads[4].wait()
    latent = lat_ref[...]
    pick = iota((edge, nodes), 0)
    pick = jnp.where(pick < height, pick * breadth, (pick - height) * breadth + breadth - 1)
    cols[...] = mm(jnp.where(pick == iota(pick.shape, 1), 1.0, 0.0).astype(BF16), latent).astype(BF16)
    pool[role_at * C + c] = lat_ref[:, pl.ds(pl.multiple_of(c * w2, 128), w2)]

    loads[3].wait()
    id_column = column(coarse_ref[...]) + 1
    spread = (nodes, id_ref.shape[1])
    keep = iota(spread, 1) == iota(spread, 0) + c * nodes
    id_row = jnp.sum(jnp.where(keep, jnp.broadcast_to(id_column, spread), 0), 0, keepdims=True)
    id_ref[...] = id_row
    ids[q, z, c] = id_row
    plane_ids[q, c] = id_row
    left, right = p.sides
    p.met()

    for step in range(1, most):
        if step < Z:
            push(lat_ref.at[:, halves[0]], pool.at[z * C + c], pool_sem.at[step * C + c], (lax.rem(z + step, Z), q * C))
        if step < Q:
            push(lat_ref.at[:, halves[1]], pool.at[q * C + c], pool_sem.at[step * C + c], (z, lax.rem(q + step, Q) * C + 1))
    give = pl.ds(pl.multiple_of((1 - c) * w2, 128), w2)
    push(lat_ref.at[:, give], pool.at[other_at * C + c], pool_sem.at[c], mate)
    for core in range(C):
        for step in range(1, Z):
            push(id_ref, ids.at[q, z, c], id_sem.at[step * C + c], (lax.rem(z + step, Z), q * C + core))
        for step in range(1, Q):
            push(id_ref, plane_ids.at[q, c], id_sem.at[(Z + step) * C + c], (z, lax.rem(q + step, Q) * C + core))
    push(id_ref, ids.at[q, z, c], id_sem.at[c], mate)
    push(id_ref, plane_ids.at[q, c], id_sem.at[Z * C + c], mate)
    above, below = p.rows
    first_rows, last_rows = lat_ref.at[pl.ds(0, edge)], lat_ref.at[pl.ds(nodes - edge, edge)]
    borders = [
        (last_rows, (below, p.lon)), (first_rows, (above, p.lon)), (cols, (z, right)), (cols, (z, left)),
        (last_rows, (below, right)), (last_rows, (below, left)), (first_rows, (above, right)), (first_rows, (above, left)),
    ]
    for k, (src, peer) in enumerate(borders):
        push(src, halo.at[k], halo_sem.at[k], peer)

    def met_line():
        for step in range(1, Z):
            for core in range(C):
                arrive(ids.at[q, lax.rem(z + Z - step, Z), core], id_sem.at[step * C + core])
        arrive(ids.at[q, z, 1 - c], id_sem.at[1 - c])

    def met_plane():
        for step in range(1, Q):
            for core in range(C):
                arrive(plane_ids.at[lax.rem(q + Q - step, Q), core], id_sem.at[(Z + step) * C + core])
        arrive(plane_ids.at[q, 1 - c], id_sem.at[Z * C + 1 - c])

    def met_halo():
        for k in range(len(borders)):
            arrive(halo.at[k], halo_sem.at[k])

    def met_pool():
        for step in range(1, most):
            at = role_step(-step)
            for core in range(C):
                arrive(pool.at[at * C + core], pool_sem.at[step * C + core], limit(step, role_size))
        arrive(pool.at[role_at * C + 1 - c], pool_sem.at[1 - c])

    def met_ids():
        for step in range(1, Q):
            arrive(ids.at[lax.rem(q + Q - step, Q)], id_sem.at[(Z + Q) * C + step])

    def met_got():
        for step in range(1, Q):
            arrive(got.at[0, lax.rem(q + Q - step, Q)], got_sem.at[step])
        for step in range(1, Z):
            arrive(got.at[1, lax.rem(z + Z - step, Z)], got_sem.at[most + step])
        arrive(got.at[1 - c, role_at], got_sem.at[0])

    for load in loads[:3]:
        load.wait()
    sub, lane = iota((blocks, blocks), 0), iota((blocks, blocks), 1)
    owner = jnp.broadcast_to(owner_ref[...], (blocks, blocks))
    owner = jnp.sum(jnp.where(sub == lane, owner, 0), 1, keepdims=True)
    is_left = (owner == left).astype(jnp.int32)
    is_right = (owner == right).astype(jnp.int32)

    def ranks(column):
        row = jnp.sum(jnp.where(sub == lane, jnp.broadcast_to(column, sub.shape), 0), 0, keepdims=True)
        return jnp.sum(jnp.where(lane < sub, jnp.broadcast_to(row, sub.shape), 0), 1, keepdims=True)

    place = jnp.where(is_left == 1, ranks(is_left), jnp.where(is_right == 1, CAP + ranks(is_right), -1))
    wide_place = jnp.broadcast_to(place, (blocks, block_len))
    for r in range(2 * CAP):
        mine = wide_place == r
        side, row = divmod(r, CAP)
        pack[side, 0, row:row + 1] = jnp.sum(jnp.where(mine, src_ref[...], 0), 0, keepdims=True)
        pack[side, 1, row:row + 1] = jnp.sum(jnp.where(mine, tgt_ref[...] + 1, 0), 0, keepdims=True) - 1
    edges = [go(pack.at[0], pack.at[3], esem, 0, (z, left)), go(pack.at[1], pack.at[2], esem, 1, (z, right))]
    def tally(source, target):
        tall = jnp.where(target < 0, -1, target % group_rows)
        both = jnp.where(target < 0, 0, target // group_rows) * nodes + source
        count = source.shape[0]
        tall = jnp.concatenate([tall[r:r + 1] for r in range(count)], 1)
        both = jnp.concatenate([both[r:r + 1] for r in range(count)], 1)
        tall = jnp.broadcast_to(tall, (group_rows, tall.shape[1]))
        both = jnp.broadcast_to(both, (groups * nodes, both.shape[1]))
        hot_t = jnp.where(tall == iota(tall.shape, 0), 1.0, 0.0).astype(BF16)
        hot_b = jnp.where(both == iota(both.shape, 0), 1.0, 0.0).astype(BF16)
        return mm_nt(hot_b, hot_t)

    def keep_tally(kind, counts):
        over = jnp.floor(counts * (1.0 / 256.0)) * 256.0
        high, low = over.astype(BF16), (counts - over).astype(BF16)
        for g in range(groups):
            tally_high[g, kind * nodes:(kind + 1) * nodes] = high[g * nodes:(g + 1) * nodes]
            tally_low[g, kind * nodes:(kind + 1) * nodes] = low[g * nodes:(g + 1) * nodes]

    stays = jnp.broadcast_to((owner == p.lon).astype(jnp.int32), (blocks, block_len))
    keep_tally(0, tally(src_ref[...], jnp.where(stays == 1, tgt_ref[...], -1)))

    loads[5].wait()
    at_row, at_col = iota((height, breadth), 0), iota((height, breadth), 1)
    wheres = []
    first_line, last_line = jnp.where(z == 0, 1, 0), jnp.where(z == Z - 1, 1, 0)
    for k in range(slots):
        code = code_ref[k]
        down = jnp.where(code >= 6, 1, jnp.where(code >= 3, 0, -1))
        rows, columns = at_row + down, at_col + code - 3 * down - 4
        up, low = rows < 0, rows >= height
        before, after = columns < 0, columns >= breadth
        middle = jnp.where(before, nodes + 2 * edge + height + rows, jnp.where(after, nodes + 3 * edge + rows, rows * breadth + columns))
        top = jnp.where(before, nodes + 4 * edge + edge - 1, jnp.where(after, nodes + 5 * edge + edge - breadth, nodes + edge - breadth + columns))
        bottom = jnp.where(before, nodes + 6 * edge + breadth - 1, jnp.where(after, nodes + 7 * edge, nodes + edge + columns))
        spot = jnp.where(up, top - first_line * (1 << 20), jnp.where(low, bottom - last_line * (1 << 20), middle))
        wheres.append(column(spot))
    where = jnp.concatenate(wheres, 0)
    hot = jnp.broadcast_to(where, (where.shape[0], nodes + 8 * edge))
    hot = jnp.where(hot == iota(hot.shape, 1), 1.0, 0.0).astype(BF16)

    for copy in edges:
        copy.wait_recv()
    for side in range(2):
        keep_tally(side + 1, tally(pack[2 + side, 0], pack[2 + side, 1]))
    loads[6].wait()
    cot_sums = jnp.zeros((3 * nodes, width), F32)
    for g in range(groups):
        part = cot_ref[g * group_rows:(g + 1) * group_rows]
        cot_sums = cot_sums + mm(tally_high[g], part) + mm(tally_low[g], part)
    backs[0] = cot_sums[nodes:2 * nodes].astype(BF16)
    backs[1] = cot_sums[2 * nodes:3 * nodes].astype(BF16)
    returns = [go(backs.at[0], back.at[0], esem, 2, (z, left)), go(backs.at[1], back.at[1], esem, 3, (z, right))]

    met_line()
    for step in range(1, Q):
        push(ids.at[q], ids.at[q], id_sem.at[(Z + Q) * C + step], (z, lax.rem(q + step, Q) * C + c))
    met_plane()

    def id_rows(rows):
        rows = [jnp.sum(rows[at].reshape(C, C * nodes), 0, keepdims=True) for at in range(rows.shape[0])]
        return rows + [jnp.zeros_like(rows[0])] * (most - len(rows))

    line_rows, plane_rows = id_rows(ids[q]), id_rows(plane_ids[...])
    source_row = jnp.concatenate([jnp.where(c == 0, a, b) for a, b in zip(line_rows, plane_rows)], 1)
    eye = iota((C * nodes, C * nodes), 0) == iota((C * nodes, C * nodes), 1)
    tall = [jnp.where(c == 0, b, a) for a, b in zip(line_rows, plane_rows)]
    tall = [jnp.sum(jnp.where(eye, jnp.broadcast_to(row, eye.shape), 0), 1, keepdims=True) for row in tall]
    tall = jnp.concatenate(tall, 0)
    same = jnp.broadcast_to(tall, (tall.shape[0], source_row.shape[1])) == jnp.broadcast_to(source_row, (tall.shape[0], source_row.shape[1]))
    same = jnp.where(same, 1.0, 0.0).astype(BF16)

    loads[7].wait()
    toward = mm(latent, wt_ref[...])
    met_halo()
    near = jnp.concatenate([latent, halo[...].reshape(8 * edge, width)], 0)
    beside = mm(hot, near).astype(BF16)
    loads[8].wait()
    edges_pre = mm(beside, ws_ref[...]).reshape(slots, nodes, width) + toward[None]
    agg = jnp.sum(edges_pre * jax.nn.sigmoid(edges_pre), 0).astype(BF16)

    met_pool()
    sums = mm(same, pool[...].reshape(most * C * nodes, w2)).astype(BF16)
    parts[...] = sums.reshape(most * C, nodes, w2)
    got[c, other_at] = parts[other_at * C + c]
    for step in range(1, most):
        at = jnp.where(c == 0, lax.rem(q + step, Q), lax.rem(z + step, Z))
        for core in range(C):
            peer = (jnp.where(c == 0, z, at), jnp.where(c == 0, at, q) * C + core)
            push(parts.at[at * C + core], got.at[c, other_at], got_sem.at[c * most + step], peer, limit(step, other_size))
    push(parts.at[other_at * C + 1 - c], got.at[c, other_at], got_sem.at[0], mate)
    loads[9].wait()
    agg_out = mm(agg, wn_ref[...])
    slope_edges = silu_slope(edges_pre)
    met_ids()
    row = jnp.concatenate([r for at in range(Q) for r in [jnp.sum(ids[at, line].reshape(C, C * nodes), 0, keepdims=True) for line in range(Z)]], 1)
    alike = jnp.broadcast_to(row, (nodes, row.shape[1])) == jnp.broadcast_to(id_column, (nodes, row.shape[1]))
    count_of = jnp.sum(jnp.where(alike, 1.0, 0.0), 1, keepdims=True)
    scale = lax.rsqrt(count_of)
    met_got()
    pooled = [jnp.sum(got[0, 0:Q].astype(F32), 0), jnp.sum(got[1, 0:Z].astype(F32), 0)]
    coarse_in = (jnp.concatenate(pooled, 1) * scale).astype(BF16)
    loads[10].wait()
    cpre = mm(coarse_in, wc_ref[...])
    coarse_out = (cpre * jax.nn.sigmoid(cpre)).astype(BF16)

    npre = agg_out + coarse_out.astype(F32)
    mesh_out = (latent.astype(F32) + npre * jax.nn.sigmoid(npre)).astype(BF16)
    mesh_ref[...] = mesh_out

    loads[11].wait()
    pre = mm(mesh_out, wd_ref[...])
    msgs[0:nodes] = (pre * jax.nn.sigmoid(pre)).astype(BF16)
    mine = msgs.at[pl.ds(0, nodes)]

    kinds = ("half", "half", "half", "half", "line")
    line_first = [m for m in range(many) if kinds[m] == "line"]
    cut = Z // 2
    near_z, far_z = pl.ds(0, cut), pl.ds(cut, Z - cut)

    def hop_core(m, value):
        if R % 8 == 0:
            whole = value.reshape(Z, Y, X, C, R, width)
            grad[m] = whole
            grad_out[m] = whole.astype(BF16)
        else:
            for at in range(Z * Q * C):
                spot = (at // (Q * C), at // (C * X) % Y, at // C % X, at % C)
                grad[(m, *spot)] = value[at * R:(at + 1) * R]
                grad_out[(m, *spot)] = value[at * R:(at + 1) * R].astype(BF16)
        one[m] = go(grad_out.at[m, :, :, :, 1 - c], core_in.at[m], core_sem, m, mate)

    def hop_first(m):
        one[m].wait_recv()
        total = grad[m, :, :, :, c] + core_in[m].astype(F32)
        pair[m] = total
        pair_out[m] = total.astype(BF16)
        two[m] = []
        if kinds[m] == "line":
            for off in range(1, Z):
                there, k = lax.rem(z + off, Z), line_first.index(m) * (Z - 1) + off - 1
                two[m].append((k, go(pair_out.at[m, there], line_wide.at[k], line_wide_sem, k, (there, p.lon))))
        elif kinds[m] == "plane":
            for off in range(1, Q):
                there, k = lax.rem(q + off, Q), m * (Q - 1) + off - 1
                src = pair_out.at[m, :, there // X, lax.rem(there, X)]
                two[m].append((k, go(src, plane_wide.at[k], plane_wide_sem, k, (z, there * C + c))))
        else:
            for off in range(1, X):
                there, k = lax.rem(x + off, X), m * (X - 1) + off - 1
                two[m].append((0, k, go(pair_out.at[m, near_z, :, there], x_wide.at[k], x_sem, k, p.at(x=there))))
            for off in range(1, Y):
                there, k = lax.rem(y + off, Y), m * (Y - 1) + off - 1
                two[m].append((1, k, go(pair_out.at[m, far_z, there], y_wide.at[k], y_sem, k, p.at(y=there))))

    def hop_middle(m):
        totals = [pair[m, near_z, :, x], pair[m, far_z, y]]
        middle[m] = []
        for side, k, copy in two[m]:
            copy.wait_recv()
            totals[side] = totals[side] + (y_wide if side else x_wide)[k].astype(F32)
        x_sum[m], y_sum[m] = totals
        x_out[m], y_out[m] = totals[0].astype(BF16), totals[1].astype(BF16)
        for off in range(1, Y):
            there, k = lax.rem(y + off, Y), m * (Y - 1) + off - 1
            middle[m].append((0, k, go(x_out.at[m, :, there], x_slim.at[k], x_slim_sem, k, p.at(y=there))))
        for off in range(1, X):
            there, k = lax.rem(x + off, X), m * (X - 1) + off - 1
            middle[m].append((1, k, go(y_out.at[m, :, there], y_slim.at[k], y_slim_sem, k, p.at(x=there))))

    def hop_second(m):
        three[m] = []
        if kinds[m] == "line":
            total, at = pair[m, z], line_first.index(m)
            for k, copy in two[m]:
                copy.wait_recv()
                total = total + line_wide[k].astype(F32)
            line_sum[at] = total
            line_out[at] = total.astype(BF16)
            for off in range(1, Q):
                there, k = lax.rem(q + off, Q), at * (Q - 1) + off - 1
                src = line_out.at[at, there // X, lax.rem(there, X)]
                three[m].append((k, go(src, plane_slim.at[k], plane_slim_sem, k, (z, there * C + c))))
            return
        if kinds[m] == "plane":
            total = pair[m, :, y, x]
            for k, copy in two[m]:
                copy.wait_recv()
                total = total + plane_wide[k].astype(F32)
            plane_sum[m] = total
            plane_out[m] = total.astype(BF16)
        else:
            totals = [x_sum[m, :, y], y_sum[m, :, x]]
            for side, k, copy in middle[m]:
                copy.wait_recv()
                totals[side] = totals[side] + (y_slim if side else x_slim)[k].astype(F32)
            plane_sum[m, near_z], plane_sum[m, far_z] = totals
            plane_out[m, near_z], plane_out[m, far_z] = totals[0].astype(BF16), totals[1].astype(BF16)
        for off in range(1, Z):
            there, k = lax.rem(z + off, Z), m * (Z - 1) + off - 1
            three[m].append((k, go(plane_out.at[m, there], line_slim.at[k], line_slim_sem, k, (there, p.lon))))

    def last(m):
        total = line_sum[line_first.index(m), y, x] if m in line_first else plane_sum[m, z]
        for k, copy in three[m]:
            copy.wait_recv()
            total = total + (plane_slim[k] if m in line_first else line_slim[k]).astype(F32)
        for r in range(R):
            share[m:m + 1, r * width:(r + 1) * width] = total[r:r + 1]
        return total * total

    one, two, middle, three = {}, {}, {}, {}
    for copy in returns:
        copy.wait_recv()
    cot_sum = cot_sums[:nodes] + back[0].astype(F32) + back[1].astype(F32)
    d_high, d_low = split_float(cot_sum * silu_slope(pre))
    hop_core(4, mm_t(mesh_out, d_high) + mm_t(mesh_out, d_low))
    d_node = (mm_nt(d_high, wd_ref[...]) * silu_slope(npre)).astype(BF16)
    hop_core(2, mm_t(agg, d_node))
    hop_first(4)
    c_high, c_low = split_float(d_node.astype(F32) * silu_slope(cpre))
    hop_core(3, mm_t(coarse_in, c_high) + mm_t(coarse_in, c_low))
    hop_first(2)
    d_edges = (mm_nt(d_node, wn_ref[...])[None] * slope_edges).astype(BF16)
    d_sum = jnp.sum(d_edges.astype(F32), 0).astype(BF16)
    hop_core(1, mm_t(latent, d_sum))
    hop_first(3)
    hop_core(0, mm_t(beside, d_edges.reshape(slots * nodes, width)))
    hop_first(1)
    hop_first(0)
    hop_middle(2)
    hop_middle(3)
    hop_middle(1)
    hop_second(4)
    hop_middle(0)
    spoken = [
        go(mine, msgs.at[pl.ds(nodes, nodes)], esem, 4, (z, right)),
        go(mine, msgs.at[pl.ds(2 * nodes, nodes)], esem, 5, (z, left)),
    ]
    hop_second(2)
    hop_second(3)
    hop_second(1)
    hop_second(0)
    for copy in spoken:
        copy.wait_recv()
    for g in range(groups):
        decoded = mm_t(tally_high[g], msgs[...]) + mm_t(tally_low[g], msgs[...])
        grid_ref[g * group_rows:(g + 1) * group_rows] = decoded.astype(BF16)
    square = jnp.zeros((R, width), F32)
    for m in (2, 3, 4, 1, 0):
        square = square + last(m)
    square = sum(square[:, k * 128:(k + 1) * 128] for k in range(width // 128))
    square = jnp.broadcast_to(jnp.sum(square, keepdims=True), square_out.shape)
    square_out[...] = square
    mine = []
    for step in range(1, Z * p.L):
        peer = (lax.rem(z + step // p.L, Z), lax.rem(p.lon + step % p.L, p.L))
        mine.append(go(square_out, squares.at[step - 1], square_sem, step - 1, peer))
    for copy in mine:
        copy.wait_recv()
    norm = jnp.sqrt(square + jnp.sum(squares[...], 0))[:, 0:1] + 1e-06
    out_ref[...] = share[...] * (1.0 / norm)
    for only, copy in pushed:
        if only is None:
            copy.wait_send()
        else:
            pl.when(only)(copy.wait_send)
    for copy in copies:
        copy.wait_send()


def run_step(sizes, latent, cot, weights, codes, ids, source, target, owner):
    Z, Y, X, C = sizes
    L = Y * X * C
    many = len(weights)
    nodes, width = latent.shape
    grid_rows = cot.shape[0]
    blocks, block_len = source.shape
    slots, height, breadth = codes.shape
    edge = 2 * max(height, breadth)
    groups = 4 if grid_rows % 4 == 0 else 1
    group_rows = grid_rows // groups
    Q, most = Y * X, max(Z, Y * X)
    R = width // (Z * L)
    w2 = width // 2
    vmem = pl.BlockSpec(memory_space=pltpu.VMEM)

    def buf(dtype, *dims):
        return pltpu.VMEM(dims, dtype)

    def sems(*counts):
        return [pltpu.SemaphoreType.DMA((2, n)) for n in counts]

    def single(*counts):
        return [pltpu.SemaphoreType.DMA((n,)) for n in counts]

    cut = Z // 2
    operands = [latent, cot, *weights, codes, ids, source, target, owner]
    pushes = Z - 1 + Q - 1 + 1 + C * (Z - 1 + Q - 1) + 2 + 8 + Q - 1 + C * (most - 1) + 1
    return pl.pallas_call(
        functools.partial(step_kernel, sizes),
        out_shape=(
            pltpu.VMEM((nodes, width), BF16),
            pltpu.VMEM((grid_rows, width), BF16),
            pltpu.VMEM((many, R * width), F32),
        ),
        in_specs=[pl.BlockSpec(memory_space=pltpu.HBM)] * len(operands),
        out_specs=(vmem,) * 3,
        scratch_shapes=[
            *[pltpu.VMEM(a.shape, a.dtype) for a in operands],
            buf(BF16, most * C, nodes, w2), buf(BF16, most * C, nodes, w2), buf(BF16, 2, most, nodes, w2),
            buf(jnp.int32, Q, Z, C, 1, C * nodes), buf(jnp.int32, Q, C, 1, C * nodes),
            buf(BF16, 8, edge, width), buf(BF16, edge, width), buf(jnp.int32, 4, 2, CAP, block_len),
            buf(BF16, groups, 3 * nodes, group_rows), buf(BF16, groups, 3 * nodes, group_rows),
            buf(BF16, 2, nodes, width), buf(BF16, 2, nodes, width), buf(BF16, 3 * nodes, width),
            buf(jnp.int32, 1, C * nodes),
            buf(F32, many, Z, Y, X, C, R, width), buf(BF16, many, Z, Y, X, C, R, width), buf(BF16, many, Z, Y, X, R, width),
            buf(F32, many, Z, Y, X, R, width), buf(BF16, many, Z, Y, X, R, width),
            buf(BF16, many * (Z - 1), Y, X, R, width), buf(BF16, many * (Q - 1), Z, R, width),
            buf(BF16, many * (X - 1), cut, Y, R, width), buf(BF16, many * (Y - 1), Z - cut, X, R, width),
            buf(F32, many, cut, Y, R, width), buf(F32, many, Z - cut, X, R, width),
            buf(BF16, many, cut, Y, R, width), buf(BF16, many, Z - cut, X, R, width),
            buf(BF16, many * (Y - 1), cut, R, width), buf(BF16, many * (X - 1), Z - cut, R, width),
            buf(F32, many, Y, X, R, width), buf(BF16, many, Y, X, R, width), buf(F32, many, Z, R, width),
            buf(BF16, many, Z, R, width),
            buf(BF16, many * (Q - 1), R, width), buf(BF16, many * (Z - 1), R, width),
            buf(F32, many, R * width), buf(F32, 1, 128), buf(F32, 1, 128), buf(F32, Z * L - 1, 1, 128),
            *single(len(operands), pushes, most * C, 2 * most, (Z + Q) * C + Q, 8), *sems(6, many, many * (Z - 1), many * (X - 1), many * (Y - 1), many * (Y - 1), many * (X - 1), many * (Q - 1), many * (Q - 1), many * (Z - 1), Z * L - 1),
        ],
        compiler_params=pltpu.CompilerParams(
            collective_id=0, has_side_effects=True, vmem_limit_bytes=56 * 1024 * 1024
        ),
        name="whole_step",
    )(*[pltpu.with_memory_space_constraint(a, pltpu.HBM) for a in operands])


def write_kernel(*refs):
    count = len(refs) // 2
    sems = refs[-1]
    moves = [pltpu.make_async_copy(refs[i], refs[count + i], sems.at[i]) for i in range(count)]
    for move in moves:
        move.start()
    for move in moves:
        move.wait()


def write_results(*results):
    return pl.pallas_call(
        write_kernel,
        out_shape=tuple(jax.ShapeDtypeStruct(r.shape, r.dtype) for r in results),
        in_specs=[pl.BlockSpec(memory_space=pltpu.VMEM)] * len(results),
        out_specs=(pl.BlockSpec(memory_space=pl.ANY),) * len(results),
        scratch_shapes=[pltpu.SemaphoreType.DMA((len(results),))],
        compiler_params=pltpu.CompilerParams(vmem_limit_bytes=8 * 1024 * 1024),
        name="write_results",
    )(*results)


def lon_parts(lat_count, lon_count):
    chips = lon_count // 2
    x = next(d for d in range(math.isqrt(chips), 0, -1) if chips % d == 0)
    return lat_count, chips // x, x, 2


def local(
    mesh_latent,
    grid_cotangent,
    w_source,
    w_target,
    w_node,
    w_coarse,
    w_decode,
    neighbour_codes,
    coarse_ids,
    edge_source,
    edge_target,
    edge_owner,
):
    height, breadth, width = mesh_latent.shape
    nodes = height * breadth
    sizes = lon_parts(lax.axis_size("lat"), lax.axis_size("lon"))
    blocks = edge_owner.shape[0]
    mesh_out, grid_out, clipped = run_step(
        sizes,
        mesh_latent.reshape(nodes, width),
        grid_cotangent,
        (w_source, w_target, w_node, w_coarse, w_decode),
        neighbour_codes,
        coarse_ids.reshape(height, breadth),
        edge_source.reshape(blocks, -1),
        edge_target.reshape(blocks, -1),
        edge_owner.reshape(1, blocks),
    )
    mesh_out, grid_out, clipped = write_results(mesh_out, grid_out, clipped)
    return (mesh_out.reshape(height, breadth, width), grid_out, clipped)


def solution(mesh):
    in_specs = (
        P("lat", "lon", None),
        P(("lat", "lon"), None),
        P(),
        P(),
        P(),
        P(),
        P(),
        P(None, "lat", "lon"),
        P("lat", "lon", None),
        P(("lat", "lon")),
        P(("lat", "lon")),
        P(("lat", "lon"), None),
    )
    out_specs = (P("lat", "lon", None), P(("lat", "lon"), None), P(None, ("lat", "lon")))
    return jax.shard_map(local, mesh=mesh, in_specs=in_specs, out_specs=out_specs, check_vma=False)
```

```python
import functools
import math

import jax
import jax.numpy as jnp
from jax import lax
from jax.experimental import pallas as pl
from jax.experimental.pallas import tpu as pltpu
from jax.sharding import PartitionSpec as P

CAP = 3
F32 = jnp.float32
BF16 = jnp.bfloat16


def silu_slope(value):
    sig = jax.nn.sigmoid(value)
    return sig * (1.0 + value * (1.0 - sig))


def mm(left, right):
    return jnp.dot(left, right, preferred_element_type=F32)


def mm_t(left, right):
    return lax.dot_general(left, right, (((0,), (0,)), ((), ())), preferred_element_type=F32)


def mm_nt(left, right):
    return lax.dot_general(left, right, (((1,), (1,)), ((), ())), preferred_element_type=F32)


def split_float(value):
    high = value.astype(BF16)
    return high, (value - high.astype(F32)).astype(BF16)


MESH = pl.DeviceIdType.MESH


class Place:
    def __init__(self, sizes):
        self.Z, self.Y, self.X, self.C = sizes
        self.L = self.Y * self.X * self.C
        self.lat, self.lon = lax.axis_index("lat"), lax.axis_index("lon")
        self.z, self.c = self.lat, lax.rem(self.lon, self.C)
        self.x = lax.rem(self.lon // self.C, self.X)
        self.y = self.lon // (self.C * self.X)
        self.Q, self.q = self.Y * self.X, self.lon // self.C
        self.rows = (lax.rem(self.z + self.Z - 1, self.Z), lax.rem(self.z + 1, self.Z))
        self.sides = (lax.rem(self.lon + self.L - 1, self.L), lax.rem(self.lon + 1, self.L))

    def at(self, y=None, x=None, c=None):
        y, x, c = (old if new is None else new for new, old in ((y, self.y), (x, self.x), (c, self.c)))
        return (self.lat, (y * self.X + x) * self.C + c)

    def greeted(self):
        line = [(lax.rem(self.z + step, self.Z), self.q * self.C + core) for step in range(1, self.Z) for core in range(self.C)]
        return line + [(self.z, lax.rem(self.lon + step, self.L)) for step in range(1, self.L)]

    def meet(self):
        barrier = pltpu.get_barrier_semaphore()

        def greet(peer):
            pl.semaphore_signal(barrier, inc=1, device_id=peer, device_id_type=MESH)

        for peer in self.greeted():
            greet(peer)
        for lat, there in zip(self.rows, (self.z > 0, self.z < self.Z - 1)):
            for lon in self.sides:
                pl.when(there)(functools.partial(greet, (lat, lon)))

    def met(self):
        corners = 2 * (jnp.where(self.z > 0, 1, 0) + jnp.where(self.z < self.Z - 1, 1, 0))
        pl.semaphore_wait(pltpu.get_barrier_semaphore(), len(self.greeted()) + corners)


def send(src, dst, sems, slot, peer):
    copy = pltpu.make_async_remote_copy(
        src_ref=src, dst_ref=dst, send_sem=sems.at[0, slot], recv_sem=sems.at[1, slot],
        device_id=peer, device_id_type=MESH,
    )
    copy.start()
    return copy


def iota(shape, dim):
    return lax.broadcasted_iota(jnp.int32, shape, dim)


def step_kernel(sizes, *refs):
    (lat_hbm, cot_hbm, ws_hbm, wt_hbm, wn_hbm, wc_hbm, wd_hbm, code_hbm, coarse_hbm, src_hbm, tgt_hbm,
     owner_hbm) = refs[:12]
    mesh_ref, grid_ref, out_ref = refs[12:15]
    (lat_ref, cot_ref, ws_ref, wt_ref, wn_ref, wc_ref, wd_ref, code_ref, coarse_ref, src_ref, tgt_ref, owner_ref,
     pool, parts, got, ids, plane_ids, halo, cols, pack, tally_high, tally_low, back, backs, msgs, id_ref, grad, grad_out,
     core_in, pair, pair_out, line_wide, plane_wide, x_wide, y_wide, x_sum, y_sum, x_out, y_out, x_slim, y_slim, line_sum, line_out, plane_sum, plane_out, plane_slim, line_slim,
     share, square_out, square_line, squares) = refs[15:66]
    (load_sem, out_sem, pool_sem, got_sem, id_sem, halo_sem, esem, core_sem, line_wide_sem, x_sem, y_sem, x_slim_sem, y_slim_sem, plane_wide_sem, plane_slim_sem,
     line_slim_sem, square_sem) = refs[66:]
    p = Place(sizes)
    Z, Y, X, C, z, y, x, c = p.Z, p.Y, p.X, p.C, p.z, p.y, p.x, p.c
    Q, q = p.Q, p.q
    nodes, width = lat_ref.shape
    grid_rows = cot_ref.shape[0]
    blocks, block_len = src_ref.shape
    groups, _, group_rows = tally_high.shape
    many = out_ref.shape[0]
    R = line_sum.shape[3]
    w2 = width // 2
    halves = (pl.ds(0, w2), pl.ds(w2, w2))
    copies, pushed = [], []
    mate = (z, q * C + 1 - c)
    most = max(Z, Q)
    role_size, role_at = jnp.where(c == 0, Z, Q), jnp.where(c == 0, z, q)
    other_size, other_at = jnp.where(c == 0, Q, Z), jnp.where(c == 0, q, z)

    def go(src, dst, sems, slot, peer):
        copy = send(src, dst, sems, slot, peer)
        copies.append(copy)
        return copy

    used = [0]

    def describe(src, dst, recv, peer, send_sem=None):
        return pltpu.make_async_remote_copy(
            src_ref=src, dst_ref=dst, send_sem=recv if send_sem is None else send_sem, recv_sem=recv, device_id=peer,
            device_id_type=MESH)

    def push(src, dst, recv, peer, only=None):
        copy = describe(src, dst, recv, peer, out_sem.at[used[0]])
        used[0] += 1
        if only is None:
            copy.start()
        else:
            pl.when(only)(copy.start)
        pushed.append((only, copy))

    def arrive(dst, recv, only=None):
        if only is None:
            describe(dst, dst, recv, mate).wait_recv()
        else:
            pl.when(only)(lambda: describe(dst, dst, recv, mate).wait_recv())

    def role_step(step):
        return jnp.where(c == 0, lax.rem(z + most * Z + step, Z), lax.rem(q + most * Q + step, Q))

    def limit(step, size):
        return step < size if step >= min(Z, Q) else None

    if Z != Q:
        pool[...] = jnp.zeros_like(pool)
    p.meet()

    def empty(at):
        for k in at:
            halo[k] = jnp.zeros(halo.shape[1:], BF16)

    pl.when(z == 0)(lambda: empty((0, 4, 5)))
    pl.when(z == Z - 1)(lambda: empty((1, 6, 7)))
    needed = (src_hbm, tgt_hbm, owner_hbm, coarse_hbm, lat_hbm, code_hbm, cot_hbm, wt_hbm, ws_hbm, wn_hbm, wc_hbm, wd_hbm)
    places = (src_ref, tgt_ref, owner_ref, coarse_ref, lat_ref, code_ref, cot_ref, wt_ref, ws_ref, wn_ref, wc_ref, wd_ref)
    loads = [pltpu.make_async_copy(a, b, load_sem.at[i]) for i, (a, b) in enumerate(zip(needed, places))]
    for at in (4, 3, 0, 1, 2, 5, 6, 7, 8, 9, 10, 11):
        loads[at].start()
    slots, height, breadth = code_ref.shape
    edge = halo.shape[1]

    def column(square):
        tall = jnp.concatenate([jnp.broadcast_to(square[i:i + 1], (breadth, breadth)) for i in range(height)], 0)
        keep = iota(tall.shape, 0) % breadth == iota(tall.shape, 1)
        return jnp.sum(jnp.where(keep, tall, 0), 1, keepdims=True)

    loads[4].wait()
    latent = lat_ref[...]
    pick = iota((edge, nodes), 0)
    pick = jnp.where(pick < height, pick * breadth, (pick - height) * breadth + breadth - 1)
    cols[...] = mm(jnp.where(pick == iota(pick.shape, 1), 1.0, 0.0).astype(BF16), latent).astype(BF16)
    pool[role_at * C + c] = lat_ref[:, pl.ds(pl.multiple_of(c * w2, 128), w2)]

    loads[3].wait()
    id_column = column(coarse_ref[...]) + 1
    spread = (nodes, id_ref.shape[1])
    keep = iota(spread, 1) == iota(spread, 0) + c * nodes
    id_row = jnp.sum(jnp.where(keep, jnp.broadcast_to(id_column, spread), 0), 0, keepdims=True)
    id_ref[...] = id_row
    ids[q, z, c] = id_row
    plane_ids[q, c] = id_row
    left, right = p.sides
    p.met()

    for step in range(1, most):
        if step < Z:
            push(lat_ref.at[:, halves[0]], pool.at[z * C + c], pool_sem.at[step * C + c], (lax.rem(z + step, Z), q * C))
        if step < Q:
            push(lat_ref.at[:, halves[1]], pool.at[q * C + c], pool_sem.at[step * C + c], (z, lax.rem(q + step, Q) * C + 1))
    give = pl.ds(pl.multiple_of((1 - c) * w2, 128), w2)
    push(lat_ref.at[:, give], pool.at[other_at * C + c], pool_sem.at[c], mate)
    for core in range(C):
        for step in range(1, Z):
            push(id_ref, ids.at[q, z, c], id_sem.at[step * C + c], (lax.rem(z + step, Z), q * C + core))
        for step in range(1, Q):
            push(id_ref, plane_ids.at[q, c], id_sem.at[(Z + step) * C + c], (z, lax.rem(q + step, Q) * C + core))
    push(id_ref, ids.at[q, z, c], id_sem.at[c], mate)
    push(id_ref, plane_ids.at[q, c], id_sem.at[Z * C + c], mate)
    above, below = p.rows
    first_rows, last_rows = lat_ref.at[pl.ds(0, edge)], lat_ref.at[pl.ds(nodes - edge, edge)]
    has_above, has_below = z > 0, z < Z - 1
    borders = [
        (last_rows, (below, p.lon), has_below, has_above), (first_rows, (above, p.lon), has_above, has_below),
        (cols, (z, right), None, None), (cols, (z, left), None, None),
        (last_rows, (below, right), has_below, has_above), (last_rows, (below, left), has_below, has_above),
        (first_rows, (above, right), has_above, has_below), (first_rows, (above, left), has_above, has_below),
    ]
    for k, (src, peer, gives, takes) in enumerate(borders):
        push(src, halo.at[k], halo_sem.at[k], peer, gives)

    def met_line():
        for step in range(1, Z):
            for core in range(C):
                arrive(ids.at[q, lax.rem(z + Z - step, Z), core], id_sem.at[step * C + core])
        arrive(ids.at[q, z, 1 - c], id_sem.at[1 - c])

    def met_plane():
        for step in range(1, Q):
            for core in range(C):
                arrive(plane_ids.at[lax.rem(q + Q - step, Q), core], id_sem.at[(Z + step) * C + core])
        arrive(plane_ids.at[q, 1 - c], id_sem.at[Z * C + 1 - c])

    def met_halo():
        for k, border in enumerate(borders):
            arrive(halo.at[k], halo_sem.at[k], border[3])

    def met_pool():
        for step in range(1, most):
            at = role_step(-step)
            for core in range(C):
                arrive(pool.at[at * C + core], pool_sem.at[step * C + core], limit(step, role_size))
        arrive(pool.at[role_at * C + 1 - c], pool_sem.at[1 - c])

    def met_ids():
        for step in range(1, Q):
            arrive(ids.at[lax.rem(q + Q - step, Q)], id_sem.at[(Z + Q) * C + step])

    def met_got():
        for step in range(1, Q):
            arrive(got.at[0, lax.rem(q + Q - step, Q)], got_sem.at[step])
        for step in range(1, Z):
            arrive(got.at[1, lax.rem(z + Z - step, Z)], got_sem.at[most + step])
        arrive(got.at[1 - c, role_at], got_sem.at[0])

    for load in loads[:3]:
        load.wait()
    sub, lane = iota((blocks, blocks), 0), iota((blocks, blocks), 1)
    owner = jnp.broadcast_to(owner_ref[...], (blocks, blocks))
    owner = jnp.sum(jnp.where(sub == lane, owner, 0), 1, keepdims=True)
    is_left = (owner == left).astype(jnp.int32)
    is_right = (owner == right).astype(jnp.int32)

    def ranks(column):
        row = jnp.sum(jnp.where(sub == lane, jnp.broadcast_to(column, sub.shape), 0), 0, keepdims=True)
        return jnp.sum(jnp.where(lane < sub, jnp.broadcast_to(row, sub.shape), 0), 1, keepdims=True)

    place = jnp.where(is_left == 1, ranks(is_left), jnp.where(is_right == 1, CAP + ranks(is_right), -1))
    wide_place = jnp.broadcast_to(place, (blocks, block_len))
    for r in range(2 * CAP):
        mine = wide_place == r
        side, row = divmod(r, CAP)
        pack[side, 0, row:row + 1] = jnp.sum(jnp.where(mine, src_ref[...], 0), 0, keepdims=True)
        pack[side, 1, row:row + 1] = jnp.sum(jnp.where(mine, tgt_ref[...] + 1, 0), 0, keepdims=True) - 1
    edges = [go(pack.at[0], pack.at[3], esem, 0, (z, left)), go(pack.at[1], pack.at[2], esem, 1, (z, right))]
    def tally(source, target):
        tall = jnp.where(target < 0, -1, target % group_rows)
        both = jnp.where(target < 0, 0, target // group_rows) * nodes + source
        count = source.shape[0]
        tall = jnp.concatenate([tall[r:r + 1] for r in range(count)], 1)
        both = jnp.concatenate([both[r:r + 1] for r in range(count)], 1)
        tall = jnp.broadcast_to(tall, (group_rows, tall.shape[1]))
        both = jnp.broadcast_to(both, (groups * nodes, both.shape[1]))
        hot_t = jnp.where(tall == iota(tall.shape, 0), 1.0, 0.0).astype(BF16)
        hot_b = jnp.where(both == iota(both.shape, 0), 1.0, 0.0).astype(BF16)
        return mm_nt(hot_b, hot_t)

    def keep_tally(kind, counts):
        over = jnp.floor(counts * (1.0 / 256.0)) * 256.0
        high, low = over.astype(BF16), (counts - over).astype(BF16)
        for g in range(groups):
            tally_high[g, kind * nodes:(kind + 1) * nodes] = high[g * nodes:(g + 1) * nodes]
            tally_low[g, kind * nodes:(kind + 1) * nodes] = low[g * nodes:(g + 1) * nodes]

    stays = jnp.broadcast_to((owner == p.lon).astype(jnp.int32), (blocks, block_len))
    keep_tally(0, tally(src_ref[...], jnp.where(stays == 1, tgt_ref[...], -1)))

    loads[5].wait()
    at_row, at_col = iota((height, breadth), 0), iota((height, breadth), 1)
    wheres = []
    first_line, last_line = jnp.where(z == 0, 1, 0), jnp.where(z == Z - 1, 1, 0)
    for k in range(slots):
        code = code_ref[k]
        down = jnp.where(code >= 6, 1, jnp.where(code >= 3, 0, -1))
        rows, columns = at_row + down, at_col + code - 3 * down - 4
        up, low = rows < 0, rows >= height
        before, after = columns < 0, columns >= breadth
        middle = jnp.where(before, nodes + 2 * edge + height + rows, jnp.where(after, nodes + 3 * edge + rows, rows * breadth + columns))
        top = jnp.where(before, nodes + 4 * edge + edge - 1, jnp.where(after, nodes + 5 * edge + edge - breadth, nodes + edge - breadth + columns))
        bottom = jnp.where(before, nodes + 6 * edge + breadth - 1, jnp.where(after, nodes + 7 * edge, nodes + edge + columns))
        spot = jnp.where(up, top - first_line * (1 << 20), jnp.where(low, bottom - last_line * (1 << 20), middle))
        wheres.append(column(spot))
    where = jnp.concatenate(wheres, 0)
    hot = jnp.broadcast_to(where, (where.shape[0], nodes + 8 * edge))
    hot = jnp.where(hot == iota(hot.shape, 1), 1.0, 0.0).astype(BF16)

    for copy in edges:
        copy.wait_recv()
    for side in range(2):
        keep_tally(side + 1, tally(pack[2 + side, 0], pack[2 + side, 1]))
    loads[6].wait()
    cot_sums = jnp.zeros((3 * nodes, width), F32)
    for g in range(groups):
        part = cot_ref[g * group_rows:(g + 1) * group_rows]
        cot_sums = cot_sums + mm(tally_high[g], part) + mm(tally_low[g], part)
    backs[0] = cot_sums[nodes:2 * nodes].astype(BF16)
    backs[1] = cot_sums[2 * nodes:3 * nodes].astype(BF16)
    returns = [go(backs.at[0], back.at[0], esem, 2, (z, left)), go(backs.at[1], back.at[1], esem, 3, (z, right))]

    met_line()
    for step in range(1, Q):
        push(ids.at[q], ids.at[q], id_sem.at[(Z + Q) * C + step], (z, lax.rem(q + step, Q) * C + c))
    met_plane()

    def id_rows(rows):
        rows = [jnp.sum(rows[at].reshape(C, C * nodes), 0, keepdims=True) for at in range(rows.shape[0])]
        return rows + [jnp.zeros_like(rows[0])] * (most - len(rows))

    line_rows, plane_rows = id_rows(ids[q]), id_rows(plane_ids[...])
    source_row = jnp.concatenate([jnp.where(c == 0, a, b) for a, b in zip(line_rows, plane_rows)], 1)
    eye = iota((C * nodes, C * nodes), 0) == iota((C * nodes, C * nodes), 1)
    tall = [jnp.where(c == 0, b, a) for a, b in zip(line_rows, plane_rows)]
    tall = [jnp.sum(jnp.where(eye, jnp.broadcast_to(row, eye.shape), 0), 1, keepdims=True) for row in tall]
    tall = jnp.concatenate(tall, 0)
    same = jnp.broadcast_to(tall, (tall.shape[0], source_row.shape[1])) == jnp.broadcast_to(source_row, (tall.shape[0], source_row.shape[1]))
    same = jnp.where(same, 1.0, 0.0).astype(BF16)

    loads[7].wait()
    toward = mm(latent, wt_ref[...])
    met_halo()
    near = jnp.concatenate([latent, halo[...].reshape(8 * edge, width)], 0)
    beside = mm(hot, near).astype(BF16)
    loads[8].wait()
    edges_pre = mm(beside, ws_ref[...]).reshape(slots, nodes, width) + toward[None]
    agg = jnp.sum(edges_pre * jax.nn.sigmoid(edges_pre), 0).astype(BF16)

    met_pool()
    sums = mm(same, pool[...].reshape(most * C * nodes, w2)).astype(BF16)
    parts[...] = sums.reshape(most * C, nodes, w2)
    got[c, other_at] = parts[other_at * C + c]
    for step in range(1, most):
        at = jnp.where(c == 0, lax.rem(q + step, Q), lax.rem(z + step, Z))
        for core in range(C):
            peer = (jnp.where(c == 0, z, at), jnp.where(c == 0, at, q) * C + core)
            push(parts.at[at * C + core], got.at[c, other_at], got_sem.at[c * most + step], peer, limit(step, other_size))
    push(parts.at[other_at * C + 1 - c], got.at[c, other_at], got_sem.at[0], mate)
    loads[9].wait()
    agg_out = mm(agg, wn_ref[...])
    slope_edges = silu_slope(edges_pre)
    met_ids()
    row = jnp.concatenate([r for at in range(Q) for r in [jnp.sum(ids[at, line].reshape(C, C * nodes), 0, keepdims=True) for line in range(Z)]], 1)
    alike = jnp.broadcast_to(row, (nodes, row.shape[1])) == jnp.broadcast_to(id_column, (nodes, row.shape[1]))
    count_of = jnp.sum(jnp.where(alike, 1.0, 0.0), 1, keepdims=True)
    scale = lax.rsqrt(count_of)
    met_got()
    pooled = [jnp.sum(got[0, 0:Q].astype(F32), 0), jnp.sum(got[1, 0:Z].astype(F32), 0)]
    coarse_in = (jnp.concatenate(pooled, 1) * scale).astype(BF16)
    loads[10].wait()
    cpre = mm(coarse_in, wc_ref[...])
    coarse_out = (cpre * jax.nn.sigmoid(cpre)).astype(BF16)

    npre = agg_out + coarse_out.astype(F32)
    mesh_out = (latent.astype(F32) + npre * jax.nn.sigmoid(npre)).astype(BF16)
    mesh_ref[...] = mesh_out

    loads[11].wait()
    pre = mm(mesh_out, wd_ref[...])
    msgs[0:nodes] = (pre * jax.nn.sigmoid(pre)).astype(BF16)
    mine = msgs.at[pl.ds(0, nodes)]

    kinds = ("half", "half", "half", "half", "line")
    line_first = [m for m in range(many) if kinds[m] == "line"]
    cut = Z // 2
    near_z, far_z = pl.ds(0, cut), pl.ds(cut, Z - cut)

    def hop_core(m, value):
        if R % 8 == 0:
            whole = value.reshape(Z, Y, X, C, R, width)
            grad[m] = whole
            grad_out[m] = whole.astype(BF16)
        else:
            for at in range(Z * Q * C):
                spot = (at // (Q * C), at // (C * X) % Y, at // C % X, at % C)
                grad[(m, *spot)] = value[at * R:(at + 1) * R]
                grad_out[(m, *spot)] = value[at * R:(at + 1) * R].astype(BF16)
        one[m] = go(grad_out.at[m, :, :, :, 1 - c], core_in.at[m], core_sem, m, mate)

    def hop_first(m):
        one[m].wait_recv()
        total = grad[m, :, :, :, c] + core_in[m].astype(F32)
        pair[m] = total
        pair_out[m] = total.astype(BF16)
        two[m] = []
        if kinds[m] == "line":
            for off in range(1, Z):
                there, k = lax.rem(z + off, Z), line_first.index(m) * (Z - 1) + off - 1
                two[m].append((k, go(pair_out.at[m, there], line_wide.at[k], line_wide_sem, k, (there, p.lon))))
        elif kinds[m] == "plane":
            for off in range(1, Q):
                there, k = lax.rem(q + off, Q), m * (Q - 1) + off - 1
                src = pair_out.at[m, :, there // X, lax.rem(there, X)]
                two[m].append((k, go(src, plane_wide.at[k], plane_wide_sem, k, (z, there * C + c))))
        else:
            for off in range(1, X):
                there, k = lax.rem(x + off, X), m * (X - 1) + off - 1
                two[m].append((0, k, go(pair_out.at[m, near_z, :, there], x_wide.at[k], x_sem, k, p.at(x=there))))
            for off in range(1, Y):
                there, k = lax.rem(y + off, Y), m * (Y - 1) + off - 1
                two[m].append((1, k, go(pair_out.at[m, far_z, there], y_wide.at[k], y_sem, k, p.at(y=there))))

    def hop_middle(m):
        totals = [pair[m, near_z, :, x], pair[m, far_z, y]]
        middle[m] = []
        for side, k, copy in two[m]:
            copy.wait_recv()
            totals[side] = totals[side] + (y_wide if side else x_wide)[k].astype(F32)
        x_sum[m], y_sum[m] = totals
        x_out[m], y_out[m] = totals[0].astype(BF16), totals[1].astype(BF16)
        for off in range(1, Y):
            there, k = lax.rem(y + off, Y), m * (Y - 1) + off - 1
            middle[m].append((0, k, go(x_out.at[m, :, there], x_slim.at[k], x_slim_sem, k, p.at(y=there))))
        for off in range(1, X):
            there, k = lax.rem(x + off, X), m * (X - 1) + off - 1
            middle[m].append((1, k, go(y_out.at[m, :, there], y_slim.at[k], y_slim_sem, k, p.at(x=there))))

    def hop_second(m):
        three[m] = []
        if kinds[m] == "line":
            total, at = pair[m, z], line_first.index(m)
            for k, copy in two[m]:
                copy.wait_recv()
                total = total + line_wide[k].astype(F32)
            line_sum[at] = total
            line_out[at] = total.astype(BF16)
            for off in range(1, Q):
                there, k = lax.rem(q + off, Q), at * (Q - 1) + off - 1
                src = line_out.at[at, there // X, lax.rem(there, X)]
                three[m].append((k, go(src, plane_slim.at[k], plane_slim_sem, k, (z, there * C + c))))
            return
        if kinds[m] == "plane":
            total = pair[m, :, y, x]
            for k, copy in two[m]:
                copy.wait_recv()
                total = total + plane_wide[k].astype(F32)
            plane_sum[m] = total
            plane_out[m] = total.astype(BF16)
        else:
            totals = [x_sum[m, :, y], y_sum[m, :, x]]
            for side, k, copy in middle[m]:
                copy.wait_recv()
                totals[side] = totals[side] + (y_slim if side else x_slim)[k].astype(F32)
            plane_sum[m, near_z], plane_sum[m, far_z] = totals
            plane_out[m, near_z], plane_out[m, far_z] = totals[0].astype(BF16), totals[1].astype(BF16)
        for off in range(1, Z):
            there, k = lax.rem(z + off, Z), m * (Z - 1) + off - 1
            three[m].append((k, go(plane_out.at[m, there], line_slim.at[k], line_slim_sem, k, (there, p.lon))))

    def last(m):
        total = line_sum[line_first.index(m), y, x] if m in line_first else plane_sum[m, z]
        for k, copy in three[m]:
            copy.wait_recv()
            total = total + (plane_slim[k] if m in line_first else line_slim[k]).astype(F32)
        for r in range(R):
            share[m:m + 1, r * width:(r + 1) * width] = total[r:r + 1]
        return total * total

    one, two, middle, three = {}, {}, {}, {}
    for copy in returns:
        copy.wait_recv()
    cot_sum = cot_sums[:nodes] + back[0].astype(F32) + back[1].astype(F32)
    d_high, d_low = split_float(cot_sum * silu_slope(pre))
    hop_core(4, mm_t(mesh_out, d_high) + mm_t(mesh_out, d_low))
    d_node = (mm_nt(d_high, wd_ref[...]) * silu_slope(npre)).astype(BF16)
    hop_core(2, mm_t(agg, d_node))
    hop_first(4)
    c_high, c_low = split_float(d_node.astype(F32) * silu_slope(cpre))
    hop_core(3, mm_t(coarse_in, c_high) + mm_t(coarse_in, c_low))
    hop_first(2)
    d_edges = (mm_nt(d_node, wn_ref[...])[None] * slope_edges).astype(BF16)
    d_sum = jnp.sum(d_edges.astype(F32), 0).astype(BF16)
    hop_core(1, mm_t(latent, d_sum))
    hop_first(3)
    hop_core(0, mm_t(beside, d_edges.reshape(slots * nodes, width)))
    hop_first(1)
    hop_first(0)
    hop_middle(2)
    hop_middle(3)
    hop_middle(1)
    hop_second(4)
    hop_middle(0)
    spoken = [
        go(mine, msgs.at[pl.ds(nodes, nodes)], esem, 4, (z, right)),
        go(mine, msgs.at[pl.ds(2 * nodes, nodes)], esem, 5, (z, left)),
    ]
    hop_second(2)
    hop_second(3)
    hop_second(1)
    hop_second(0)
    for copy in spoken:
        copy.wait_recv()
    for g in range(groups):
        decoded = mm_t(tally_high[g], msgs[...]) + mm_t(tally_low[g], msgs[...])
        grid_ref[g * group_rows:(g + 1) * group_rows] = decoded.astype(BF16)
    square = jnp.zeros((R, width), F32)
    for m in (2, 3, 4, 1, 0):
        square = square + last(m)
    square = sum(square[:, k * 128:(k + 1) * 128] for k in range(width // 128))
    square = jnp.broadcast_to(jnp.sum(square, keepdims=True), square_out.shape)
    square_out[...] = square
    mine = []
    for step in range(1, Z * p.L):
        peer = (lax.rem(z + step // p.L, Z), lax.rem(p.lon + step % p.L, p.L))
        mine.append(go(square_out, squares.at[step - 1], square_sem, step - 1, peer))
    for copy in mine:
        copy.wait_recv()
    norm = jnp.sqrt(square + jnp.sum(squares[...], 0))[:, 0:1] + 1e-06
    out_ref[...] = share[...] * (1.0 / norm)
    for only, copy in pushed:
        if only is None:
            copy.wait_send()
        else:
            pl.when(only)(copy.wait_send)
    for copy in copies:
        copy.wait_send()


def run_step(sizes, latent, cot, weights, codes, ids, source, target, owner):
    Z, Y, X, C = sizes
    L = Y * X * C
    many = len(weights)
    nodes, width = latent.shape
    grid_rows = cot.shape[0]
    blocks, block_len = source.shape
    slots, height, breadth = codes.shape
    edge = 2 * max(height, breadth)
    groups = 4 if grid_rows % 4 == 0 else 1
    group_rows = grid_rows // groups
    Q, most = Y * X, max(Z, Y * X)
    R = width // (Z * L)
    w2 = width // 2
    vmem = pl.BlockSpec(memory_space=pltpu.VMEM)

    def buf(dtype, *dims):
        return pltpu.VMEM(dims, dtype)

    def sems(*counts):
        return [pltpu.SemaphoreType.DMA((2, n)) for n in counts]

    def single(*counts):
        return [pltpu.SemaphoreType.DMA((n,)) for n in counts]

    cut = Z // 2
    operands = [latent, cot, *weights, codes, ids, source, target, owner]
    pushes = Z - 1 + Q - 1 + 1 + C * (Z - 1 + Q - 1) + 2 + 8 + Q - 1 + C * (most - 1) + 1
    return pl.pallas_call(
        functools.partial(step_kernel, sizes),
        out_shape=(
            pltpu.VMEM((nodes, width), BF16),
            pltpu.VMEM((grid_rows, width), BF16),
            pltpu.VMEM((many, R * width), F32),
        ),
        in_specs=[pl.BlockSpec(memory_space=pltpu.HBM)] * len(operands),
        out_specs=(vmem,) * 3,
        scratch_shapes=[
            *[pltpu.VMEM(a.shape, a.dtype) for a in operands],
            buf(BF16, most * C, nodes, w2), buf(BF16, most * C, nodes, w2), buf(BF16, 2, most, nodes, w2),
            buf(jnp.int32, Q, Z, C, 1, C * nodes), buf(jnp.int32, Q, C, 1, C * nodes),
            buf(BF16, 8, edge, width), buf(BF16, edge, width), buf(jnp.int32, 4, 2, CAP, block_len),
            buf(BF16, groups, 3 * nodes, group_rows), buf(BF16, groups, 3 * nodes, group_rows),
            buf(BF16, 2, nodes, width), buf(BF16, 2, nodes, width), buf(BF16, 3 * nodes, width),
            buf(jnp.int32, 1, C * nodes),
            buf(F32, many, Z, Y, X, C, R, width), buf(BF16, many, Z, Y, X, C, R, width), buf(BF16, many, Z, Y, X, R, width),
            buf(F32, many, Z, Y, X, R, width), buf(BF16, many, Z, Y, X, R, width),
            buf(BF16, many * (Z - 1), Y, X, R, width), buf(BF16, many * (Q - 1), Z, R, width),
            buf(BF16, many * (X - 1), cut, Y, R, width), buf(BF16, many * (Y - 1), Z - cut, X, R, width),
            buf(F32, many, cut, Y, R, width), buf(F32, many, Z - cut, X, R, width),
            buf(BF16, many, cut, Y, R, width), buf(BF16, many, Z - cut, X, R, width),
            buf(BF16, many * (Y - 1), cut, R, width), buf(BF16, many * (X - 1), Z - cut, R, width),
            buf(F32, many, Y, X, R, width), buf(BF16, many, Y, X, R, width), buf(F32, many, Z, R, width),
            buf(BF16, many, Z, R, width),
            buf(BF16, many * (Q - 1), R, width), buf(BF16, many * (Z - 1), R, width),
            buf(F32, many, R * width), buf(F32, 1, 128), buf(F32, 1, 128), buf(F32, Z * L - 1, 1, 128),
            *single(len(operands), pushes, most * C, 2 * most, (Z + Q) * C + Q, 8), *sems(6, many, many * (Z - 1), many * (X - 1), many * (Y - 1), many * (Y - 1), many * (X - 1), many * (Q - 1), many * (Q - 1), many * (Z - 1), Z * L - 1),
        ],
        compiler_params=pltpu.CompilerParams(
            collective_id=0, has_side_effects=True, vmem_limit_bytes=56 * 1024 * 1024
        ),
        name="whole_step",
    )(*[pltpu.with_memory_space_constraint(a, pltpu.HBM) for a in operands])


def write_kernel(*refs):
    count = len(refs) // 2
    sems = refs[-1]
    moves = [pltpu.make_async_copy(refs[i], refs[count + i], sems.at[i]) for i in range(count)]
    for move in moves:
        move.start()
    for move in moves:
        move.wait()


def write_results(*results):
    return pl.pallas_call(
        write_kernel,
        out_shape=tuple(jax.ShapeDtypeStruct(r.shape, r.dtype) for r in results),
        in_specs=[pl.BlockSpec(memory_space=pltpu.VMEM)] * len(results),
        out_specs=(pl.BlockSpec(memory_space=pl.ANY),) * len(results),
        scratch_shapes=[pltpu.SemaphoreType.DMA((len(results),))],
        compiler_params=pltpu.CompilerParams(vmem_limit_bytes=8 * 1024 * 1024),
        name="write_results",
    )(*results)


def lon_parts(lat_count, lon_count):
    chips = lon_count // 2
    x = next(d for d in range(math.isqrt(chips), 0, -1) if chips % d == 0)
    return lat_count, chips // x, x, 2


def local(
    mesh_latent,
    grid_cotangent,
    w_source,
    w_target,
    w_node,
    w_coarse,
    w_decode,
    neighbour_codes,
    coarse_ids,
    edge_source,
    edge_target,
    edge_owner,
):
    height, breadth, width = mesh_latent.shape
    nodes = height * breadth
    sizes = lon_parts(lax.axis_size("lat"), lax.axis_size("lon"))
    blocks = edge_owner.shape[0]
    mesh_out, grid_out, clipped = run_step(
        sizes,
        mesh_latent.reshape(nodes, width),
        grid_cotangent,
        (w_source, w_target, w_node, w_coarse, w_decode),
        neighbour_codes,
        coarse_ids.reshape(height, breadth),
        edge_source.reshape(blocks, -1),
        edge_target.reshape(blocks, -1),
        edge_owner.reshape(1, blocks),
    )
    mesh_out, grid_out, clipped = write_results(mesh_out, grid_out, clipped)
    return (mesh_out.reshape(height, breadth, width), grid_out, clipped)


def solution(mesh):
    in_specs = (
        P("lat", "lon", None),
        P(("lat", "lon"), None),
        P(),
        P(),
        P(),
        P(),
        P(),
        P(None, "lat", "lon"),
        P("lat", "lon", None),
        P(("lat", "lon")),
        P(("lat", "lon")),
        P(("lat", "lon"), None),
    )
    out_specs = (P("lat", "lon", None), P(("lat", "lon"), None), P(None, ("lat", "lon")))
    return jax.shard_map(local, mesh=mesh, in_specs=in_specs, out_specs=out_specs, check_vma=False)
```

```python
import functools
import math

import jax
import jax.numpy as jnp
from jax import lax
from jax.experimental import pallas as pl
from jax.experimental.pallas import tpu as pltpu
from jax.sharding import PartitionSpec as P

CAP = 3
F32 = jnp.float32
BF16 = jnp.bfloat16


def silu_slope(value):
    sig = jax.nn.sigmoid(value)
    return sig * (1.0 + value * (1.0 - sig))


def mm(left, right):
    return jnp.dot(left, right, preferred_element_type=F32)


def mm_t(left, right):
    return lax.dot_general(left, right, (((0,), (0,)), ((), ())), preferred_element_type=F32)


def mm_nt(left, right):
    return lax.dot_general(left, right, (((1,), (1,)), ((), ())), preferred_element_type=F32)


def split_float(value):
    high = value.astype(BF16)
    return high, (value - high.astype(F32)).astype(BF16)


MESH = pl.DeviceIdType.MESH


class Place:
    def __init__(self, sizes):
        self.Z, self.Y, self.X, self.C = sizes
        self.L = self.Y * self.X * self.C
        self.lat, self.lon = lax.axis_index("lat"), lax.axis_index("lon")
        self.z, self.c = self.lat, lax.rem(self.lon, self.C)
        self.x = lax.rem(self.lon // self.C, self.X)
        self.y = self.lon // (self.C * self.X)
        self.Q, self.q = self.Y * self.X, self.lon // self.C
        self.rows = (lax.rem(self.z + self.Z - 1, self.Z), lax.rem(self.z + 1, self.Z))
        self.sides = (lax.rem(self.lon + self.L - 1, self.L), lax.rem(self.lon + 1, self.L))

    def at(self, y=None, x=None, c=None):
        y, x, c = (old if new is None else new for new, old in ((y, self.y), (x, self.x), (c, self.c)))
        return (self.lat, (y * self.X + x) * self.C + c)

    def greeted(self):
        line = [(lax.rem(self.z + step, self.Z), self.q * self.C + core) for step in range(1, self.Z) for core in range(self.C)]
        return line + [(self.z, lax.rem(self.lon + step, self.L)) for step in range(1, self.L)]

    def meet(self):
        barrier = pltpu.get_barrier_semaphore()

        def greet(peer):
            pl.semaphore_signal(barrier, inc=1, device_id=peer, device_id_type=MESH)

        for peer in self.greeted():
            greet(peer)
        for lat, there in zip(self.rows, (self.z > 0, self.z < self.Z - 1)):
            for lon in self.sides:
                pl.when(there)(functools.partial(greet, (lat, lon)))

    def met(self):
        corners = 2 * (jnp.where(self.z > 0, 1, 0) + jnp.where(self.z < self.Z - 1, 1, 0))
        pl.semaphore_wait(pltpu.get_barrier_semaphore(), len(self.greeted()) + corners)


def send(src, dst, sems, slot, peer):
    copy = pltpu.make_async_remote_copy(
        src_ref=src, dst_ref=dst, send_sem=sems.at[0, slot], recv_sem=sems.at[1, slot],
        device_id=peer, device_id_type=MESH,
    )
    copy.start()
    return copy


def iota(shape, dim):
    return lax.broadcasted_iota(jnp.int32, shape, dim)


def step_kernel(sizes, *refs):
    (lat_hbm, cot_hbm, ws_hbm, wt_hbm, wn_hbm, wc_hbm, wd_hbm, code_hbm, coarse_hbm, src_hbm, tgt_hbm,
     owner_hbm) = refs[:12]
    mesh_ref, grid_ref, out_ref = refs[12:15]
    (lat_ref, cot_ref, ws_ref, wt_ref, wn_ref, wc_ref, wd_ref, code_ref, coarse_ref, src_ref, tgt_ref, owner_ref,
     pool, parts, got, ids, plane_ids, halo, cols, pack, tally_high, tally_low, back, backs, msgs, id_ref, grad, grad_out,
     core_in, pair, pair_out, line_wide, plane_wide, x_wide, y_wide, x_sum, y_sum, x_out, y_out, x_slim, y_slim, line_sum, line_out, plane_sum, plane_out, plane_slim, line_slim,
     share, square_out, square_line, squares) = refs[15:66]
    (load_sem, out_sem, pool_sem, got_sem, id_sem, halo_sem, esem, core_sem, line_wide_sem, x_sem, y_sem, x_slim_sem, y_slim_sem, plane_wide_sem, plane_slim_sem,
     line_slim_sem, square_sem) = refs[66:]
    p = Place(sizes)
    Z, Y, X, C, z, y, x, c = p.Z, p.Y, p.X, p.C, p.z, p.y, p.x, p.c
    Q, q = p.Q, p.q
    nodes, width = lat_ref.shape
    grid_rows = cot_ref.shape[0]
    blocks, block_len = src_ref.shape
    groups, _, group_rows = tally_high.shape
    many = out_ref.shape[0]
    R = line_sum.shape[3]
    w2 = width // 2
    halves = (pl.ds(0, w2), pl.ds(w2, w2))
    copies, pushed = [], []
    mate = (z, q * C + 1 - c)
    most = max(Z, Q)
    role_size, role_at = jnp.where(c == 0, Z, Q), jnp.where(c == 0, z, q)
    other_size, other_at = jnp.where(c == 0, Q, Z), jnp.where(c == 0, q, z)

    def go(src, dst, sems, slot, peer):
        copy = send(src, dst, sems, slot, peer)
        copies.append(copy)
        return copy

    used = [0]

    def describe(src, dst, recv, peer, send_sem=None):
        return pltpu.make_async_remote_copy(
            src_ref=src, dst_ref=dst, send_sem=recv if send_sem is None else send_sem, recv_sem=recv, device_id=peer,
            device_id_type=MESH)

    def push(src, dst, recv, peer, only=None):
        copy = describe(src, dst, recv, peer, out_sem.at[used[0]])
        used[0] += 1
        if only is None:
            copy.start()
        else:
            pl.when(only)(copy.start)
        pushed.append((only, copy))

    def arrive(dst, recv, only=None):
        if only is None:
            describe(dst, dst, recv, mate).wait_recv()
        else:
            pl.when(only)(lambda: describe(dst, dst, recv, mate).wait_recv())

    def role_step(step):
        return jnp.where(c == 0, lax.rem(z + most * Z + step, Z), lax.rem(q + most * Q + step, Q))

    def limit(step, size):
        return step < size if step >= min(Z, Q) else None

    if Z != Q:
        pool[...] = jnp.zeros_like(pool)
    p.meet()

    def empty(at):
        for k in at:
            halo[k] = jnp.zeros(halo.shape[1:], BF16)

    pl.when(z == 0)(lambda: empty((0, 4, 5)))
    pl.when(z == Z - 1)(lambda: empty((1, 6, 7)))
    needed = (src_hbm, tgt_hbm, owner_hbm, coarse_hbm, lat_hbm, code_hbm, cot_hbm, wt_hbm, ws_hbm, wn_hbm, wc_hbm, wd_hbm)
    places = (src_ref, tgt_ref, owner_ref, coarse_ref, lat_ref, code_ref, cot_ref, wt_ref, ws_ref, wn_ref, wc_ref, wd_ref)
    loads = [pltpu.make_async_copy(a, b, load_sem.at[i]) for i, (a, b) in enumerate(zip(needed, places))]
    for at in (4, 3, 0, 1, 2, 5, 6, 7, 8, 9, 10, 11):
        loads[at].start()
    slots, height, breadth = code_ref.shape
    edge = halo.shape[1]

    def column(square):
        tall = jnp.concatenate([jnp.broadcast_to(square[i:i + 1], (breadth, breadth)) for i in range(height)], 0)
        keep = iota(tall.shape, 0) % breadth == iota(tall.shape, 1)
        return jnp.sum(jnp.where(keep, tall, 0), 1, keepdims=True)

    loads[4].wait()
    latent = lat_ref[...]
    pick = iota((edge, nodes), 0)
    pick = jnp.where(pick < height, pick * breadth, (pick - height) * breadth + breadth - 1)
    cols[...] = mm(jnp.where(pick == iota(pick.shape, 1), 1.0, 0.0).astype(BF16), latent).astype(BF16)
    pool[role_at * C + c] = lat_ref[:, pl.ds(pl.multiple_of(c * w2, 128), w2)]

    loads[3].wait()
    id_column = column(coarse_ref[...]) + 1
    spread = (nodes, id_ref.shape[1])
    keep = iota(spread, 1) == iota(spread, 0) + c * nodes
    id_row = jnp.sum(jnp.where(keep, jnp.broadcast_to(id_column, spread), 0), 0, keepdims=True)
    id_ref[...] = id_row
    ids[q, z, c] = id_row
    plane_ids[q, c] = id_row
    left, right = p.sides
    p.met()

    for step in range(1, most):
        if step < Z:
            push(lat_ref.at[:, halves[0]], pool.at[z * C + c], pool_sem.at[step * C + c], (lax.rem(z + step, Z), q * C))
        if step < Q:
            push(lat_ref.at[:, halves[1]], pool.at[q * C + c], pool_sem.at[step * C + c], (z, lax.rem(q + step, Q) * C + 1))
    give = pl.ds(pl.multiple_of((1 - c) * w2, 128), w2)
    push(lat_ref.at[:, give], pool.at[other_at * C + c], pool_sem.at[c], mate)
    for core in range(C):
        for step in range(1, Z):
            push(id_ref, ids.at[q, z, c], id_sem.at[step * C + c], (lax.rem(z + step, Z), q * C + core))
        for step in range(1, Q):
            push(id_ref, plane_ids.at[q, c], id_sem.at[(Z + step) * C + c], (z, lax.rem(q + step, Q) * C + core))
    push(id_ref, ids.at[q, z, c], id_sem.at[c], mate)
    push(id_ref, plane_ids.at[q, c], id_sem.at[Z * C + c], mate)
    above, below = p.rows
    first_rows, last_rows = lat_ref.at[pl.ds(0, edge)], lat_ref.at[pl.ds(nodes - edge, edge)]
    has_above, has_below = z > 0, z < Z - 1
    borders = [
        (last_rows, (below, p.lon), has_below, has_above), (first_rows, (above, p.lon), has_above, has_below),
        (cols, (z, right), None, None), (cols, (z, left), None, None),
        (last_rows, (below, right), has_below, has_above), (last_rows, (below, left), has_below, has_above),
        (first_rows, (above, right), has_above, has_below), (first_rows, (above, left), has_above, has_below),
    ]
    for k, (src, peer, gives, takes) in enumerate(borders):
        push(src, halo.at[k], halo_sem.at[k], peer, gives)

    def met_line():
        for step in range(1, Z):
            for core in range(C):
                arrive(ids.at[q, lax.rem(z + Z - step, Z), core], id_sem.at[step * C + core])
        arrive(ids.at[q, z, 1 - c], id_sem.at[1 - c])

    def met_plane():
        for step in range(1, Q):
            for core in range(C):
                arrive(plane_ids.at[lax.rem(q + Q - step, Q), core], id_sem.at[(Z + step) * C + core])
        arrive(plane_ids.at[q, 1 - c], id_sem.at[Z * C + 1 - c])

    def met_halo():
        for k, border in enumerate(borders):
            arrive(halo.at[k], halo_sem.at[k], border[3])

    def met_pool():
        for step in range(1, most):
            at = role_step(-step)
            for core in range(C):
                arrive(pool.at[at * C + core], pool_sem.at[step * C + core], limit(step, role_size))
        arrive(pool.at[role_at * C + 1 - c], pool_sem.at[1 - c])

    def met_ids():
        for step in range(1, Q):
            arrive(ids.at[lax.rem(q + Q - step, Q)], id_sem.at[(Z + Q) * C + step])

    def met_got():
        for step in range(1, Q):
            arrive(got.at[0, lax.rem(q + Q - step, Q)], got_sem.at[step])
        for step in range(1, Z):
            arrive(got.at[1, lax.rem(z + Z - step, Z)], got_sem.at[most + step])
        arrive(got.at[1 - c, role_at], got_sem.at[0])

    for load in loads[:3]:
        load.wait()
    sub, lane = iota((blocks, blocks), 0), iota((blocks, blocks), 1)
    owner = jnp.broadcast_to(owner_ref[...], (blocks, blocks))
    owner = jnp.sum(jnp.where(sub == lane, owner, 0), 1, keepdims=True)
    is_left = (owner == left).astype(jnp.int32)
    is_right = (owner == right).astype(jnp.int32)

    def ranks(column):
        row = jnp.sum(jnp.where(sub == lane, jnp.broadcast_to(column, sub.shape), 0), 0, keepdims=True)
        return jnp.sum(jnp.where(lane < sub, jnp.broadcast_to(row, sub.shape), 0), 1, keepdims=True)

    place = jnp.where(is_left == 1, ranks(is_left), jnp.where(is_right == 1, CAP + ranks(is_right), -1))
    wide_place = jnp.broadcast_to(place, (blocks, block_len))
    for r in range(2 * CAP):
        mine = wide_place == r
        side, row = divmod(r, CAP)
        pack[side, 0, row:row + 1] = jnp.sum(jnp.where(mine, src_ref[...], 0), 0, keepdims=True)
        pack[side, 1, row:row + 1] = jnp.sum(jnp.where(mine, tgt_ref[...] + 1, 0), 0, keepdims=True) - 1
    edges = [go(pack.at[0], pack.at[3], esem, 0, (z, left)), go(pack.at[1], pack.at[2], esem, 1, (z, right))]
    def tally(source, target):
        tall = jnp.where(target < 0, -1, target % group_rows)
        both = jnp.where(target < 0, 0, target // group_rows) * nodes + source
        count = source.shape[0]
        tall = jnp.concatenate([tall[r:r + 1] for r in range(count)], 1)
        both = jnp.concatenate([both[r:r + 1] for r in range(count)], 1)
        tall = jnp.broadcast_to(tall, (group_rows, tall.shape[1]))
        both = jnp.broadcast_to(both, (groups * nodes, both.shape[1]))
        hot_t = jnp.where(tall == iota(tall.shape, 0), 1.0, 0.0).astype(BF16)
        hot_b = jnp.where(both == iota(both.shape, 0), 1.0, 0.0).astype(BF16)
        return mm_nt(hot_b, hot_t)

    def keep_tally(kind, counts):
        over = jnp.floor(counts * (1.0 / 256.0)) * 256.0
        high, low = over.astype(BF16), (counts - over).astype(BF16)
        for g in range(groups):
            tally_high[g, kind * nodes:(kind + 1) * nodes] = high[g * nodes:(g + 1) * nodes]
            tally_low[g, kind * nodes:(kind + 1) * nodes] = low[g * nodes:(g + 1) * nodes]

    stays = jnp.broadcast_to((owner == p.lon).astype(jnp.int32), (blocks, block_len))
    keep_tally(0, tally(src_ref[...], jnp.where(stays == 1, tgt_ref[...], -1)))

    loads[5].wait()
    at_row, at_col = iota((height, breadth), 0), iota((height, breadth), 1)
    wheres = []
    first_line, last_line = jnp.where(z == 0, 1, 0), jnp.where(z == Z - 1, 1, 0)
    for k in range(slots):
        code = code_ref[k]
        down = jnp.where(code >= 6, 1, jnp.where(code >= 3, 0, -1))
        rows, columns = at_row + down, at_col + code - 3 * down - 4
        up, low = rows < 0, rows >= height
        before, after = columns < 0, columns >= breadth
        middle = jnp.where(before, nodes + 2 * edge + height + rows, jnp.where(after, nodes + 3 * edge + rows, rows * breadth + columns))
        top = jnp.where(before, nodes + 4 * edge + edge - 1, jnp.where(after, nodes + 5 * edge + edge - breadth, nodes + edge - breadth + columns))
        bottom = jnp.where(before, nodes + 6 * edge + breadth - 1, jnp.where(after, nodes + 7 * edge, nodes + edge + columns))
        spot = jnp.where(up, top - first_line * (1 << 20), jnp.where(low, bottom - last_line * (1 << 20), middle))
        wheres.append(column(spot))
    where = jnp.concatenate(wheres, 0)
    hot = jnp.broadcast_to(where, (where.shape[0], nodes + 8 * edge))
    hot = jnp.where(hot == iota(hot.shape, 1), 1.0, 0.0).astype(BF16)

    for copy in edges:
        copy.wait_recv()
    for side in range(2):
        keep_tally(side + 1, tally(pack[2 + side, 0], pack[2 + side, 1]))
    loads[6].wait()
    cot_sums = jnp.zeros((3 * nodes, width), F32)
    for g in range(groups):
        part = cot_ref[g * group_rows:(g + 1) * group_rows]
        cot_sums = cot_sums + mm(tally_high[g], part) + mm(tally_low[g], part)
    backs[0] = cot_sums[nodes:2 * nodes].astype(BF16)
    backs[1] = cot_sums[2 * nodes:3 * nodes].astype(BF16)
    returns = [go(backs.at[0], back.at[0], esem, 2, (z, left)), go(backs.at[1], back.at[1], esem, 3, (z, right))]

    met_line()
    for step in range(1, Q):
        push(ids.at[q], ids.at[q], id_sem.at[(Z + Q) * C + step], (z, lax.rem(q + step, Q) * C + c))
    met_plane()

    def id_rows(rows):
        rows = [jnp.sum(rows[at].reshape(C, C * nodes), 0, keepdims=True) for at in range(rows.shape[0])]
        return rows + [jnp.zeros_like(rows[0])] * (most - len(rows))

    line_rows, plane_rows = id_rows(ids[q]), id_rows(plane_ids[...])
    source_row = jnp.concatenate([jnp.where(c == 0, a, b) for a, b in zip(line_rows, plane_rows)], 1)
    eye = iota((C * nodes, C * nodes), 0) == iota((C * nodes, C * nodes), 1)
    tall = [jnp.where(c == 0, b, a) for a, b in zip(line_rows, plane_rows)]
    tall = [jnp.sum(jnp.where(eye, jnp.broadcast_to(row, eye.shape), 0), 1, keepdims=True) for row in tall]
    tall = jnp.concatenate(tall, 0)
    same = jnp.broadcast_to(tall, (tall.shape[0], source_row.shape[1])) == jnp.broadcast_to(source_row, (tall.shape[0], source_row.shape[1]))
    same = jnp.where(same, 1.0, 0.0).astype(BF16)

    loads[7].wait()
    toward = mm(latent, wt_ref[...])
    met_halo()
    near = jnp.concatenate([latent, halo[...].reshape(8 * edge, width)], 0)
    beside = mm(hot, near).astype(BF16)
    loads[8].wait()
    edges_pre = mm(beside, ws_ref[...]).reshape(slots, nodes, width) + toward[None]
    agg = jnp.sum(edges_pre * jax.nn.sigmoid(edges_pre), 0).astype(BF16)

    met_pool()
    sums = mm(same, pool[...].reshape(most * C * nodes, w2)).astype(BF16)
    parts[...] = sums.reshape(most * C, nodes, w2)
    got[c, other_at] = parts[other_at * C + c]
    for step in range(1, most):
        at = jnp.where(c == 0, lax.rem(q + step, Q), lax.rem(z + step, Z))
        for core in range(C):
            peer = (jnp.where(c == 0, z, at), jnp.where(c == 0, at, q) * C + core)
            push(parts.at[at * C + core], got.at[c, other_at], got_sem.at[c * most + step], peer, limit(step, other_size))
    push(parts.at[other_at * C + 1 - c], got.at[c, other_at], got_sem.at[0], mate)
    loads[9].wait()
    agg_out = mm(agg, wn_ref[...])
    slope_edges = silu_slope(edges_pre)
    met_ids()
    row = jnp.concatenate([r for at in range(Q) for r in [jnp.sum(ids[at, line].reshape(C, C * nodes), 0, keepdims=True) for line in range(Z)]], 1)
    alike = jnp.broadcast_to(row, (nodes, row.shape[1])) == jnp.broadcast_to(id_column, (nodes, row.shape[1]))
    count_of = jnp.sum(jnp.where(alike, 1.0, 0.0), 1, keepdims=True)
    scale = lax.rsqrt(count_of)
    met_got()
    pooled = [jnp.sum(got[0, 0:Q].astype(F32), 0), jnp.sum(got[1, 0:Z].astype(F32), 0)]
    coarse_in = (jnp.concatenate(pooled, 1) * scale).astype(BF16)
    loads[10].wait()
    cpre = mm(coarse_in, wc_ref[...])
    coarse_out = (cpre * jax.nn.sigmoid(cpre)).astype(BF16)

    npre = agg_out + coarse_out.astype(F32)
    mesh_out = (latent.astype(F32) + npre * jax.nn.sigmoid(npre)).astype(BF16)
    mesh_ref[...] = mesh_out

    loads[11].wait()
    pre = mm(mesh_out, wd_ref[...])
    msgs[0:nodes] = (pre * jax.nn.sigmoid(pre)).astype(BF16)
    mine = msgs.at[pl.ds(0, nodes)]

    kinds = ("half", "half", "half", "half", "line")
    line_first = [m for m in range(many) if kinds[m] == "line"]
    cut = Z // 2
    near_z, far_z = pl.ds(0, cut), pl.ds(cut, Z - cut)

    def hop_core(m, value):
        if R % 8 == 0:
            whole = value.reshape(Z, Y, X, C, R, width)
            grad_out[m] = whole.astype(BF16)
        else:
            for at in range(Z * Q * C):
                spot = (at // (Q * C), at // (C * X) % Y, at // C % X, at % C)
                grad[(m, *spot)] = value[at * R:(at + 1) * R]
                grad_out[(m, *spot)] = value[at * R:(at + 1) * R].astype(BF16)
        one[m] = go(grad_out.at[m, :, :, :, 1 - c], core_in.at[m], core_sem, m, mate)
        if R % 8 == 0:
            grad[m] = whole

    def hop_first(m):
        one[m].wait_recv()
        total = grad[m, :, :, :, c] + core_in[m].astype(F32)
        pair_out[m] = total.astype(BF16)
        two[m] = []
        if kinds[m] == "line":
            for off in range(1, Z):
                there, k = lax.rem(z + off, Z), line_first.index(m) * (Z - 1) + off - 1
                two[m].append((k, go(pair_out.at[m, there], line_wide.at[k], line_wide_sem, k, (there, p.lon))))
        elif kinds[m] == "plane":
            for off in range(1, Q):
                there, k = lax.rem(q + off, Q), m * (Q - 1) + off - 1
                src = pair_out.at[m, :, there // X, lax.rem(there, X)]
                two[m].append((k, go(src, plane_wide.at[k], plane_wide_sem, k, (z, there * C + c))))
        else:
            for off in range(1, X):
                there, k = lax.rem(x + off, X), m * (X - 1) + off - 1
                two[m].append((0, k, go(pair_out.at[m, near_z, :, there], x_wide.at[k], x_sem, k, p.at(x=there))))
            for off in range(1, Y):
                there, k = lax.rem(y + off, Y), m * (Y - 1) + off - 1
                two[m].append((1, k, go(pair_out.at[m, far_z, there], y_wide.at[k], y_sem, k, p.at(y=there))))
        pair[m] = total

    def hop_middle(m):
        totals = [pair[m, near_z, :, x], pair[m, far_z, y]]
        middle[m] = []
        for side, k, copy in two[m]:
            copy.wait_recv()
            totals[side] = totals[side] + (y_wide if side else x_wide)[k].astype(F32)
        x_out[m], y_out[m] = totals[0].astype(BF16), totals[1].astype(BF16)
        for off in range(1, Y):
            there, k = lax.rem(y + off, Y), m * (Y - 1) + off - 1
            middle[m].append((0, k, go(x_out.at[m, :, there], x_slim.at[k], x_slim_sem, k, p.at(y=there))))
        for off in range(1, X):
            there, k = lax.rem(x + off, X), m * (X - 1) + off - 1
            middle[m].append((1, k, go(y_out.at[m, :, there], y_slim.at[k], y_slim_sem, k, p.at(x=there))))
        x_sum[m], y_sum[m] = totals

    def hop_second(m):
        three[m] = []
        if kinds[m] == "line":
            total, at = pair[m, z], line_first.index(m)
            for k, copy in two[m]:
                copy.wait_recv()
                total = total + line_wide[k].astype(F32)
            line_sum[at] = total
            line_out[at] = total.astype(BF16)
            for off in range(1, Q):
                there, k = lax.rem(q + off, Q), at * (Q - 1) + off - 1
                src = line_out.at[at, there // X, lax.rem(there, X)]
                three[m].append((k, go(src, plane_slim.at[k], plane_slim_sem, k, (z, there * C + c))))
            return
        if kinds[m] == "plane":
            total = pair[m, :, y, x]
            for k, copy in two[m]:
                copy.wait_recv()
                total = total + plane_wide[k].astype(F32)
            plane_sum[m] = total
            plane_out[m] = total.astype(BF16)
        else:
            totals = [x_sum[m, :, y], y_sum[m, :, x]]
            for side, k, copy in middle[m]:
                copy.wait_recv()
                totals[side] = totals[side] + (y_slim if side else x_slim)[k].astype(F32)
            plane_sum[m, near_z], plane_sum[m, far_z] = totals
            plane_out[m, near_z], plane_out[m, far_z] = totals[0].astype(BF16), totals[1].astype(BF16)
        for off in range(1, Z):
            there, k = lax.rem(z + off, Z), m * (Z - 1) + off - 1
            three[m].append((k, go(plane_out.at[m, there], line_slim.at[k], line_slim_sem, k, (there, p.lon))))

    def last(m):
        total = line_sum[line_first.index(m), y, x] if m in line_first else plane_sum[m, z]
        for k, copy in three[m]:
            copy.wait_recv()
            total = total + (plane_slim[k] if m in line_first else line_slim[k]).astype(F32)
        return total

    one, two, middle, three = {}, {}, {}, {}
    for copy in returns:
        copy.wait_recv()
    cot_sum = cot_sums[:nodes] + back[0].astype(F32) + back[1].astype(F32)
    d_high, d_low = split_float(cot_sum * silu_slope(pre))
    hop_core(4, mm_t(mesh_out, d_high) + mm_t(mesh_out, d_low))
    d_node = (mm_nt(d_high, wd_ref[...]) * silu_slope(npre)).astype(BF16)
    hop_core(2, mm_t(agg, d_node))
    hop_first(4)
    c_high, c_low = split_float(d_node.astype(F32) * silu_slope(cpre))
    hop_core(3, mm_t(coarse_in, c_high) + mm_t(coarse_in, c_low))
    hop_first(2)
    d_edges = (mm_nt(d_node, wn_ref[...])[None] * slope_edges).astype(BF16)
    d_sum = jnp.sum(d_edges.astype(F32), 0).astype(BF16)
    hop_core(1, mm_t(latent, d_sum))
    hop_first(3)
    hop_core(0, mm_t(beside, d_edges.reshape(slots * nodes, width)))
    hop_first(1)
    hop_first(0)
    hop_middle(2)
    hop_middle(3)
    hop_middle(1)
    hop_second(4)
    hop_middle(0)
    spoken = [
        go(mine, msgs.at[pl.ds(nodes, nodes)], esem, 4, (z, right)),
        go(mine, msgs.at[pl.ds(2 * nodes, nodes)], esem, 5, (z, left)),
    ]
    hop_second(2)
    hop_second(3)
    hop_second(1)
    hop_second(0)
    for copy in spoken:
        copy.wait_recv()
    for g in range(groups):
        decoded = mm_t(tally_high[g], msgs[...]) + mm_t(tally_low[g], msgs[...])
        grid_ref[g * group_rows:(g + 1) * group_rows] = decoded.astype(BF16)
    square, shares = jnp.zeros((R, width), F32), {}
    for m in (2, 3, 4, 1, 0):
        shares[m] = last(m)
        square = square + shares[m] * shares[m]
    square = sum(square[:, k * 128:(k + 1) * 128] for k in range(width // 128))
    square = jnp.broadcast_to(jnp.sum(square, keepdims=True), square_out.shape)
    square_out[...] = square
    mine = []
    for step in range(1, Z * p.L):
        peer = (lax.rem(z + step // p.L, Z), lax.rem(p.lon + step % p.L, p.L))
        mine.append(go(square_out, squares.at[step - 1], square_sem, step - 1, peer))
    for m, total in shares.items():
        for r in range(R):
            share[m:m + 1, r * width:(r + 1) * width] = total[r:r + 1]
    for copy in mine:
        copy.wait_recv()
    norm = jnp.sqrt(square + jnp.sum(squares[...], 0))[:, 0:1] + 1e-06
    out_ref[...] = share[...] * (1.0 / norm)
    for only, copy in pushed:
        if only is None:
            copy.wait_send()
        else:
            pl.when(only)(copy.wait_send)
    for copy in copies:
        copy.wait_send()


def run_step(sizes, latent, cot, weights, codes, ids, source, target, owner):
    Z, Y, X, C = sizes
    L = Y * X * C
    many = len(weights)
    nodes, width = latent.shape
    grid_rows = cot.shape[0]
    blocks, block_len = source.shape
    slots, height, breadth = codes.shape
    edge = 2 * max(height, breadth)
    groups = 4 if grid_rows % 4 == 0 else 1
    group_rows = grid_rows // groups
    Q, most = Y * X, max(Z, Y * X)
    R = width // (Z * L)
    w2 = width // 2
    vmem = pl.BlockSpec(memory_space=pltpu.VMEM)

    def buf(dtype, *dims):
        return pltpu.VMEM(dims, dtype)

    def sems(*counts):
        return [pltpu.SemaphoreType.DMA((2, n)) for n in counts]

    def single(*counts):
        return [pltpu.SemaphoreType.DMA((n,)) for n in counts]

    cut = Z // 2
    operands = [latent, cot, *weights, codes, ids, source, target, owner]
    pushes = Z - 1 + Q - 1 + 1 + C * (Z - 1 + Q - 1) + 2 + 8 + Q - 1 + C * (most - 1) + 1
    return pl.pallas_call(
        functools.partial(step_kernel, sizes),
        out_shape=(
            pltpu.VMEM((nodes, width), BF16),
            pltpu.VMEM((grid_rows, width), BF16),
            pltpu.VMEM((many, R * width), F32),
        ),
        in_specs=[pl.BlockSpec(memory_space=pltpu.HBM)] * len(operands),
        out_specs=(vmem,) * 3,
        scratch_shapes=[
            *[pltpu.VMEM(a.shape, a.dtype) for a in operands],
            buf(BF16, most * C, nodes, w2), buf(BF16, most * C, nodes, w2), buf(BF16, 2, most, nodes, w2),
            buf(jnp.int32, Q, Z, C, 1, C * nodes), buf(jnp.int32, Q, C, 1, C * nodes),
            buf(BF16, 8, edge, width), buf(BF16, edge, width), buf(jnp.int32, 4, 2, CAP, block_len),
            buf(BF16, groups, 3 * nodes, group_rows), buf(BF16, groups, 3 * nodes, group_rows),
            buf(BF16, 2, nodes, width), buf(BF16, 2, nodes, width), buf(BF16, 3 * nodes, width),
            buf(jnp.int32, 1, C * nodes),
            buf(F32, many, Z, Y, X, C, R, width), buf(BF16, many, Z, Y, X, C, R, width), buf(BF16, many, Z, Y, X, R, width),
            buf(F32, many, Z, Y, X, R, width), buf(BF16, many, Z, Y, X, R, width),
            buf(BF16, many * (Z - 1), Y, X, R, width), buf(BF16, many * (Q - 1), Z, R, width),
            buf(BF16, many * (X - 1), cut, Y, R, width), buf(BF16, many * (Y - 1), Z - cut, X, R, width),
            buf(F32, many, cut, Y, R, width), buf(F32, many, Z - cut, X, R, width),
            buf(BF16, many, cut, Y, R, width), buf(BF16, many, Z - cut, X, R, width),
            buf(BF16, many * (Y - 1), cut, R, width), buf(BF16, many * (X - 1), Z - cut, R, width),
            buf(F32, many, Y, X, R, width), buf(BF16, many, Y, X, R, width), buf(F32, many, Z, R, width),
            buf(BF16, many, Z, R, width),
            buf(BF16, many * (Q - 1), R, width), buf(BF16, many * (Z - 1), R, width),
            buf(F32, many, R * width), buf(F32, 1, 128), buf(F32, 1, 128), buf(F32, Z * L - 1, 1, 128),
            *single(len(operands), pushes, most * C, 2 * most, (Z + Q) * C + Q, 8), *sems(6, many, many * (Z - 1), many * (X - 1), many * (Y - 1), many * (Y - 1), many * (X - 1), many * (Q - 1), many * (Q - 1), many * (Z - 1), Z * L - 1),
        ],
        compiler_params=pltpu.CompilerParams(
            collective_id=0, has_side_effects=True, vmem_limit_bytes=56 * 1024 * 1024
        ),
        name="whole_step",
    )(*[pltpu.with_memory_space_constraint(a, pltpu.HBM) for a in operands])


def write_kernel(*refs):
    count = len(refs) // 2
    sems = refs[-1]
    moves = [pltpu.make_async_copy(refs[i], refs[count + i], sems.at[i]) for i in range(count)]
    for move in moves:
        move.start()
    for move in moves:
        move.wait()


def write_results(*results):
    return pl.pallas_call(
        write_kernel,
        out_shape=tuple(jax.ShapeDtypeStruct(r.shape, r.dtype) for r in results),
        in_specs=[pl.BlockSpec(memory_space=pltpu.VMEM)] * len(results),
        out_specs=(pl.BlockSpec(memory_space=pl.ANY),) * len(results),
        scratch_shapes=[pltpu.SemaphoreType.DMA((len(results),))],
        compiler_params=pltpu.CompilerParams(vmem_limit_bytes=8 * 1024 * 1024),
        name="write_results",
    )(*results)


def lon_parts(lat_count, lon_count):
    chips = lon_count // 2
    x = next(d for d in range(math.isqrt(chips), 0, -1) if chips % d == 0)
    return lat_count, chips // x, x, 2


def local(
    mesh_latent,
    grid_cotangent,
    w_source,
    w_target,
    w_node,
    w_coarse,
    w_decode,
    neighbour_codes,
    coarse_ids,
    edge_source,
    edge_target,
    edge_owner,
):
    height, breadth, width = mesh_latent.shape
    nodes = height * breadth
    sizes = lon_parts(lax.axis_size("lat"), lax.axis_size("lon"))
    blocks = edge_owner.shape[0]
    mesh_out, grid_out, clipped = run_step(
        sizes,
        mesh_latent.reshape(nodes, width),
        grid_cotangent,
        (w_source, w_target, w_node, w_coarse, w_decode),
        neighbour_codes,
        coarse_ids.reshape(height, breadth),
        edge_source.reshape(blocks, -1),
        edge_target.reshape(blocks, -1),
        edge_owner.reshape(1, blocks),
    )
    mesh_out, grid_out, clipped = write_results(mesh_out, grid_out, clipped)
    return (mesh_out.reshape(height, breadth, width), grid_out, clipped)


def solution(mesh):
    in_specs = (
        P("lat", "lon", None),
        P(("lat", "lon"), None),
        P(),
        P(),
        P(),
        P(),
        P(),
        P(None, "lat", "lon"),
        P("lat", "lon", None),
        P(("lat", "lon")),
        P(("lat", "lon")),
        P(("lat", "lon"), None),
    )
    out_specs = (P("lat", "lon", None), P(("lat", "lon"), None), P(None, ("lat", "lon")))
    return jax.shard_map(local, mesh=mesh, in_specs=in_specs, out_specs=out_specs, check_vma=False)
```

```python
import functools
import math

import jax
import jax.numpy as jnp
from jax import lax
from jax.experimental import pallas as pl
from jax.experimental.pallas import tpu as pltpu
from jax.sharding import PartitionSpec as P

CAP = 3
F32 = jnp.float32
BF16 = jnp.bfloat16


def silu_slope(value):
    sig = jax.nn.sigmoid(value)
    return sig * (1.0 + value * (1.0 - sig))


def mm(left, right):
    return jnp.dot(left, right, preferred_element_type=F32)


def mm_t(left, right):
    return lax.dot_general(left, right, (((0,), (0,)), ((), ())), preferred_element_type=F32)


def mm_nt(left, right):
    return lax.dot_general(left, right, (((1,), (1,)), ((), ())), preferred_element_type=F32)


def split_float(value):
    high = value.astype(BF16)
    return high, (value - high.astype(F32)).astype(BF16)


MESH = pl.DeviceIdType.MESH


class Place:
    def __init__(self, sizes):
        self.Z, self.Y, self.X, self.C = sizes
        self.L = self.Y * self.X * self.C
        self.lat, self.lon = lax.axis_index("lat"), lax.axis_index("lon")
        self.z, self.c = self.lat, lax.rem(self.lon, self.C)
        self.x = lax.rem(self.lon // self.C, self.X)
        self.y = self.lon // (self.C * self.X)
        self.Q, self.q = self.Y * self.X, self.lon // self.C
        self.rows = (lax.rem(self.z + self.Z - 1, self.Z), lax.rem(self.z + 1, self.Z))
        self.sides = (lax.rem(self.lon + self.L - 1, self.L), lax.rem(self.lon + 1, self.L))

    def at(self, y=None, x=None, c=None):
        y, x, c = (old if new is None else new for new, old in ((y, self.y), (x, self.x), (c, self.c)))
        return (self.lat, (y * self.X + x) * self.C + c)

    def greeted(self):
        line = [(lax.rem(self.z + step, self.Z), self.q * self.C + core) for step in range(1, self.Z) for core in range(self.C)]
        return line + [(self.z, lax.rem(self.lon + step, self.L)) for step in range(1, self.L)]

    def meet(self):
        barrier = pltpu.get_barrier_semaphore()

        def greet(peer):
            pl.semaphore_signal(barrier, inc=1, device_id=peer, device_id_type=MESH)

        for peer in self.greeted():
            greet(peer)
        for lat, there in zip(self.rows, (self.z > 0, self.z < self.Z - 1)):
            for lon in self.sides:
                pl.when(there)(functools.partial(greet, (lat, lon)))

    def met(self):
        corners = 2 * (jnp.where(self.z > 0, 1, 0) + jnp.where(self.z < self.Z - 1, 1, 0))
        pl.semaphore_wait(pltpu.get_barrier_semaphore(), len(self.greeted()) + corners)


def send(src, dst, sems, slot, peer):
    copy = pltpu.make_async_remote_copy(
        src_ref=src, dst_ref=dst, send_sem=sems.at[0, slot], recv_sem=sems.at[1, slot],
        device_id=peer, device_id_type=MESH,
    )
    copy.start()
    return copy


def iota(shape, dim):
    return lax.broadcasted_iota(jnp.int32, shape, dim)


def step_kernel(sizes, *refs):
    (lat_hbm, cot_hbm, ws_hbm, wt_hbm, wn_hbm, wc_hbm, wd_hbm, code_hbm, coarse_hbm, src_hbm, tgt_hbm,
     owner_hbm) = refs[:12]
    mesh_ref, grid_ref, out_ref = refs[12:15]
    (lat_ref, cot_ref, ws_ref, wt_ref, wn_ref, wc_ref, wd_ref, code_ref, coarse_ref, src_ref, tgt_ref, owner_ref,
     pool, parts, got, ids, plane_ids, halo, cols, pack, tally_high, tally_low, back, backs, msgs, id_ref, grad, grad_out,
     core_in, pair, pair_out, line_wide, plane_wide, x_wide, y_wide, x_sum, y_sum, x_out, y_out, x_slim, y_slim, line_sum, line_out, plane_sum, plane_out, plane_slim, line_slim,
     share, square_out, square_line, squares) = refs[15:66]
    (load_sem, out_sem, pool_sem, got_sem, id_sem, halo_sem, esem, core_sem, line_wide_sem, x_sem, y_sem, x_slim_sem, y_slim_sem, plane_wide_sem, plane_slim_sem,
     line_slim_sem, square_sem) = refs[66:]
    p = Place(sizes)
    Z, Y, X, C, z, y, x, c = p.Z, p.Y, p.X, p.C, p.z, p.y, p.x, p.c
    Q, q = p.Q, p.q
    nodes, width = lat_ref.shape
    grid_rows = cot_ref.shape[0]
    blocks, block_len = src_ref.shape
    groups, _, group_rows = tally_high.shape
    many = out_ref.shape[0]
    R = line_sum.shape[3]
    w2 = width // 2
    halves = (pl.ds(0, w2), pl.ds(w2, w2))
    copies, pushed = [], []
    mate = (z, q * C + 1 - c)
    most = max(Z, Q)
    role_size, role_at = jnp.where(c == 0, Z, Q), jnp.where(c == 0, z, q)
    other_size, other_at = jnp.where(c == 0, Q, Z), jnp.where(c == 0, q, z)

    def go(src, dst, sems, slot, peer):
        copy = send(src, dst, sems, slot, peer)
        copies.append(copy)
        return copy

    used = [0]

    def describe(src, dst, recv, peer, send_sem=None):
        return pltpu.make_async_remote_copy(
            src_ref=src, dst_ref=dst, send_sem=recv if send_sem is None else send_sem, recv_sem=recv, device_id=peer,
            device_id_type=MESH)

    def push(src, dst, recv, peer, only=None):
        copy = describe(src, dst, recv, peer, out_sem.at[used[0]])
        used[0] += 1
        if only is None:
            copy.start()
        else:
            pl.when(only)(copy.start)
        pushed.append((only, copy))

    def arrive(dst, recv, only=None):
        if only is None:
            describe(dst, dst, recv, mate).wait_recv()
        else:
            pl.when(only)(lambda: describe(dst, dst, recv, mate).wait_recv())

    def role_step(step):
        return jnp.where(c == 0, lax.rem(z + most * Z + step, Z), lax.rem(q + most * Q + step, Q))

    def limit(step, size):
        return step < size if step >= min(Z, Q) else None

    if Z != Q:
        pool[...] = jnp.zeros_like(pool)
    p.meet()

    def empty(at):
        for k in at:
            halo[k] = jnp.zeros(halo.shape[1:], BF16)

    pl.when(z == 0)(lambda: empty((0, 4, 5)))
    pl.when(z == Z - 1)(lambda: empty((1, 6, 7)))
    needed = (src_hbm, tgt_hbm, owner_hbm, coarse_hbm, lat_hbm, code_hbm, cot_hbm, wt_hbm, ws_hbm, wn_hbm, wc_hbm, wd_hbm)
    places = (src_ref, tgt_ref, owner_ref, coarse_ref, lat_ref, code_ref, cot_ref, wt_ref, ws_ref, wn_ref, wc_ref, wd_ref)
    loads = [pltpu.make_async_copy(a, b, load_sem.at[i]) for i, (a, b) in enumerate(zip(needed, places))]
    for at in (4, 3, 0, 1, 2, 5, 6, 7, 8, 9, 10, 11):
        loads[at].start()
    slots, height, breadth = code_ref.shape
    edge = halo.shape[1]

    def column(square):
        tall = jnp.concatenate([jnp.broadcast_to(square[i:i + 1], (breadth, breadth)) for i in range(height)], 0)
        keep = iota(tall.shape, 0) % breadth == iota(tall.shape, 1)
        return jnp.sum(jnp.where(keep, tall, 0), 1, keepdims=True)

    loads[4].wait()
    latent = lat_ref[...]
    pick = iota((edge, nodes), 0)
    pick = jnp.where(pick < height, pick * breadth, (pick - height) * breadth + breadth - 1)
    cols[...] = mm(jnp.where(pick == iota(pick.shape, 1), 1.0, 0.0).astype(BF16), latent).astype(BF16)
    pool[role_at * C + c] = lat_ref[:, pl.ds(pl.multiple_of(c * w2, 128), w2)]

    loads[3].wait()
    id_column = column(coarse_ref[...]) + 1
    spread = (nodes, id_ref.shape[1])
    keep = iota(spread, 1) == iota(spread, 0) + c * nodes
    id_row = jnp.sum(jnp.where(keep, jnp.broadcast_to(id_column, spread), 0), 0, keepdims=True)
    id_ref[...] = id_row
    ids[q, z, c] = id_row
    plane_ids[q, c] = id_row
    left, right = p.sides
    p.met()

    for step in range(1, most):
        if step < Z:
            push(lat_ref.at[:, halves[0]], pool.at[z * C + c], pool_sem.at[step * C + c], (lax.rem(z + step, Z), q * C))
        if step < Q:
            push(lat_ref.at[:, halves[1]], pool.at[q * C + c], pool_sem.at[step * C + c], (z, lax.rem(q + step, Q) * C + 1))
    give = pl.ds(pl.multiple_of((1 - c) * w2, 128), w2)
    push(lat_ref.at[:, give], pool.at[other_at * C + c], pool_sem.at[c], mate)
    for core in range(C):
        for step in range(1, Z):
            push(id_ref, ids.at[q, z, c], id_sem.at[step * C + c], (lax.rem(z + step, Z), q * C + core))
        for step in range(1, Q):
            push(id_ref, plane_ids.at[q, c], id_sem.at[(Z + step) * C + c], (z, lax.rem(q + step, Q) * C + core))
    push(id_ref, ids.at[q, z, c], id_sem.at[c], mate)
    push(id_ref, plane_ids.at[q, c], id_sem.at[Z * C + c], mate)
    above, below = p.rows
    first_rows, last_rows = lat_ref.at[pl.ds(0, edge)], lat_ref.at[pl.ds(nodes - edge, edge)]
    has_above, has_below = z > 0, z < Z - 1
    borders = [
        (last_rows, (below, p.lon), has_below, has_above), (first_rows, (above, p.lon), has_above, has_below),
        (cols, (z, right), None, None), (cols, (z, left), None, None),
        (last_rows, (below, right), has_below, has_above), (last_rows, (below, left), has_below, has_above),
        (first_rows, (above, right), has_above, has_below), (first_rows, (above, left), has_above, has_below),
    ]
    for k, (src, peer, gives, takes) in enumerate(borders):
        push(src, halo.at[k], halo_sem.at[k], peer, gives)

    def met_line():
        for step in range(1, Z):
            for core in range(C):
                arrive(ids.at[q, lax.rem(z + Z - step, Z), core], id_sem.at[step * C + core])
        arrive(ids.at[q, z, 1 - c], id_sem.at[1 - c])

    def met_plane():
        for step in range(1, Q):
            for core in range(C):
                arrive(plane_ids.at[lax.rem(q + Q - step, Q), core], id_sem.at[(Z + step) * C + core])
        arrive(plane_ids.at[q, 1 - c], id_sem.at[Z * C + 1 - c])

    def met_halo():
        for k, border in enumerate(borders):
            arrive(halo.at[k], halo_sem.at[k], border[3])

    def met_pool():
        for step in range(1, most):
            at = role_step(-step)
            for core in range(C):
                arrive(pool.at[at * C + core], pool_sem.at[step * C + core], limit(step, role_size))
        arrive(pool.at[role_at * C + 1 - c], pool_sem.at[1 - c])

    def met_ids():
        for step in range(1, Q):
            arrive(ids.at[lax.rem(q + Q - step, Q)], id_sem.at[(Z + Q) * C + step])

    def met_got():
        for step in range(1, Q):
            arrive(got.at[0, lax.rem(q + Q - step, Q)], got_sem.at[step])
        for step in range(1, Z):
            arrive(got.at[1, lax.rem(z + Z - step, Z)], got_sem.at[most + step])
        arrive(got.at[1 - c, role_at], got_sem.at[0])

    for load in loads[:3]:
        load.wait()
    sub, lane = iota((blocks, blocks), 0), iota((blocks, blocks), 1)
    owner = jnp.broadcast_to(owner_ref[...], (blocks, blocks))
    owner = jnp.sum(jnp.where(sub == lane, owner, 0), 1, keepdims=True)
    is_left = (owner == left).astype(jnp.int32)
    is_right = (owner == right).astype(jnp.int32)

    def ranks(column):
        row = jnp.sum(jnp.where(sub == lane, jnp.broadcast_to(column, sub.shape), 0), 0, keepdims=True)
        return jnp.sum(jnp.where(lane < sub, jnp.broadcast_to(row, sub.shape), 0), 1, keepdims=True)

    place = jnp.where(is_left == 1, ranks(is_left), jnp.where(is_right == 1, CAP + ranks(is_right), -1))
    wide_place = jnp.broadcast_to(place, (blocks, block_len))
    for r in range(2 * CAP):
        mine = wide_place == r
        side, row = divmod(r, CAP)
        pack[side, 0, row:row + 1] = jnp.sum(jnp.where(mine, src_ref[...], 0), 0, keepdims=True)
        pack[side, 1, row:row + 1] = jnp.sum(jnp.where(mine, tgt_ref[...] + 1, 0), 0, keepdims=True) - 1
    edges = [go(pack.at[0], pack.at[3], esem, 0, (z, left)), go(pack.at[1], pack.at[2], esem, 1, (z, right))]
    def tally(source, target):
        tall = jnp.where(target < 0, -1, target % group_rows)
        both = jnp.where(target < 0, 0, target // group_rows) * nodes + source
        count = source.shape[0]
        tall = jnp.concatenate([tall[r:r + 1] for r in range(count)], 1)
        both = jnp.concatenate([both[r:r + 1] for r in range(count)], 1)
        tall = jnp.broadcast_to(tall, (group_rows, tall.shape[1]))
        both = jnp.broadcast_to(both, (groups * nodes, both.shape[1]))
        hot_t = jnp.where(tall == iota(tall.shape, 0), 1.0, 0.0).astype(BF16)
        hot_b = jnp.where(both == iota(both.shape, 0), 1.0, 0.0).astype(BF16)
        return mm_nt(hot_b, hot_t)

    def keep_tally(kind, counts):
        over = jnp.floor(counts * (1.0 / 256.0)) * 256.0
        high, low = over.astype(BF16), (counts - over).astype(BF16)
        for g in range(groups):
            tally_high[g, kind * nodes:(kind + 1) * nodes] = high[g * nodes:(g + 1) * nodes]
            tally_low[g, kind * nodes:(kind + 1) * nodes] = low[g * nodes:(g + 1) * nodes]

    stays = jnp.broadcast_to((owner == p.lon).astype(jnp.int32), (blocks, block_len))
    keep_tally(0, tally(src_ref[...], jnp.where(stays == 1, tgt_ref[...], -1)))

    loads[5].wait()
    at_row, at_col = iota((height, breadth), 0), iota((height, breadth), 1)
    wheres = []
    first_line, last_line = jnp.where(z == 0, 1, 0), jnp.where(z == Z - 1, 1, 0)
    for k in range(slots):
        code = code_ref[k]
        down = jnp.where(code >= 6, 1, jnp.where(code >= 3, 0, -1))
        rows, columns = at_row + down, at_col + code - 3 * down - 4
        up, low = rows < 0, rows >= height
        before, after = columns < 0, columns >= breadth
        middle = jnp.where(before, nodes + 2 * edge + height + rows, jnp.where(after, nodes + 3 * edge + rows, rows * breadth + columns))
        top = jnp.where(before, nodes + 4 * edge + edge - 1, jnp.where(after, nodes + 5 * edge + edge - breadth, nodes + edge - breadth + columns))
        bottom = jnp.where(before, nodes + 6 * edge + breadth - 1, jnp.where(after, nodes + 7 * edge, nodes + edge + columns))
        spot = jnp.where(up, top - first_line * (1 << 20), jnp.where(low, bottom - last_line * (1 << 20), middle))
        wheres.append(column(spot))
    where = jnp.concatenate(wheres, 0)
    hot = jnp.broadcast_to(where, (where.shape[0], nodes + 8 * edge))
    hot = jnp.where(hot == iota(hot.shape, 1), 1.0, 0.0).astype(BF16)

    for copy in edges:
        copy.wait_recv()
    for side in range(2):
        keep_tally(side + 1, tally(pack[2 + side, 0], pack[2 + side, 1]))
    loads[6].wait()
    cot_sums = jnp.zeros((3 * nodes, width), F32)
    for g in range(groups):
        part = cot_ref[g * group_rows:(g + 1) * group_rows]
        cot_sums = cot_sums + mm(tally_high[g], part) + mm(tally_low[g], part)
    backs[0] = cot_sums[nodes:2 * nodes].astype(BF16)
    backs[1] = cot_sums[2 * nodes:3 * nodes].astype(BF16)
    returns = [go(backs.at[0], back.at[0], esem, 2, (z, left)), go(backs.at[1], back.at[1], esem, 3, (z, right))]

    met_line()
    for step in range(1, Q):
        push(ids.at[q], ids.at[q], id_sem.at[(Z + Q) * C + step], (z, lax.rem(q + step, Q) * C + c))
    met_plane()

    def id_rows(rows):
        rows = [jnp.sum(rows[at].reshape(C, C * nodes), 0, keepdims=True) for at in range(rows.shape[0])]
        return rows + [jnp.zeros_like(rows[0])] * (most - len(rows))

    line_rows, plane_rows = id_rows(ids[q]), id_rows(plane_ids[...])
    source_row = jnp.concatenate([jnp.where(c == 0, a, b) for a, b in zip(line_rows, plane_rows)], 1)
    eye = iota((C * nodes, C * nodes), 0) == iota((C * nodes, C * nodes), 1)
    tall = []
    for step in range(most):
        a, b = plane_ids[lax.rem(q + step, Q)], ids[q, lax.rem(z + step, Z)]
        tall.append(jnp.sum(jnp.where(c == 0, a, b).reshape(C, C * nodes), 0, keepdims=True))
    tall = [jnp.sum(jnp.where(eye, jnp.broadcast_to(row, eye.shape), 0), 1, keepdims=True) for row in tall]
    tall = jnp.concatenate(tall, 0)
    same = jnp.broadcast_to(tall, (tall.shape[0], source_row.shape[1])) == jnp.broadcast_to(source_row, (tall.shape[0], source_row.shape[1]))
    same = jnp.where(same, 1.0, 0.0).astype(BF16)

    loads[7].wait()
    toward = mm(latent, wt_ref[...])
    met_halo()
    near = jnp.concatenate([latent, halo[...].reshape(8 * edge, width)], 0)
    beside = mm(hot, near).astype(BF16)
    loads[8].wait()
    edges_pre = mm(beside, ws_ref[...]).reshape(slots, nodes, width) + toward[None]
    agg = jnp.sum(edges_pre * jax.nn.sigmoid(edges_pre), 0).astype(BF16)

    met_pool()
    gathered, tile = pool[...].reshape(most * C * nodes, w2), C * nodes
    for step in range(most - 1, -1, -1):
        sums = mm(same[step * tile:(step + 1) * tile], gathered).astype(BF16)
        parts[step * C:(step + 1) * C] = sums.reshape(C, nodes, w2)
        at = jnp.where(c == 0, lax.rem(q + step, Q), lax.rem(z + step, Z))
        for core in range(C if step else 0):
            peer = (jnp.where(c == 0, z, at), jnp.where(c == 0, at, q) * C + core)
            push(parts.at[step * C + core], got.at[c, other_at], got_sem.at[c * most + step], peer, limit(step, other_size))
    got[c, other_at] = parts[c]
    push(parts.at[1 - c], got.at[c, other_at], got_sem.at[0], mate)
    loads[9].wait()
    agg_out = mm(agg, wn_ref[...])
    slope_edges = silu_slope(edges_pre)
    met_ids()
    row = jnp.concatenate([r for at in range(Q) for r in [jnp.sum(ids[at, line].reshape(C, C * nodes), 0, keepdims=True) for line in range(Z)]], 1)
    alike = jnp.broadcast_to(row, (nodes, row.shape[1])) == jnp.broadcast_to(id_column, (nodes, row.shape[1]))
    count_of = jnp.sum(jnp.where(alike, 1.0, 0.0), 1, keepdims=True)
    scale = lax.rsqrt(count_of)
    met_got()
    pooled = [jnp.sum(got[0, 0:Q].astype(F32), 0), jnp.sum(got[1, 0:Z].astype(F32), 0)]
    coarse_in = (jnp.concatenate(pooled, 1) * scale).astype(BF16)
    loads[10].wait()
    cpre = mm(coarse_in, wc_ref[...])
    coarse_out = (cpre * jax.nn.sigmoid(cpre)).astype(BF16)

    npre = agg_out + coarse_out.astype(F32)
    mesh_out = (latent.astype(F32) + npre * jax.nn.sigmoid(npre)).astype(BF16)
    mesh_ref[...] = mesh_out

    loads[11].wait()
    pre = mm(mesh_out, wd_ref[...])
    msgs[0:nodes] = (pre * jax.nn.sigmoid(pre)).astype(BF16)
    mine = msgs.at[pl.ds(0, nodes)]

    kinds = ("half", "half", "half", "half", "line")
    line_first = [m for m in range(many) if kinds[m] == "line"]
    cut = Z // 2
    near_z, far_z = pl.ds(0, cut), pl.ds(cut, Z - cut)

    def hop_core(m, value):
        if R % 8 == 0:
            whole = value.reshape(Z, Y, X, C, R, width)
            grad_out[m] = whole.astype(BF16)
        else:
            for at in range(Z * Q * C):
                spot = (at // (Q * C), at // (C * X) % Y, at // C % X, at % C)
                grad[(m, *spot)] = value[at * R:(at + 1) * R]
                grad_out[(m, *spot)] = value[at * R:(at + 1) * R].astype(BF16)
        one[m] = go(grad_out.at[m, :, :, :, 1 - c], core_in.at[m], core_sem, m, mate)
        if R % 8 == 0:
            grad[m] = whole

    def hop_first(m):
        one[m].wait_recv()
        total = grad[m, :, :, :, c] + core_in[m].astype(F32)
        pair_out[m] = total.astype(BF16)
        two[m] = []
        if kinds[m] == "line":
            for off in range(1, Z):
                there, k = lax.rem(z + off, Z), line_first.index(m) * (Z - 1) + off - 1
                two[m].append((k, go(pair_out.at[m, there], line_wide.at[k], line_wide_sem, k, (there, p.lon))))
        elif kinds[m] == "plane":
            for off in range(1, Q):
                there, k = lax.rem(q + off, Q), m * (Q - 1) + off - 1
                src = pair_out.at[m, :, there // X, lax.rem(there, X)]
                two[m].append((k, go(src, plane_wide.at[k], plane_wide_sem, k, (z, there * C + c))))
        else:
            for off in range(1, X):
                there, k = lax.rem(x + off, X), m * (X - 1) + off - 1
                two[m].append((0, k, go(pair_out.at[m, near_z, :, there], x_wide.at[k], x_sem, k, p.at(x=there))))
            for off in range(1, Y):
                there, k = lax.rem(y + off, Y), m * (Y - 1) + off - 1
                two[m].append((1, k, go(pair_out.at[m, far_z, there], y_wide.at[k], y_sem, k, p.at(y=there))))
        pair[m] = total

    def hop_middle(m):
        totals = [pair[m, near_z, :, x], pair[m, far_z, y]]
        middle[m] = []
        for side, k, copy in two[m]:
            copy.wait_recv()
            totals[side] = totals[side] + (y_wide if side else x_wide)[k].astype(F32)
        x_out[m], y_out[m] = totals[0].astype(BF16), totals[1].astype(BF16)
        for off in range(1, Y):
            there, k = lax.rem(y + off, Y), m * (Y - 1) + off - 1
            middle[m].append((0, k, go(x_out.at[m, :, there], x_slim.at[k], x_slim_sem, k, p.at(y=there))))
        for off in range(1, X):
            there, k = lax.rem(x + off, X), m * (X - 1) + off - 1
            middle[m].append((1, k, go(y_out.at[m, :, there], y_slim.at[k], y_slim_sem, k, p.at(x=there))))
        x_sum[m], y_sum[m] = totals

    def hop_second(m):
        three[m] = []
        if kinds[m] == "line":
            total, at = pair[m, z], line_first.index(m)
            for k, copy in two[m]:
                copy.wait_recv()
                total = total + line_wide[k].astype(F32)
            line_sum[at] = total
            line_out[at] = total.astype(BF16)
            for off in range(1, Q):
                there, k = lax.rem(q + off, Q), at * (Q - 1) + off - 1
                src = line_out.at[at, there // X, lax.rem(there, X)]
                three[m].append((k, go(src, plane_slim.at[k], plane_slim_sem, k, (z, there * C + c))))
            return
        if kinds[m] == "plane":
            total = pair[m, :, y, x]
            for k, copy in two[m]:
                copy.wait_recv()
                total = total + plane_wide[k].astype(F32)
            plane_sum[m] = total
            plane_out[m] = total.astype(BF16)
        else:
            totals = [x_sum[m, :, y], y_sum[m, :, x]]
            for side, k, copy in middle[m]:
                copy.wait_recv()
                totals[side] = totals[side] + (y_slim if side else x_slim)[k].astype(F32)
            plane_sum[m, near_z], plane_sum[m, far_z] = totals
            plane_out[m, near_z], plane_out[m, far_z] = totals[0].astype(BF16), totals[1].astype(BF16)
        for off in range(1, Z):
            there, k = lax.rem(z + off, Z), m * (Z - 1) + off - 1
            three[m].append((k, go(plane_out.at[m, there], line_slim.at[k], line_slim_sem, k, (there, p.lon))))

    def last(m):
        total = line_sum[line_first.index(m), y, x] if m in line_first else plane_sum[m, z]
        for k, copy in three[m]:
            copy.wait_recv()
            total = total + (plane_slim[k] if m in line_first else line_slim[k]).astype(F32)
        return total

    one, two, middle, three = {}, {}, {}, {}
    for copy in returns:
        copy.wait_recv()
    cot_sum = cot_sums[:nodes] + back[0].astype(F32) + back[1].astype(F32)
    d_high, d_low = split_float(cot_sum * silu_slope(pre))
    hop_core(4, mm_t(mesh_out, d_high) + mm_t(mesh_out, d_low))
    d_node = (mm_nt(d_high, wd_ref[...]) * silu_slope(npre)).astype(BF16)
    hop_core(2, mm_t(agg, d_node))
    hop_first(4)
    c_high, c_low = split_float(d_node.astype(F32) * silu_slope(cpre))
    hop_core(3, mm_t(coarse_in, c_high) + mm_t(coarse_in, c_low))
    hop_first(2)
    d_edges = (mm_nt(d_node, wn_ref[...])[None] * slope_edges).astype(BF16)
    d_sum = jnp.sum(d_edges.astype(F32), 0).astype(BF16)
    hop_core(1, mm_t(latent, d_sum))
    hop_first(3)
    hop_core(0, mm_t(beside, d_edges.reshape(slots * nodes, width)))
    hop_first(1)
    hop_first(0)
    hop_middle(2)
    hop_middle(3)
    hop_middle(1)
    hop_second(4)
    hop_middle(0)
    spoken = [
        go(mine, msgs.at[pl.ds(nodes, nodes)], esem, 4, (z, right)),
        go(mine, msgs.at[pl.ds(2 * nodes, nodes)], esem, 5, (z, left)),
    ]
    hop_second(2)
    hop_second(3)
    hop_second(1)
    hop_second(0)
    for copy in spoken:
        copy.wait_recv()
    for g in range(groups):
        decoded = mm_t(tally_high[g], msgs[...]) + mm_t(tally_low[g], msgs[...])
        grid_ref[g * group_rows:(g + 1) * group_rows] = decoded.astype(BF16)
    square, shares = jnp.zeros((R, width), F32), {}
    for m in (2, 3, 4, 1, 0):
        shares[m] = last(m)
        square = square + shares[m] * shares[m]
    square = sum(square[:, k * 128:(k + 1) * 128] for k in range(width // 128))
    square = jnp.broadcast_to(jnp.sum(square, keepdims=True), square_out.shape)
    square_out[...] = square
    mine = []
    for step in range(1, Z * p.L):
        peer = (lax.rem(z + step // p.L, Z), lax.rem(p.lon + step % p.L, p.L))
        mine.append(go(square_out, squares.at[step - 1], square_sem, step - 1, peer))
    for m, total in shares.items():
        for r in range(R):
            share[m:m + 1, r * width:(r + 1) * width] = total[r:r + 1]
    for copy in mine:
        copy.wait_recv()
    norm = jnp.sqrt(square + jnp.sum(squares[...], 0))[:, 0:1] + 1e-06
    out_ref[...] = share[...] * (1.0 / norm)
    for only, copy in pushed:
        if only is None:
            copy.wait_send()
        else:
            pl.when(only)(copy.wait_send)
    for copy in copies:
        copy.wait_send()


def run_step(sizes, latent, cot, weights, codes, ids, source, target, owner):
    Z, Y, X, C = sizes
    L = Y * X * C
    many = len(weights)
    nodes, width = latent.shape
    grid_rows = cot.shape[0]
    blocks, block_len = source.shape
    slots, height, breadth = codes.shape
    edge = 2 * max(height, breadth)
    groups = 4 if grid_rows % 4 == 0 else 1
    group_rows = grid_rows // groups
    Q, most = Y * X, max(Z, Y * X)
    R = width // (Z * L)
    w2 = width // 2
    vmem = pl.BlockSpec(memory_space=pltpu.VMEM)

    def buf(dtype, *dims):
        return pltpu.VMEM(dims, dtype)

    def sems(*counts):
        return [pltpu.SemaphoreType.DMA((2, n)) for n in counts]

    def single(*counts):
        return [pltpu.SemaphoreType.DMA((n,)) for n in counts]

    cut = Z // 2
    operands = [latent, cot, *weights, codes, ids, source, target, owner]
    pushes = Z - 1 + Q - 1 + 1 + C * (Z - 1 + Q - 1) + 2 + 8 + Q - 1 + C * (most - 1) + 1
    return pl.pallas_call(
        functools.partial(step_kernel, sizes),
        out_shape=(
            pltpu.VMEM((nodes, width), BF16),
            pltpu.VMEM((grid_rows, width), BF16),
            pltpu.VMEM((many, R * width), F32),
        ),
        in_specs=[pl.BlockSpec(memory_space=pltpu.HBM)] * len(operands),
        out_specs=(vmem,) * 3,
        scratch_shapes=[
            *[pltpu.VMEM(a.shape, a.dtype) for a in operands],
            buf(BF16, most * C, nodes, w2), buf(BF16, most * C, nodes, w2), buf(BF16, 2, most, nodes, w2),
            buf(jnp.int32, Q, Z, C, 1, C * nodes), buf(jnp.int32, Q, C, 1, C * nodes),
            buf(BF16, 8, edge, width), buf(BF16, edge, width), buf(jnp.int32, 4, 2, CAP, block_len),
            buf(BF16, groups, 3 * nodes, group_rows), buf(BF16, groups, 3 * nodes, group_rows),
            buf(BF16, 2, nodes, width), buf(BF16, 2, nodes, width), buf(BF16, 3 * nodes, width),
            buf(jnp.int32, 1, C * nodes),
            buf(F32, many, Z, Y, X, C, R, width), buf(BF16, many, Z, Y, X, C, R, width), buf(BF16, many, Z, Y, X, R, width),
            buf(F32, many, Z, Y, X, R, width), buf(BF16, many, Z, Y, X, R, width),
            buf(BF16, many * (Z - 1), Y, X, R, width), buf(BF16, many * (Q - 1), Z, R, width),
            buf(BF16, many * (X - 1), cut, Y, R, width), buf(BF16, many * (Y - 1), Z - cut, X, R, width),
            buf(F32, many, cut, Y, R, width), buf(F32, many, Z - cut, X, R, width),
            buf(BF16, many, cut, Y, R, width), buf(BF16, many, Z - cut, X, R, width),
            buf(BF16, many * (Y - 1), cut, R, width), buf(BF16, many * (X - 1), Z - cut, R, width),
            buf(F32, many, Y, X, R, width), buf(BF16, many, Y, X, R, width), buf(F32, many, Z, R, width),
            buf(BF16, many, Z, R, width),
            buf(BF16, many * (Q - 1), R, width), buf(BF16, many * (Z - 1), R, width),
            buf(F32, many, R * width), buf(F32, 1, 128), buf(F32, 1, 128), buf(F32, Z * L - 1, 1, 128),
            *single(len(operands), pushes, most * C, 2 * most, (Z + Q) * C + Q, 8), *sems(6, many, many * (Z - 1), many * (X - 1), many * (Y - 1), many * (Y - 1), many * (X - 1), many * (Q - 1), many * (Q - 1), many * (Z - 1), Z * L - 1),
        ],
        compiler_params=pltpu.CompilerParams(
            collective_id=0, has_side_effects=True, vmem_limit_bytes=56 * 1024 * 1024
        ),
        name="whole_step",
    )(*[pltpu.with_memory_space_constraint(a, pltpu.HBM) for a in operands])


def write_kernel(*refs):
    count = len(refs) // 2
    sems = refs[-1]
    moves = [pltpu.make_async_copy(refs[i], refs[count + i], sems.at[i]) for i in range(count)]
    for move in moves:
        move.start()
    for move in moves:
        move.wait()


def write_results(*results):
    return pl.pallas_call(
        write_kernel,
        out_shape=tuple(jax.ShapeDtypeStruct(r.shape, r.dtype) for r in results),
        in_specs=[pl.BlockSpec(memory_space=pltpu.VMEM)] * len(results),
        out_specs=(pl.BlockSpec(memory_space=pl.ANY),) * len(results),
        scratch_shapes=[pltpu.SemaphoreType.DMA((len(results),))],
        compiler_params=pltpu.CompilerParams(vmem_limit_bytes=8 * 1024 * 1024),
        name="write_results",
    )(*results)


def lon_parts(lat_count, lon_count):
    chips = lon_count // 2
    x = next(d for d in range(math.isqrt(chips), 0, -1) if chips % d == 0)
    return lat_count, chips // x, x, 2


def local(
    mesh_latent,
    grid_cotangent,
    w_source,
    w_target,
    w_node,
    w_coarse,
    w_decode,
    neighbour_codes,
    coarse_ids,
    edge_source,
    edge_target,
    edge_owner,
):
    height, breadth, width = mesh_latent.shape
    nodes = height * breadth
    sizes = lon_parts(lax.axis_size("lat"), lax.axis_size("lon"))
    blocks = edge_owner.shape[0]
    mesh_out, grid_out, clipped = run_step(
        sizes,
        mesh_latent.reshape(nodes, width),
        grid_cotangent,
        (w_source, w_target, w_node, w_coarse, w_decode),
        neighbour_codes,
        coarse_ids.reshape(height, breadth),
        edge_source.reshape(blocks, -1),
        edge_target.reshape(blocks, -1),
        edge_owner.reshape(1, blocks),
    )
    mesh_out, grid_out, clipped = write_results(mesh_out, grid_out, clipped)
    return (mesh_out.reshape(height, breadth, width), grid_out, clipped)


def solution(mesh):
    in_specs = (
        P("lat", "lon", None),
        P(("lat", "lon"), None),
        P(),
        P(),
        P(),
        P(),
        P(),
        P(None, "lat", "lon"),
        P("lat", "lon", None),
        P(("lat", "lon")),
        P(("lat", "lon")),
        P(("lat", "lon"), None),
    )
    out_specs = (P("lat", "lon", None), P(("lat", "lon"), None), P(None, ("lat", "lon")))
    return jax.shard_map(local, mesh=mesh, in_specs=in_specs, out_specs=out_specs, check_vma=False)
```
